32 devices in a mesh: req: 8 (over z, y), tp: 4 (over x, core).
Axes of the slice: x: 2, y: 2, z: 4, core: 2. Of those that a mesh axis runs over, the one named last changes fastest.
Arguments:
- hidden: bfloat16 [2048, 5120], P('req', 'tp'), may hold values from -200 to 200
- norm_gain: bfloat16 [5120], replicated, may hold values from 0.099609375 to 1.8984375
- wq: bfloat16 [5120, 4096], P(None, 'tp'), may hold values from -0.078125 to 0.078125
- wkv: bfloat16 [5120, 2, 1024], P(None, None, 'tp'), may hold values from -0.15625 to 0.15625
- wo: bfloat16 [4096, 5120], P('tp'), may hold values from -1 to 1
- perm: int32 [16], replicated, may hold values from 0 to 15, as said below
- prior_len: int32 [16], P('req'), may hold values from 128 to 8192, as said below
- page_table: int32 [16, 64], P('req'), may hold values from 0 to 127, as said below
- pool: bfloat16 [1024, 128, 2, 1024], P('req', None, None, 'tp'), may hold values from -400 to 400
- send_table: int32 [8, 8, 17], P('req'), may hold values from -1 to 129, as said below
Outputs:
- attn_out: bfloat16 [2048, 5120], P('req', 'tp')
- decode_cache: bfloat16 [8, 8, 17, 128, 2, 1024], P('req', None, None, None, None, 'tp')
The draws below stay inside these ranges and needn't reach their ends.
Inputs may be any that keep to these rules, and one draw needn't show every extreme that they name: `perm`: a permutation of the requests. `prior_len`: one request has exactly 8192 cached tokens and another exactly 128. `page_table`: row r names pages of the pool block of the device that holds the dealt slot of request r; the rows of the 2 requests dealt to one device name all different pages. `send_table`: codes l * 65 + p name updated page p of slot l of the sending device, -1 an empty slot; every page p < (lengths + 255) // 128 of each of its slots is named exactly once in the sending device's row, no other page is named, and in every draw some block is full.
All inputs are finite; a program needn't handle non-finite values.
Results may differ from the reference program's by a relative error of at most 0.013.
The reference program's roundings to bfloat16 on the way count: a program that leaves them out, or rounds other values in their place, can miss the bound.
Values may be sent and summed in bfloat16 or wider, within the bound.
A program may use at most 256 MiB of HBM per device.

```python
import math
import jax
import jax.numpy as jnp
from jax import lax

MODEL_WIDTH = 5120
QUERY_HEADS = 32
KEY_VALUE_HEADS = 8
HEAD_SIZE = 128
PAGE_TOKENS = 128
NEW_TOKENS = 128
SLOTS = 2
PRIOR_PAGE_LIMIT = 64
REQUEST_COUNT = 16
BLOCK_PAGE_LIMIT = 17
N_REQ = 8
N_TP = 4


def pool_order(device_key):
    return jax.random.permutation(device_key, SLOTS * PRIOR_PAGE_LIMIT)


def device_order(device_key):
    return jax.random.permutation(device_key, REQUEST_COUNT // SLOTS)


def shared_tables(key):
    base_key = jax.random.fold_in(key, 17)
    devices = REQUEST_COUNT // SLOTS
    dealt_order = jax.random.permutation(jax.random.fold_in(base_key, 1), REQUEST_COUNT).astype(jnp.int32)
    request_lengths = jax.random.randint(jax.random.fold_in(base_key, 2), (REQUEST_COUNT,), PAGE_TOKENS, PRIOR_PAGE_LIMIT * PAGE_TOKENS + 1, dtype=jnp.int32)
    longest = dealt_order[SLOTS - 1]
    shortest = (longest + 1 + jax.random.randint(jax.random.fold_in(base_key, 4), (), 0, REQUEST_COUNT - 1, dtype=jnp.int32)) % REQUEST_COUNT
    request_lengths = request_lengths.at[longest].set(PRIOR_PAGE_LIMIT * PAGE_TOKENS).at[shortest].set(PAGE_TOKENS)
    pool_orders = jax.vmap(pool_order)(jax.random.split(jax.random.fold_in(base_key, 5), devices)).astype(jnp.int32)
    dealt_tables = pool_orders.reshape(REQUEST_COUNT, PRIOR_PAGE_LIMIT)
    inverse = jnp.argsort(dealt_order).astype(jnp.int32)
    table = dealt_tables[inverse]
    dealt_lengths = request_lengths[dealt_order].reshape(devices, SLOTS)
    pages_needed = (dealt_lengths + NEW_TOKENS + PAGE_TOKENS - 1) // PAGE_TOKENS
    code_width = PRIOR_PAGE_LIMIT + 1
    page_ids = jnp.arange(code_width, dtype=jnp.int32)
    is_valid = (page_ids[None, None, :] < pages_needed[:, :, None]).reshape(devices, SLOTS * code_width)
    page_codes = jnp.broadcast_to(jnp.arange(SLOTS * code_width, dtype=jnp.int32)[None, :], (devices, SLOTS * code_width))
    fill_rank = jnp.cumsum(is_valid.astype(jnp.int32), axis=1) - 1
    targets_order = jax.vmap(device_order)(jax.random.split(jax.random.fold_in(base_key, 6), devices)).astype(jnp.int32)
    dest_block = jnp.clip(fill_rank // BLOCK_PAGE_LIMIT, 0, devices - 1)
    target = jnp.take_along_axis(targets_order, dest_block, axis=1) * BLOCK_PAGE_LIMIT + jnp.maximum(fill_rank, 0) % BLOCK_PAGE_LIMIT
    target = jnp.where(is_valid, target, devices * BLOCK_PAGE_LIMIT)
    row_ids = jnp.broadcast_to(jnp.arange(devices, dtype=jnp.int32)[:, None], target.shape)
    sending = jnp.full((devices, devices * BLOCK_PAGE_LIMIT), -1, jnp.int32).at[row_ids, target].set(page_codes, mode='drop')
    return (dealt_order, request_lengths, table, sending.reshape(devices, devices, BLOCK_PAGE_LIMIT))


def draw_perm(key, part):
    return shared_tables(key)[0]


def draw_prior_len(key, part):
    return shared_tables(key)[1]


def draw_page_table(key, part):
    return shared_tables(key)[2]


def draw_send_table(key, part):
    return shared_tables(key)[3]


def draw_hidden(key, part):
    key_one = jax.random.fold_in(key, 0)
    page_dimensions = (REQUEST_COUNT * NEW_TOKENS, MODEL_WIDTH)
    column = jnp.arange(MODEL_WIDTH, dtype=jnp.float32) / MODEL_WIDTH
    base_values = jnp.clip(jax.random.normal(key_one, page_dimensions, jnp.float32), -6.0, 6.0)
    values = base_values * jnp.power(3.0, 0.5 * column)[None, :]
    return values.astype(jnp.bfloat16)


def draw_pool(key, part):
    key_one = jax.random.fold_in(key, 0)
    page_dimensions = (REQUEST_COUNT * PRIOR_PAGE_LIMIT, PAGE_TOKENS, 2, KEY_VALUE_HEADS * HEAD_SIZE)
    plane_index = jnp.arange(2, dtype=jnp.int32)[None, None, :, None]
    plane_scale = jnp.where(plane_index == 0, 1.5, 1.0)
    values = jnp.clip(jax.random.normal(key_one, page_dimensions, jnp.float32), -6.0, 6.0) * plane_scale
    return values.astype(jnp.bfloat16)


def level_of(stream_key, shape, cuts, low, largest):
    factor_of = 1.0
    for dim, blocks in cuts:
        heights = jax.random.uniform(jax.random.fold_in(jax.random.fold_in(stream_key, 6), dim), (blocks,), jnp.float32, low / len(cuts), largest / len(cuts))
        factor_of = factor_of * jnp.repeat(jnp.exp(heights), shape[dim] // blocks).reshape((-1,) + (1,) * (len(shape) - 1 - dim))
    return factor_of


def noise(rng, dims, deviation, limit, cuts=(), kind=jnp.bfloat16):
    level = level_of(rng, dims, cuts, -0.22, 0.18) if cuts else 1.0
    drawn = jax.random.normal(rng, dims, jnp.float32) * deviation * level
    return jnp.minimum(jnp.maximum(drawn, -limit), limit).astype(kind)


def setup_inputs(seed: int = 0) -> dict:
    key_list = jax.random.split(jax.random.key(seed), 11)
    return {
        "hidden": draw_hidden(jax.random.fold_in(key_list[10], 71), 0),
        "norm_gain": jnp.clip(1.0 + 0.18 * jax.random.normal(key_list[1], (MODEL_WIDTH,), jnp.float32), 0.099609375, 1.8984375).astype(jnp.bfloat16),
        "wq": noise(key_list[2], (MODEL_WIDTH, QUERY_HEADS * HEAD_SIZE), MODEL_WIDTH ** -0.5, 0.078125, ((1, 4),)),
        "wkv": noise(key_list[3], (MODEL_WIDTH, 2, KEY_VALUE_HEADS * HEAD_SIZE), (MODEL_WIDTH // 4) ** -0.5, 0.15625, ((2, 4),)),
        "wo": noise(key_list[4], (QUERY_HEADS * HEAD_SIZE, MODEL_WIDTH), (HEAD_SIZE // 4) ** -0.5, 1.0, ((0, 4),)),
        "perm": draw_perm(jax.random.fold_in(key_list[10], 71), 0),
        "prior_len": draw_prior_len(jax.random.fold_in(key_list[10], 71), 0),
        "page_table": draw_page_table(jax.random.fold_in(key_list[10], 71), 0),
        "pool": draw_pool(jax.random.fold_in(key_list[10], 71), 0),
        "send_table": draw_send_table(jax.random.fold_in(key_list[10], 71), 0),
    }


NORM_EPSILON = 1e-05
ROPE_THETA = 100000000.0

def normalize(rows, gain):
    wide_rows = rows.astype(jnp.float32)
    mean_square = lax.optimization_barrier(jnp.mean(wide_rows * wide_rows, axis=-1, keepdims=True))
    return (wide_rows * lax.rsqrt(mean_square + NORM_EPSILON) * gain.astype(jnp.float32)).astype(jnp.bfloat16)

def rotate(vectors, positions):
    half_size = vectors.shape[-1] // 2
    frequency = jnp.power(jnp.float32(ROPE_THETA), -2.0 * jnp.arange(half_size, dtype=jnp.float32) / vectors.shape[-1])
    angles = positions.astype(jnp.float32)[:, None] * frequency[None, :]
    cosine = jnp.cos(angles)[:, None, :]
    sine_part = jnp.sin(angles)[:, None, :]
    first_half = vectors[..., :half_size]
    second_half = vectors[..., half_size:]
    return jnp.concatenate([first_half * cosine - second_half * sine_part, second_half * cosine + first_half * sine_part], axis=-1)

def reference(hidden, norm_gain, wq, wkv, wo, perm, prior_len, page_table, pool, send_table):
    request_lengths = prior_len[perm]
    page_tables = page_table[perm]
    normalized_input = normalize(hidden, norm_gain)
    query_proj = jnp.dot(normalized_input, wq, preferred_element_type=jnp.float32)
    key_value_projection = jnp.dot(normalized_input, wkv.reshape(MODEL_WIDTH, 2 * KEY_VALUE_HEADS * HEAD_SIZE), preferred_element_type=jnp.float32)
    positions = (request_lengths[:, None] + jnp.arange(NEW_TOKENS, dtype=jnp.int32)[None, :]).reshape(-1)
    query_vectors = rotate(query_proj.reshape(-1, QUERY_HEADS, HEAD_SIZE), positions).astype(jnp.bfloat16)
    key_value_heads = key_value_projection.reshape(-1, 2, KEY_VALUE_HEADS, HEAD_SIZE)
    incoming_keys = rotate(key_value_heads[:, 0], positions).astype(jnp.bfloat16)
    incoming_values = key_value_heads[:, 1].astype(jnp.bfloat16)

    def single_slot(packed):
        query_slots, slot_keys, slot_values, length, table_row, slot_id = packed
        base_page = slot_id // SLOTS * (SLOTS * PRIOR_PAGE_LIMIT)
        cached_entries = pool[base_page + table_row]
        stored_keys = cached_entries[:, :, 0].reshape(PRIOR_PAGE_LIMIT * PAGE_TOKENS, KEY_VALUE_HEADS, HEAD_SIZE)
        stored_values = cached_entries[:, :, 1].reshape(PRIOR_PAGE_LIMIT * PAGE_TOKENS, KEY_VALUE_HEADS, HEAD_SIZE)
        all_keys = jnp.concatenate([stored_keys, slot_keys], axis=0).astype(jnp.float32)
        all_values = jnp.concatenate([stored_values, slot_values], axis=0).astype(jnp.float32)
        cached_ok = jnp.arange(PRIOR_PAGE_LIMIT * PAGE_TOKENS, dtype=jnp.int32) < length
        token_ids = jnp.arange(NEW_TOKENS, dtype=jnp.int32)
        causal = token_ids[None, :] <= token_ids[:, None]
        valid = jnp.concatenate([jnp.broadcast_to(cached_ok[None, :], (NEW_TOKENS, PRIOR_PAGE_LIMIT * PAGE_TOKENS)), causal], axis=1)
        grouped_queries = query_slots.reshape(NEW_TOKENS, KEY_VALUE_HEADS, QUERY_HEADS // KEY_VALUE_HEADS, HEAD_SIZE).astype(jnp.float32)
        scores = jnp.einsum('tgjd,kgd->gjtk', grouped_queries, all_keys) / math.sqrt(HEAD_SIZE)
        masked = jnp.where(valid, scores, -1e+30)
        highest = lax.optimization_barrier(jnp.max(masked, axis=-1, keepdims=True))
        weights = jnp.where(valid, jnp.exp(masked - highest), 0.0)
        rounded = lax.optimization_barrier(weights.astype(jnp.bfloat16))
        numer = jnp.einsum('gjtk,kgd->gjtd', rounded.astype(jnp.float32), all_values)
        context = numer / lax.optimization_barrier(jnp.sum(weights, axis=-1))[..., None]
        return context.transpose(2, 0, 1, 3).reshape(NEW_TOKENS, QUERY_HEADS * HEAD_SIZE).astype(jnp.bfloat16)
    context_rows = lax.map(single_slot, (query_vectors.reshape(REQUEST_COUNT, NEW_TOKENS, QUERY_HEADS, HEAD_SIZE), incoming_keys.reshape(REQUEST_COUNT, NEW_TOKENS, KEY_VALUE_HEADS, HEAD_SIZE), incoming_values.reshape(REQUEST_COUNT, NEW_TOKENS, KEY_VALUE_HEADS, HEAD_SIZE), request_lengths, page_tables, jnp.arange(REQUEST_COUNT, dtype=jnp.int32)))
    context = context_rows.reshape(REQUEST_COUNT * NEW_TOKENS, QUERY_HEADS * HEAD_SIZE)
    group_width = QUERY_HEADS * HEAD_SIZE // N_TP
    total = jnp.zeros((REQUEST_COUNT * NEW_TOKENS, MODEL_WIDTH), jnp.float32)
    for group in range(N_TP):
        term = jnp.dot(context[:, group * group_width:(group + 1) * group_width], wo[group * group_width:(group + 1) * group_width], preferred_element_type=jnp.float32).astype(jnp.bfloat16)
        term = lax.optimization_barrier(term)
        total = total + term.astype(jnp.float32)
    attn_out = total.astype(jnp.bfloat16)
    recent_rows = jnp.stack([incoming_keys.reshape(REQUEST_COUNT, NEW_TOKENS, KEY_VALUE_HEADS * HEAD_SIZE), incoming_values.reshape(REQUEST_COUNT, NEW_TOKENS, KEY_VALUE_HEADS * HEAD_SIZE)], axis=2)

    def one_target(entries):
        flat_codes = entries.reshape(-1)
        is_valid = flat_codes >= 0
        clean_codes = jnp.maximum(flat_codes, 0)
        sources = jnp.repeat(jnp.arange(N_REQ, dtype=jnp.int32), BLOCK_PAGE_LIMIT)
        slot_ids = sources * SLOTS + clean_codes // (PRIOR_PAGE_LIMIT + 1)
        page_index = clean_codes % (PRIOR_PAGE_LIMIT + 1)
        slot_lengths = request_lengths[slot_ids]
        physical = slot_ids // SLOTS * (SLOTS * PRIOR_PAGE_LIMIT) + page_tables[slot_ids, jnp.minimum(page_index, PRIOR_PAGE_LIMIT - 1)]
        token_pos = page_index[:, None] * PAGE_TOKENS + jnp.arange(PAGE_TOKENS, dtype=jnp.int32)[None, :]
        keep_mask = is_valid[:, None] & (token_pos < slot_lengths[:, None])
        page_contents = jnp.where(keep_mask[:, :, None, None], pool[physical], jnp.zeros((), pool.dtype))
        offsets = token_pos - slot_lengths[:, None]
        inside = is_valid[:, None] & (offsets >= 0) & (offsets < NEW_TOKENS)
        picked = recent_rows[slot_ids[:, None], jnp.clip(offsets, 0, NEW_TOKENS - 1)]
        page_contents = jnp.where(inside[:, :, None, None], picked, page_contents)
        return page_contents.reshape(N_REQ, BLOCK_PAGE_LIMIT, PAGE_TOKENS, 2, KEY_VALUE_HEADS * HEAD_SIZE)
    decode_cache = lax.map(one_target, jnp.transpose(send_table, (1, 0, 2)))
    return (attn_out, decode_cache)
```

```python
import math

import jax
import jax.numpy as jnp
from jax import lax
from jax.experimental import pallas as pl
from jax.experimental.pallas import tpu as pltpu
from jax.sharding import PartitionSpec as P

HEAD_SIZE = 128
NORM_EPSILON = 1e-05
ROPE_THETA = 100000000.0
BLOCK_PAGES = 4


def normalize(rows, gain):
    wide_rows = rows.astype(jnp.float32)
    mean_square = jnp.mean(wide_rows * wide_rows, axis=-1, keepdims=True)
    return (wide_rows * lax.rsqrt(mean_square + NORM_EPSILON) * gain.astype(jnp.float32)).astype(
        jnp.bfloat16
    )


def rotate(vectors, positions):
    half_size = vectors.shape[-1] // 2
    frequency = jnp.power(
        jnp.float32(ROPE_THETA), -2.0 * jnp.arange(half_size, dtype=jnp.float32) / vectors.shape[-1]
    )
    angles = positions.astype(jnp.float32)[:, None] * frequency[None, :]
    cosine = jnp.cos(angles)[:, None, :]
    sine_part = jnp.sin(angles)[:, None, :]
    first_half = vectors[..., :half_size]
    second_half = vectors[..., half_size:]
    return jnp.concatenate(
        [
            first_half * cosine - second_half * sine_part,
            second_half * cosine + first_half * sine_part,
        ],
        axis=-1,
    )


class Layout:
    def __init__(self, slots, row_pages, peers, block):
        self.slots, self.row_pages, self.peers, self.block = slots, row_pages, peers, block
        self.code_width = row_pages + 1
        self.sends = slots + slots * row_pages
        self.used = self.sends + peers * block
        self.width = -(-self.used // 1024) * 1024
        self.late = 2 * slots
        self.early = block - self.late

    def request(self, perm, device, slot):
        request = perm[device * self.slots + slot]
        return lax.div(request, self.slots) * self.width, lax.rem(request, self.slots)

    def length(self, table, perm, device, slot):
        base, row = self.request(perm, device, slot)
        return table[base + row]

    def physical(self, table, perm, device, slot, page):
        base, row = self.request(perm, device, slot)
        return table[base + self.slots + row * self.row_pages + jnp.minimum(page, self.row_pages - 1)]

    def split(self, code):
        return lax.div(code, self.code_width), lax.rem(code, self.code_width)

    def visit(self, table, perm, source, target, page_len, use):
        whole = [
            lax.div(self.length(table, perm, source, slot), page_len) for slot in range(self.slots)
        ]
        base = source * self.width + self.sends + target * self.block
        plain, tails = jnp.int32(0), jnp.int32(self.block - 1)
        for number in range(self.block):
            code = table[base + number]
            first = whole[0]
            for slot in range(1, self.slots):
                low = slot * self.code_width
                first = jnp.where(code >= low, whole[slot] + low, first)
            valid, tail = code >= 0, code >= first
            place = jnp.where(valid, jnp.where(tail, tails, plain), -1)
            use(number, code, place)
            plain = plain + jnp.where(valid & jnp.logical_not(tail), 1, 0)
            tails = tails - jnp.where(tail, 1, 0)


def exchange_kernel(peers, mine, out, send_sems, recv_sems):
    me = lax.axis_index("req")
    barrier = pltpu.get_barrier_semaphore()
    for hop in range(1, peers):
        pl.semaphore_signal(
            barrier,
            inc=1,
            device_id={"req": lax.rem(me + hop, peers)},
            device_id_type=pl.DeviceIdType.MESH,
        )
    pl.semaphore_wait(barrier, peers - 1)
    copies = []
    for hop in range(1, peers):
        copy = pltpu.make_async_remote_copy(
            src_ref=mine,
            dst_ref=out.at[me],
            send_sem=send_sems.at[hop - 1],
            recv_sem=recv_sems.at[hop - 1],
            device_id={"req": lax.rem(me + hop, peers)},
            device_id_type=pl.DeviceIdType.MESH,
        )
        copy.start()
        copies.append(copy)
    out[me] = mine[...]
    for copy in copies:
        copy.wait()


def exchange(peers, mine):
    return pl.pallas_call(
        lambda *refs: exchange_kernel(peers, *refs),
        out_shape=jax.ShapeDtypeStruct((peers,) + mine.shape, mine.dtype),
        in_specs=[pl.BlockSpec(memory_space=pltpu.VMEM)],
        out_specs=pl.BlockSpec(memory_space=pltpu.VMEM),
        scratch_shapes=[
            pltpu.SemaphoreType.DMA((peers - 1,)),
            pltpu.SemaphoreType.DMA((peers - 1,)),
        ],
        compiler_params=pltpu.CompilerParams(collective_id=0, has_side_effects=True),
        name="exchange",
    )(mine)


BUFFERS = 32
AHEAD = 16


def ring(count, load, store, drain):
    def step(index, carry):
        @pl.when(index < count)
        def _():
            @pl.when(index >= BUFFERS)
            def _():
                drain(index - BUFFERS)

            load(index)

        @pl.when(index >= AHEAD)
        def _():
            store(index - AHEAD)

        return carry

    lax.fori_loop(0, count + AHEAD, step, 0)

    def last(index, carry):
        drain(index)
        return carry

    lax.fori_loop(max(count - BUFFERS, 0), count, last, 0)


def copy_rows(source, source_row, target, target_row, count, sem):
    size = target.shape[0]
    while size:
        offset = lax.div(count, 2 * size) * (2 * size)

        @pl.when(lax.rem(lax.div(count, size), 2) == 1)
        def _(size=size, offset=offset):
            pltpu.make_async_copy(
                source.at[pl.ds(source_row + offset, size)],
                target.at[pl.ds(target_row + offset, size)],
                sem,
            ).start()

        size //= 2


def pack_kernel(layout, late, table, perm, me, pool, *rest):
    if late:
        recent, zeros, out, codes, buffers, in_sems, out_sems = rest
    else:
        out, codes, buffers, in_sems, out_sems = rest
    page_len = buffers.shape[1]
    span = layout.late if late else layout.early
    start = layout.early if late else 0
    count = layout.peers * span

    def clear(index, carry):
        codes[index] = 0
        return carry

    lax.fori_loop(0, count, clear, 0)
    starts = []
    for slot in range(layout.slots):
        base, row = layout.request(perm, me[0], slot)
        starts.append(
            base + layout.slots + row * layout.row_pages - slot * layout.code_width
        )

    def block(target, carry):
        def use(number, code, place):
            inside = (place >= start) & (place < start + span)
            item = code
            if not late:
                origin = starts[0]
                for slot in range(1, layout.slots):
                    origin = jnp.where(code >= slot * layout.code_width, starts[slot], origin)
                item = table[jnp.where(inside, origin + code, 0)]

            @pl.when(inside)
            def _():
                codes[target * span + place - start] = item

        layout.visit(table, perm, me[0], target, page_len, use)
        return carry

    lax.fori_loop(0, layout.peers, block, 0)

    def load(index):
        spot = index & (BUFFERS - 1)
        target, sem = buffers.at[spot], in_sems.at[spot]
        if not late:
            pltpu.make_async_copy(pool.at[codes[index]], target, sem).start()
            return
        slot, page = layout.split(codes[index])
        cached = pool.at[layout.physical(table, perm, me[0], slot, page)]
        length = layout.length(table, perm, me[0], slot)
        full, kept = lax.div(length, page_len), lax.rem(length, page_len)

        @pl.when(page < full)
        def _():
            pltpu.make_async_copy(cached, target, sem).start()

        @pl.when(page == full)
        def _():
            copy_rows(cached, 0, target, 0, kept, sem)
            copy_rows(recent.at[slot], 0, target, kept, page_len - kept, sem)

        @pl.when(page > full)
        def _():
            copy_rows(recent.at[slot], page_len - kept, target, 0, kept, sem)
            copy_rows(zeros, 0, target, kept, page_len - kept, sem)

    def outward(index):
        spot = index & (BUFFERS - 1)
        return pltpu.make_async_copy(buffers.at[spot], out.at[index], out_sems.at[spot])

    def store(index):
        spot = index & (BUFFERS - 1)
        pltpu.make_async_copy(pool.at[0], buffers.at[spot], in_sems.at[spot]).wait()
        outward(index).start()

    ring(count, load, store, lambda index: outward(index).wait())


def scratch(layout, pool):
    return [
        pltpu.SMEM((layout.peers * layout.block,), jnp.int32),
        pltpu.VMEM((BUFFERS,) + pool.shape[-3:], pool.dtype),
        pltpu.SemaphoreType.DMA((BUFFERS,)),
        pltpu.SemaphoreType.DMA((BUFFERS,)),
    ]


def pack_pages(layout, table, perm, me, pool, *fresh):
    late = bool(fresh)
    span = layout.late if late else layout.early
    return pl.pallas_call(
        lambda *refs: pack_kernel(layout, late, *refs),
        out_shape=jax.ShapeDtypeStruct((layout.peers * span,) + pool.shape[1:], pool.dtype),
        grid_spec=pltpu.PrefetchScalarGridSpec(
            num_scalar_prefetch=3,
            grid=(1,),
            in_specs=[pl.BlockSpec(memory_space=pl.ANY)] * (1 + len(fresh)),
            out_specs=pl.BlockSpec(memory_space=pl.ANY),
            scratch_shapes=scratch(layout, pool),
        ),
        name="pack_late" if late else "pack_early",
    )(table, perm, me, pool, *fresh).reshape((layout.peers, span) + pool.shape[1:])


def place_kernel(layout, table, perm, me, arrived, zeros, *rest):
    out, numbers, places, buffers, in_sems, out_sems, blank, blank_sem = rest
    page_len = buffers.shape[1]

    def clear(index, carry):
        numbers[index] = -1
        return carry

    lax.fori_loop(0, layout.peers * layout.late, clear, 0)
    fill = pltpu.make_async_copy(zeros, blank, blank_sem)
    fill.start()

    def block(source, carry):
        def use(number, code, place):
            places[source * layout.block + number] = place

            @pl.when(place >= layout.early)
            def _():
                late_index = source * layout.late + place - layout.early
                numbers[late_index] = source * layout.block + number

        layout.visit(table, perm, source, me[0], page_len, use)
        return carry

    lax.fori_loop(0, layout.peers, block, 0)
    fill.wait()

    def inward(index):
        spot = index & (BUFFERS - 1)
        place = jnp.clip(places[index], 0, layout.early - 1)
        return pltpu.make_async_copy(
            arrived.at[lax.div(index, layout.block), place], buffers.at[spot], in_sems.at[spot]
        )

    def outward(index, held):
        return pltpu.make_async_copy(held, out.at[index], out_sems.at[index & (BUFFERS - 1)])

    def is_early(index):
        return (places[index] >= 0) & (places[index] < layout.early)

    def load(index):
        @pl.when(is_early(index))
        def _():
            inward(index).start()

    def store(index):
        @pl.when(is_early(index))
        def _():
            inward(index).wait()
            outward(index, buffers.at[index & (BUFFERS - 1)]).start()

        @pl.when(places[index] < 0)
        def _():
            outward(index, blank).start()

    def drain(index):
        @pl.when(places[index] < layout.early)
        def _():
            outward(index, blank).wait()

    ring(layout.peers * layout.block, load, store, drain)


def place_late_kernel(count, numbers, arrived, held, out, buffers, in_sems, out_sems):
    def inward(index):
        spot = index & (BUFFERS - 1)
        return pltpu.make_async_copy(arrived.at[index], buffers.at[spot], in_sems.at[spot])

    def outward(index):
        spot = index & (BUFFERS - 1)
        target = out.at[jnp.maximum(numbers[index], 0)]
        return pltpu.make_async_copy(buffers.at[spot], target, out_sems.at[spot])

    def load(index):
        @pl.when(numbers[index] >= 0)
        def _():
            inward(index).start()

    def store(index):
        @pl.when(numbers[index] >= 0)
        def _():
            inward(index).wait()
            outward(index).start()

    def drain(index):
        @pl.when(numbers[index] >= 0)
        def _():
            outward(index).wait()

    ring(count, load, store, drain)


def place_early_pages(layout, table, perm, me, arrived, zeros):
    page = arrived.shape[2:]
    return pl.pallas_call(
        lambda *refs: place_kernel(layout, *refs),
        out_shape=(
            jax.ShapeDtypeStruct((layout.peers * layout.block,) + page, arrived.dtype),
            jax.ShapeDtypeStruct((layout.peers * layout.late,), jnp.int32),
        ),
        grid_spec=pltpu.PrefetchScalarGridSpec(
            num_scalar_prefetch=3,
            grid=(1,),
            in_specs=[pl.BlockSpec(memory_space=pl.ANY)] * 2,
            out_specs=(
                pl.BlockSpec(memory_space=pl.ANY),
                pl.BlockSpec(memory_space=pltpu.SMEM),
            ),
            scratch_shapes=scratch(layout, arrived)
            + [pltpu.VMEM(page, arrived.dtype), pltpu.SemaphoreType.DMA],
        ),
        name="place_early",
    )(table, perm, me, arrived, zeros)


def place_late_pages(numbers, arrived, held):
    arrived = arrived.reshape((-1,) + held.shape[1:])
    return pl.pallas_call(
        lambda *refs: place_late_kernel(arrived.shape[0], *refs),
        out_shape=jax.ShapeDtypeStruct(held.shape, held.dtype),
        grid_spec=pltpu.PrefetchScalarGridSpec(
            num_scalar_prefetch=1,
            grid=(1,),
            in_specs=[pl.BlockSpec(memory_space=pl.ANY)] * 2,
            out_specs=pl.BlockSpec(memory_space=pl.ANY),
            scratch_shapes=[
                pltpu.VMEM((BUFFERS,) + held.shape[1:], held.dtype),
                pltpu.SemaphoreType.DMA((BUFFERS,)),
                pltpu.SemaphoreType.DMA((BUFFERS,)),
            ],
        ),
        input_output_aliases={2: 0},
        name="place_late",
    )(numbers, arrived, held)


def attend_kernel(lengths, tables, q_ref, nk_ref, nv_ref, *rest):
    k_refs, v_refs = rest[:BLOCK_PAGES], rest[BLOCK_PAGES : 2 * BLOCK_PAGES]
    out_ref, q_rows, top, total, acc = rest[2 * BLOCK_PAGES :]
    kv_heads, rows, head = q_rows.shape
    tokens = q_ref.shape[0]
    groups = rows // tokens
    slot, step = pl.program_id(0), pl.program_id(1)
    page_len = k_refs[0].shape[1]
    block_keys = BLOCK_PAGES * page_len
    length = lengths[slot]
    inv_scale = 1.0 / math.sqrt(head)

    def score(kv, keys):
        return (
            lax.dot_general(
                q_rows[kv], keys, (((1,), (1,)), ((), ())), preferred_element_type=jnp.float32
            )
            * inv_scale
        )

    @pl.when(step == 0)
    def _():
        for kv in range(kv_heads):
            columns = slice(kv * head, (kv + 1) * head)
            for group in range(groups):
                lane = (kv * groups + group) * head
                q_rows[kv, group * tokens : (group + 1) * tokens, :] = q_ref[:, lane : lane + head]
            scores = score(kv, nk_ref[:, columns])
            query_id = lax.broadcasted_iota(jnp.int32, scores.shape, 0) % tokens
            key_id = lax.broadcasted_iota(jnp.int32, scores.shape, 1)
            scores = jnp.where(key_id <= query_id, scores, -1e30)
            highest = jnp.max(scores, axis=-1, keepdims=True)
            weights = jnp.exp(scores - highest)
            top[kv] = jnp.broadcast_to(highest, (rows, head))
            total[kv] = jnp.broadcast_to(jnp.sum(weights, axis=-1, keepdims=True), (rows, head))
            acc[kv] = jnp.dot(
                weights.astype(jnp.bfloat16), nv_ref[:, columns], preferred_element_type=jnp.float32
            )

    @pl.when(step * block_keys < length)
    def _():
        for kv in range(kv_heads):
            columns = slice(kv * head, (kv + 1) * head)
            keys = jnp.concatenate([ref[0, :, columns] for ref in k_refs], axis=0)
            values = jnp.concatenate([ref[0, :, columns] for ref in v_refs], axis=0)
            scores = score(kv, keys)
            key_id = lax.broadcasted_iota(jnp.int32, scores.shape, 1)
            scores = jnp.where(key_id < length - step * block_keys, scores, -1e30)
            before = top[kv]
            highest = jnp.maximum(before, jnp.max(scores, axis=-1, keepdims=True))
            factor = jnp.exp(before - highest)
            weights = jnp.exp(scores - highest[:, :1])
            top[kv] = highest
            total[kv] = total[kv] * factor + jnp.sum(weights, axis=-1, keepdims=True)
            acc[kv] = acc[kv] * factor + jnp.dot(
                weights.astype(jnp.bfloat16), values, preferred_element_type=jnp.float32
            )

    @pl.when(step == pl.num_programs(1) - 1)
    def _():
        for kv in range(kv_heads):
            context = (acc[kv] / total[kv]).astype(jnp.bfloat16)
            for group in range(groups):
                lane = (kv * groups + group) * head
                out_ref[:, lane : lane + head] = context[group * tokens : (group + 1) * tokens]


def attend(lengths, tables, queries, new_keys, new_values, k_pool, v_pool):
    slots, row_pages = tables.shape
    tokens = queries.shape[0] // slots
    page_len, features = k_pool.shape[1:]
    kv_heads = features // HEAD_SIZE
    rows = tokens * (queries.shape[1] // features)
    steps = row_pages // BLOCK_PAGES

    def page_spec(number):
        def pick(slot, step, lengths, tables):
            last = (lengths[slot] + page_len - 1) // page_len - 1
            return (tables[slot * row_pages + jnp.minimum(step * BLOCK_PAGES + number, last)], 0, 0)

        return pl.BlockSpec((1, page_len, features), pick)

    def slot_rows(slot, step, lengths, tables):
        return (slot, 0)

    pages = [page_spec(number) for number in range(BLOCK_PAGES)]
    state = pltpu.VMEM((kv_heads, rows, HEAD_SIZE), jnp.float32)
    return pl.pallas_call(
        attend_kernel,
        out_shape=jax.ShapeDtypeStruct(queries.shape, jnp.bfloat16),
        grid_spec=pltpu.PrefetchScalarGridSpec(
            num_scalar_prefetch=2,
            grid=(slots, steps),
            in_specs=[
                pl.BlockSpec((tokens, queries.shape[1]), slot_rows),
                pl.BlockSpec((tokens, features), slot_rows),
                pl.BlockSpec((tokens, features), slot_rows),
            ]
            + pages
            + pages,
            out_specs=pl.BlockSpec((tokens, queries.shape[1]), slot_rows),
            scratch_shapes=[
                pltpu.VMEM((kv_heads, rows, HEAD_SIZE), jnp.bfloat16),
                state,
                state,
                state,
            ],
        ),
        compiler_params=pltpu.CompilerParams(
            dimension_semantics=("arbitrary", "arbitrary"), vmem_limit_bytes=40 << 20
        ),
        name="attend",
    )(
        lengths,
        tables.reshape(-1),
        queries,
        new_keys,
        new_values,
        *([k_pool] * BLOCK_PAGES),
        *([v_pool] * BLOCK_PAGES),
    )


LINKS = 3
LANE = 8
LATE_ROUND = 2
FIXED_ROUNDS = 8
ROUND_LIMIT = 56
SLOT_LIMIT = ROUND_LIMIT * LANE
QUEUE = 96
ARRIVALS = 512
HELD = 1024
HELD_PAGES = 384


def neighbours():
    right = [(device, device + 2) for device in range(6)]
    left = [(device + 2, device) for device in range(6)]
    across = [(device, device ^ 1) for device in range(8)]
    return right, left, across


def loop(low, high, body):
    def step(index, carry):
        body(index)
        return carry

    lax.fori_loop(low, high, step, 0)


def plan_kernel(layout, first, table, perm, me, counts, send, *rest):
    if first:
        own_codes, early_first, runs, places, heads, tails = rest
    else:
        receive, rounds = rest[:2]
        own_codes, early_first, runs, places, heads, tails = rest[2:8]
        numbers, held, arrived_device, arrived_run, arrived_place, arrived_count = rest[8:]
    peers, block = layout.peers, layout.block
    own = me[0]
    page_len = layout.page_len

    def total(pair):
        return counts[pair]

    def early(pair):
        return counts[peers * peers + pair]

    def scan(source, target, use):
        whole = [
            lax.div(layout.length(table, perm, source, slot), page_len)
            for slot in range(layout.slots)
        ]
        base = source * layout.width + layout.sends + target * block
        plain, tail_rank = jnp.int32(0), early(source * peers + target)
        for number in range(block):
            code = table[base + number]
            edge = whole[0]
            for slot in range(1, layout.slots):
                low = slot * layout.code_width
                edge = jnp.where(code >= low, whole[slot] + low, edge)
            valid, tail = code >= 0, code >= edge
            use(number, code, valid, jnp.where(tail, tail_rank, plain))
            plain = plain + jnp.where(valid & jnp.logical_not(tail), 1, 0)
            tail_rank = tail_rank + jnp.where(tail, 1, 0)

    def list_own(target):
        def use(number, code, valid, rank):
            @pl.when(valid)
            def _():
                own_codes[target * block + rank] = code

        scan(own, target, use)

    loop(0, peers, list_own)
    if not first:

        def list_numbers(source):
            def use(number, code, valid, rank):
                @pl.when(valid)
                def _():
                    numbers[source * block + rank] = source * block + number

            scan(source, own, use)

        loop(0, peers, list_numbers)

    def clear(index):
        early_first[index] = 0

    loop(0, peers * peers, clear)
    half = peers // 2
    for direction in range(2):
        sources = range(direction * half, (direction + 1) * half)
        targets = range((1 - direction) * half, (2 - direction) * half)
        loads = []
        for column in range(2):
            load = jnp.int32(0)
            for source in sources:
                if source % 2 == column:
                    for target in targets:
                        load = load + total(source * peers + target)
            loads.append(load)
        heavy = jnp.where(loads[1] > loads[0], 1, 0)
        left = lax.div(jnp.abs(loads[0] - loads[1]), 2)
        zs = sorted({source // 2 for source in sources})
        zt = sorted({target // 2 for target in targets})
        for _, a, b in sorted((abs(a - b), a, b) for a in zs for b in zt):
            pair = (2 * a + heavy) * peers + 2 * b + 1 - heavy
            moved = jnp.minimum(left, early(pair))
            early_first[pair] = moved
            left = left - moved

    def clear_queue(index):
        heads[index] = 0
        tails[index] = 0

    loop(0, peers * LINKS * 4, clear_queue)

    def push(device, run, place, turn):
        target = (run >> 10) & 7
        steps = (target >> 1) - (device >> 1)
        flip = (target ^ device) & 1
        across = (steps == 0) | turn
        link = jnp.where(across, 2, jnp.where(steps > 0, 0, 1))
        queue = (device * LINKS + link) * 4 + jnp.abs(steps) + flip - 1
        spot = tails[queue]
        runs[queue * QUEUE + spot] = run
        places[queue * QUEUE + spot] = place
        tails[queue] = spot + 1

    def make_run(pair, start, count):
        return (pair << 10) | (start << 5) | count

    def open_pair(pair):
        source = pair >> 3
        moved = early_first[pair]
        count = early(pair)
        wanted = source != (pair & 7)
        if first:
            wanted = wanted & (source == own)

        @pl.when(wanted & (moved > 0))
        def _():
            push(source, make_run(pair, 0, moved), -1, True)

        @pl.when(wanted & (count > moved))
        def _():
            push(source, make_run(pair, moved, count - moved), -1, False)

    loop(0, peers * peers, open_pair)

    def open_late(pair):
        source = pair >> 3
        count = total(pair) - early(pair)

        @pl.when((source != (pair & 7)) & (count > 0))
        def _():
            push(source, make_run(pair, early(pair), count), -1, False)

    def move(step, device, link, done):
        room = jnp.int32(LANE)
        toward = jnp.where(
            link == 2, device ^ 1, jnp.where(link == 0, device + 2, device - 2)
        )
        for rank in (3, 2, 1, 0):
            queue = (device * LINKS + link) * 4 + rank

            def more(state):
                room, head, done = state
                return (room > 0) & (head < tails[queue])

            def take(state):
                room, head, done = state
                spot = queue * QUEUE + head
                run, place = runs[spot], places[spot]
                pair, start, count = run >> 10, (run >> 5) & 31, run & 31
                taken = jnp.minimum(room, count)
                base = link * SLOT_LIMIT + step * LANE + LANE - room
                final = (pair & 7) == toward

                @pl.when(device == own)
                def _():
                    def note(index):
                        code = own_codes[(pair & 7) * block + start + index]
                        send[base + index] = jnp.where(place < 0, code, HELD + place + index)

                    loop(0, taken, note)

                if not first:
                    slot = held[toward]

                    @pl.when(toward == own)
                    def _():
                        def note(index):
                            number = numbers[(pair >> 3) * block + start + index]
                            receive[base + index] = jnp.where(final, number, HELD + slot + index)

                        loop(0, taken, note)

                    @pl.when(jnp.logical_not(final))
                    def _():
                        held[toward] = slot + taken
                        side = step & 1
                        count = arrived_count[side]
                        at = side * ARRIVALS + count
                        arrived_device[at] = toward
                        arrived_run[at] = make_run(pair, start, taken)
                        arrived_place[at] = slot
                        arrived_count[side] = count + 1

                whole = taken == count

                @pl.when(jnp.logical_not(whole))
                def _():
                    runs[spot] = make_run(pair, start + taken, count - taken)
                    places[spot] = jnp.where(place < 0, place, place + taken)

                return (
                    room - taken,
                    head + jnp.where(whole, 1, 0),
                    done + jnp.where(final, taken, 0),
                )

            head = heads[queue]
            room, head, done = lax.while_loop(more, take, (room, head, done))
            heads[queue] = head
        return done

    def blank(step):
        def one(index):
            for link in range(LINKS):
                spot = link * SLOT_LIMIT + step * LANE + index
                send[spot] = -1
                if not first:
                    receive[spot] = -1

        loop(0, LANE, one)

    if first:
        for step in range(LATE_ROUND):
            blank(step)
            for link in range(LINKS):
                move(step, own, link, jnp.int32(0))
        return

    wanted = jnp.int32(0)
    for source in range(peers):
        held[source] = 0
        for target in range(peers):
            if source != target:
                wanted = wanted + total(source * peers + target)
    arrived_count[0] = 0
    arrived_count[1] = 0

    def unfinished(state):
        step, done = state
        return (step <= FIXED_ROUNDS) | (done < wanted)

    def advance(state):
        step, done = state
        blank(step)

        @pl.when(step == LATE_ROUND)
        def _():
            loop(0, peers * peers, open_late)

        side = step & 1

        def arrive(index):
            at = side * ARRIVALS + index
            push(arrived_device[at], arrived_run[at], arrived_place[at], False)

        loop(0, arrived_count[side], arrive)
        arrived_count[side] = 0

        def one(index, done):
            device = lax.div(index, LINKS)
            return move(step, device, index - device * LINKS, done)

        done = lax.fori_loop(0, peers * LINKS, one, done)

        @pl.when(done >= wanted)
        def _():
            rounds[0] = jnp.minimum(rounds[0], step + 1)

        return step + 1, done

    rounds[0] = jnp.int32(ROUND_LIMIT)
    rounds[1] = jnp.int32(0)
    end, _ = lax.while_loop(unfinished, advance, (jnp.int32(0), jnp.int32(0)))
    blank(end)


def plan(layout, first, table, perm, me, counts):
    tables = jax.ShapeDtypeStruct((LINKS * SLOT_LIMIT,), jnp.int32)
    outs = (tables,) if first else (tables, tables, jax.ShapeDtypeStruct((2,), jnp.int32))
    peers = layout.peers

    def words(count):
        return pltpu.SMEM((count,), jnp.int32)

    queues = peers * LINKS * 4
    room = [
        words(peers * layout.block),
        words(peers * peers),
        words(queues * QUEUE),
        words(queues * QUEUE),
        words(queues),
        words(queues),
    ]
    if not first:
        room += [words(peers * layout.block), words(peers)]
        room += [words(2 * ARRIVALS)] * 3 + [words(2)]
    out = pl.pallas_call(
        lambda *refs: plan_kernel(layout, first, *refs),
        out_shape=outs,
        grid_spec=pltpu.PrefetchScalarGridSpec(
            num_scalar_prefetch=4,
            grid=(1,),
            in_specs=[],
            out_specs=tuple(pl.BlockSpec(memory_space=pltpu.SMEM) for _ in outs),
            scratch_shapes=room,
        ),
        name="plan_first" if first else "plan_rest",
    )(table, perm, me, counts)
    return out[0] if first else out


def own_page(layout, table, perm, me, pool, recent, zeros, code, target, sem):
    slot, page = layout.split(code)
    cached = pool.at[layout.physical(table, perm, me[0], slot, page)]
    if recent is None:
        pltpu.make_async_copy(cached, target, sem).start()
        return
    page_len = layout.page_len
    length = layout.length(table, perm, me[0], slot)
    full, kept = lax.div(length, page_len), lax.rem(length, page_len)

    @pl.when(page < full)
    def _():
        pltpu.make_async_copy(cached, target, sem).start()

    @pl.when(page == full)
    def _():
        copy_rows(cached, 0, target, 0, kept, sem)
        copy_rows(recent.at[slot], 0, target, kept, page_len - kept, sem)

    @pl.when(page > full)
    def _():
        copy_rows(recent.at[slot], page_len - kept, target, 0, kept, sem)
        copy_rows(zeros, 0, target, kept, page_len - kept, sem)


def step_kernel(layout, kind, table, perm, me, step, send, *rest):
    if kind == "first":
        pool, *lanes, send_sems = rest
        recent = zeros = None
    elif kind == "step":
        receive, pool, recent, zeros = rest[:4]
        arrived = rest[4:7]
        out, held, *lanes = rest[9:14]
        send_sems, receive_sems = rest[14:]
    else:
        receive = send
        arrived = rest[:3]
        out, receive_sems = rest[4:]
    if kind == "first":
        base = step[0] * LANE
    else:
        base = step[0] * LANE
        past = base - (2 * LANE if kind == "step" else LANE)

        def land(index):
            for link in range(LINKS):
                to = receive[link * SLOT_LIMIT + past + index]
                sem = receive_sems.at[link, index]

                @pl.when((to >= 0) & (to < HELD))
                def _():
                    pltpu.make_async_copy(arrived[link].at[index], out.at[to], sem).start()

                if kind == "step":

                    @pl.when(to >= HELD)
                    def _():
                        pltpu.make_async_copy(
                            arrived[link].at[index], held.at[to - HELD], sem
                        ).start()

        loop(0, LANE, land)

    def fetch(index):
        for link in range(LINKS):
            code = send[link * SLOT_LIMIT + base + index]

            @pl.when((code >= 0) & (code < HELD))
            def _():
                own_page(
                    layout, table, perm, me, pool, recent, zeros, code,
                    lanes[link].at[index], send_sems.at[link, index],
                )

    if kind != "last":
        loop(0, LANE, fetch)

    if kind != "first":

        def landed(index):
            for link in range(LINKS):
                to = receive[link * SLOT_LIMIT + past + index]

                @pl.when((to >= 0) & ((to < HELD) | (kind == "step")))
                def _():
                    pltpu.make_async_copy(
                        arrived[link].at[0], out.at[0], receive_sems.at[link, index]
                    ).wait()

        loop(0, LANE, landed)

    if kind == "step":

        def forward(index):
            for link in range(LINKS):
                code = send[link * SLOT_LIMIT + base + index]

                @pl.when(code >= HELD)
                def _():
                    pltpu.make_async_copy(
                        held.at[code - HELD], lanes[link].at[index], send_sems.at[link, index]
                    ).start()

        loop(0, LANE, forward)

    if kind != "last":

        def fetched(index):
            for link in range(LINKS):
                code = send[link * SLOT_LIMIT + base + index]

                @pl.when(code >= 0)
                def _():
                    pltpu.make_async_copy(
                        pool.at[0], lanes[link].at[0], send_sems.at[link, index]
                    ).wait()

        loop(0, LANE, fetched)


def any_specs(count):
    return [pl.BlockSpec(memory_space=pl.ANY)] * count


def lane_shapes(pool):
    lane = jax.ShapeDtypeStruct((LANE,) + pool.shape[1:], pool.dtype)
    return (lane,) * LINKS


SEMS = pltpu.SemaphoreType.DMA((LINKS, LANE))


def pack_first(layout, table, perm, me, step, send, pool):
    return pl.pallas_call(
        lambda *refs: step_kernel(layout, "first", *refs),
        out_shape=lane_shapes(pool),
        grid_spec=pltpu.PrefetchScalarGridSpec(
            num_scalar_prefetch=5,
            grid=(1,),
            in_specs=any_specs(1),
            out_specs=tuple(any_specs(LINKS)),
            scratch_shapes=[SEMS],
        ),
        name="pack_first",
    )(table, perm, me, step, send, pool)


def relay(layout, table, perm, me, step, send, receive, pool, recent, zeros, arrived, out, held):
    results = pl.pallas_call(
        lambda *refs: step_kernel(layout, "step", *refs),
        out_shape=(
            jax.ShapeDtypeStruct(out.shape, out.dtype),
            jax.ShapeDtypeStruct(held.shape, held.dtype),
        )
        + lane_shapes(pool),
        grid_spec=pltpu.PrefetchScalarGridSpec(
            num_scalar_prefetch=6,
            grid=(1,),
            in_specs=any_specs(8),
            out_specs=tuple(any_specs(2 + LINKS)),
            scratch_shapes=[SEMS, SEMS],
        ),
        input_output_aliases={12: 0, 13: 1},
        name="relay",
    )(table, perm, me, step, send, receive, pool, recent, zeros, *arrived, out, held)
    return results[2:], results[0], results[1]


def land_last(layout, table, perm, me, step, receive, arrived, out):
    return pl.pallas_call(
        lambda *refs: step_kernel(layout, "last", *refs),
        out_shape=jax.ShapeDtypeStruct(out.shape, out.dtype),
        grid_spec=pltpu.PrefetchScalarGridSpec(
            num_scalar_prefetch=5,
            grid=(1,),
            in_specs=any_specs(4),
            out_specs=pl.BlockSpec(memory_space=pl.ANY),
            scratch_shapes=[SEMS],
        ),
        input_output_aliases={8: 0},
        name="land_last",
    )(table, perm, me, step, receive, *arrived, out)


def fill_kernel(layout, table, perm, me, pool, recent, zeros, out, held, blank, sems, blank_sem):
    del held
    fill = pltpu.make_async_copy(zeros, blank, blank_sem)
    fill.start()
    fill.wait()
    count = layout.peers * layout.block

    def code_of(index):
        source = lax.div(index, layout.block)
        number = index - source * layout.block
        at = source * layout.width + layout.sends + me[0] * layout.block + number
        return source, table[at]

    def finish(index):
        source, code = code_of(index)

        @pl.when((code < 0) | (source == me[0]))
        def _():
            pltpu.make_async_copy(blank, out.at[0], sems.at[index & (BUFFERS - 1)]).wait()

    def begin(index):
        @pl.when(index >= BUFFERS)
        def _():
            finish(index - BUFFERS)

        source, code = code_of(index)
        sem = sems.at[index & (BUFFERS - 1)]

        @pl.when(code < 0)
        def _():
            pltpu.make_async_copy(blank, out.at[index], sem).start()

        @pl.when((code >= 0) & (source == me[0]))
        def _():
            own_page(layout, table, perm, me, pool, recent, zeros, code, out.at[index], sem)

    loop(0, count, begin)
    loop(max(count - BUFFERS, 0), count, finish)


def fill_local(layout, table, perm, me, pool, recent, zeros):
    page = pool.shape[1:]
    return pl.pallas_call(
        lambda *refs: fill_kernel(layout, *refs),
        out_shape=(
            jax.ShapeDtypeStruct((layout.peers * layout.block,) + page, pool.dtype),
            jax.ShapeDtypeStruct((HELD_PAGES,) + page, pool.dtype),
        ),
        grid_spec=pltpu.PrefetchScalarGridSpec(
            num_scalar_prefetch=3,
            grid=(1,),
            in_specs=any_specs(3),
            out_specs=tuple(any_specs(2)),
            scratch_shapes=[
                pltpu.VMEM(page, pool.dtype),
                pltpu.SemaphoreType.DMA((BUFFERS,)),
                pltpu.SemaphoreType.DMA,
            ],
        ),
        name="fill_local",
    )(table, perm, me, pool, recent, zeros)


def page_counts(layout, by_device, perm):
    lengths = by_device[:, : layout.slots].reshape(-1)[perm].reshape(layout.peers, layout.slots)
    whole = lax.div(lengths, layout.page_len)
    codes = by_device[:, layout.sends : layout.used].reshape(
        layout.peers, layout.peers, layout.block
    )
    edge = whole[:, 0, None, None]
    for slot in range(1, layout.slots):
        low = slot * layout.code_width
        edge = jnp.where(codes >= low, whole[:, slot, None, None] + low, edge)
    valid = codes >= 0
    plain = valid & (codes < edge)
    return jnp.concatenate(
        [
            jnp.sum(valid.astype(jnp.int32), axis=-1).reshape(-1),
            jnp.sum(plain.astype(jnp.int32), axis=-1).reshape(-1),
        ]
    )


def hop(lanes):
    return tuple(
        lax.ppermute(lane, "req", pairs) for lane, pairs in zip(lanes, neighbours())
    )


def number(value):
    return jnp.asarray(value, jnp.int32).reshape(1)


def grid_shards(hidden, norm_gain, wq, wkv, wo, perm, prior_len, page_table, pool, send_table):
    slots = prior_len.shape[0]
    tokens = hidden.shape[0] // slots
    _, peers, block = send_table.shape
    layout = Layout(slots, page_table.shape[1], peers, block)
    layout.page_len = pool.shape[1]
    features = pool.shape[-1]
    device = lax.axis_index("req")
    me = device.astype(jnp.int32).reshape(1)
    mine = jnp.concatenate([prior_len, page_table.reshape(-1), send_table.reshape(-1)])
    mine = jnp.pad(mine, (0, layout.width - layout.used)).reshape(-1, 128)
    by_device = exchange(peers, mine)
    table = by_device.reshape(-1)
    by_device = by_device.reshape(peers, layout.width)
    counts = page_counts(layout, by_device, perm)
    first = plan(layout, True, table, perm, me, counts)
    lanes = [pack_first(layout, table, perm, me, number(step), first, pool) for step in range(2)]
    arrived = [hop(lane) for lane in lanes]

    full_rows = lax.all_gather(hidden, "tp", axis=1, tiled=True)
    late_pool, wkv, _ = lax.optimization_barrier((pool, wkv, lanes[1][2]))
    requests = lax.dynamic_slice_in_dim(perm, device * slots, slots)
    lengths = by_device[:, :slots].reshape(-1)[requests]
    tables = by_device[:, slots : layout.sends].reshape(-1, layout.row_pages)[requests]

    normalized_input = normalize(full_rows, norm_gain)
    pair_proj = jnp.dot(
        normalized_input, wkv.reshape(wkv.shape[0], -1), preferred_element_type=jnp.float32
    )
    positions = (lengths[:, None] + jnp.arange(tokens, dtype=jnp.int32)[None, :]).reshape(-1)
    pair_heads = pair_proj.reshape(pair_proj.shape[0], 2, -1, HEAD_SIZE)
    new_keys = rotate(pair_heads[:, 0], positions).astype(jnp.bfloat16).reshape(-1, features)
    new_values = pair_heads[:, 1].astype(jnp.bfloat16).reshape(-1, features)
    recent = jnp.stack([new_keys, new_values], axis=1).reshape(slots, tokens, 2, features)
    zeros = jnp.zeros(pool.shape[1:], pool.dtype)
    send, receive, rounds = plan(layout, False, table, perm, me, counts)
    out, held = fill_local(layout, table, perm, me, pool, recent, zeros)

    query_proj = jnp.dot(normalized_input, wq, preferred_element_type=jnp.float32)
    queries = rotate(query_proj.reshape(query_proj.shape[0], -1, HEAD_SIZE), positions).astype(
        jnp.bfloat16
    )
    context = attend(
        lengths,
        tables,
        queries.reshape(queries.shape[0], -1),
        new_keys,
        new_values,
        late_pool[:, :, 0],
        late_pool[:, :, 1],
    )
    partial_value = jnp.dot(context, wo, preferred_element_type=jnp.float32)
    attn_out = lax.psum_scatter(
        partial_value.astype(jnp.bfloat16), "tp", scatter_dimension=1, tiled=True
    )

    def advance(step, landed, out, held):
        return relay(
            layout, table, perm, me, number(step), send, receive, pool, recent, zeros,
            landed, out, held,
        )

    for step in range(2, FIXED_ROUNDS):
        lane, out, held = advance(step, arrived[step - 2], out, held)
        arrived.append(hop(lane))
    lane, out, held = advance(FIXED_ROUNDS, arrived[FIXED_ROUNDS - 2], out, held)

    def unfinished(state):
        return state[0] < rounds[0]

    def turn(state):
        step, lane, landed, out, held = state
        coming = hop(lane)
        lane, out, held = advance(step + 1, landed, out, held)
        return step + 1, lane, coming, out, held

    step, _, landed, out, _ = lax.while_loop(
        unfinished, turn, (jnp.int32(FIXED_ROUNDS), lane, arrived[-1], out, held)
    )
    decode_pages = land_last(layout, table, perm, me, number(step), receive, landed, out)
    return (attn_out, decode_pages.reshape((1, peers, block) + pool.shape[1:]))


def shards(hidden, norm_gain, wq, wkv, wo, perm, prior_len, page_table, pool, send_table):
    slots = prior_len.shape[0]
    tokens = hidden.shape[0] // slots
    _, peers, block = send_table.shape
    layout = Layout(slots, page_table.shape[1], peers, block)
    features = pool.shape[-1]
    device = lax.axis_index("req")
    me = device.astype(jnp.int32).reshape(1)
    mine = jnp.concatenate([prior_len, page_table.reshape(-1), send_table.reshape(-1)])
    mine = jnp.pad(mine, (0, layout.width - layout.used)).reshape(-1, 128)
    by_device = exchange(peers, mine)
    table = by_device.reshape(-1)
    by_device = by_device.reshape(peers, layout.width)
    outgoing = pack_pages(layout, table, perm, me, pool)
    arrived = lax.all_to_all(outgoing, "req", split_axis=0, concat_axis=0, tiled=True)

    full_rows = lax.all_gather(hidden, "tp", axis=1, tiled=True)
    late_pool, wkv, outgoing = lax.optimization_barrier((pool, wkv, outgoing))
    requests = lax.dynamic_slice_in_dim(perm, device * slots, slots)
    lengths = by_device[:, :slots].reshape(-1)[requests]
    tables = by_device[:, slots : layout.sends].reshape(-1, layout.row_pages)[requests]

    normalized_input = normalize(full_rows, norm_gain)
    query_proj = jnp.dot(normalized_input, wq, preferred_element_type=jnp.float32)
    pair_proj = jnp.dot(
        normalized_input, wkv.reshape(wkv.shape[0], -1), preferred_element_type=jnp.float32
    )
    positions = (lengths[:, None] + jnp.arange(tokens, dtype=jnp.int32)[None, :]).reshape(-1)
    queries = rotate(query_proj.reshape(query_proj.shape[0], -1, HEAD_SIZE), positions).astype(
        jnp.bfloat16
    )
    pair_heads = pair_proj.reshape(pair_proj.shape[0], 2, -1, HEAD_SIZE)
    new_keys = rotate(pair_heads[:, 0], positions).astype(jnp.bfloat16).reshape(-1, features)
    new_values = pair_heads[:, 1].astype(jnp.bfloat16).reshape(-1, features)
    recent = jnp.stack([new_keys, new_values], axis=1).reshape(slots, tokens, 2, features)
    context = attend(
        lengths,
        tables,
        queries.reshape(queries.shape[0], -1),
        new_keys,
        new_values,
        late_pool[:, :, 0],
        late_pool[:, :, 1],
    )
    partial_value = jnp.dot(context, wo, preferred_element_type=jnp.float32)
    recent, partial_value = lax.optimization_barrier((recent, partial_value))
    attn_out = lax.psum_scatter(
        partial_value.astype(jnp.bfloat16), "tp", scatter_dimension=1, tiled=True
    )
    zeros = jnp.zeros(pool.shape[1:], pool.dtype)
    late_arrived = lax.all_to_all(
        pack_pages(layout, table, perm, me, late_pool, recent, zeros),
        "req",
        split_axis=0,
        concat_axis=0,
        tiled=True,
    )
    early_pages, numbers = place_early_pages(layout, table, perm, me, arrived, zeros)
    decode_pages = place_late_pages(numbers, late_arrived, early_pages)
    return (attn_out, decode_pages.reshape((1, peers, block) + pool.shape[1:]))


def solution(mesh):
    placed = (
        P("req", "tp"),
        P(),
        P(None, "tp"),
        P(None, None, "tp"),
        P("tp", None),
        P(),
        P("req"),
        P("req", None),
        P("req", None, None, "tp"),
        P("req", None, None),
    )
    return jax.shard_map(
        grid_shards if mesh.shape["req"] == 8 else shards,
        mesh=mesh,
        in_specs=placed,
        out_specs=(P("req", "tp"), P("req", None, None, None, None, "tp")),
        check_vma=False,
    )
```

```python
import math

import jax
import jax.numpy as jnp
from jax import lax
from jax.experimental import pallas as pl
from jax.experimental.pallas import tpu as pltpu
from jax.sharding import PartitionSpec as P

HEAD_SIZE = 128
NORM_EPSILON = 1e-05
ROPE_THETA = 100000000.0
BLOCK_PAGES = 4


def normalize(rows, gain):
    wide_rows = rows.astype(jnp.float32)
    mean_square = jnp.mean(wide_rows * wide_rows, axis=-1, keepdims=True)
    return (wide_rows * lax.rsqrt(mean_square + NORM_EPSILON) * gain.astype(jnp.float32)).astype(
        jnp.bfloat16
    )


def rotate(vectors, positions):
    half_size = vectors.shape[-1] // 2
    frequency = jnp.power(
        jnp.float32(ROPE_THETA), -2.0 * jnp.arange(half_size, dtype=jnp.float32) / vectors.shape[-1]
    )
    angles = positions.astype(jnp.float32)[:, None] * frequency[None, :]
    cosine = jnp.cos(angles)[:, None, :]
    sine_part = jnp.sin(angles)[:, None, :]
    first_half = vectors[..., :half_size]
    second_half = vectors[..., half_size:]
    return jnp.concatenate(
        [
            first_half * cosine - second_half * sine_part,
            second_half * cosine + first_half * sine_part,
        ],
        axis=-1,
    )


class Layout:
    def __init__(self, slots, row_pages, peers, block):
        self.slots, self.row_pages, self.peers, self.block = slots, row_pages, peers, block
        self.code_width = row_pages + 1
        self.sends = slots + slots * row_pages
        self.used = self.sends + peers * block
        self.width = -(-self.used // 1024) * 1024
        self.late = 2 * slots
        self.early = block - self.late

    def request(self, perm, device, slot):
        request = perm[device * self.slots + slot]
        return lax.div(request, self.slots) * self.width, lax.rem(request, self.slots)

    def length(self, table, perm, device, slot):
        base, row = self.request(perm, device, slot)
        return table[base + row]

    def physical(self, table, perm, device, slot, page):
        base, row = self.request(perm, device, slot)
        return table[base + self.slots + row * self.row_pages + jnp.minimum(page, self.row_pages - 1)]

    def split(self, code):
        return lax.div(code, self.code_width), lax.rem(code, self.code_width)

    def visit(self, table, perm, source, target, page_len, use):
        whole = [
            lax.div(self.length(table, perm, source, slot), page_len) for slot in range(self.slots)
        ]
        base = source * self.width + self.sends + target * self.block
        plain, tails = jnp.int32(0), jnp.int32(self.block - 1)
        for number in range(self.block):
            code = table[base + number]
            first = whole[0]
            for slot in range(1, self.slots):
                low = slot * self.code_width
                first = jnp.where(code >= low, whole[slot] + low, first)
            valid, tail = code >= 0, code >= first
            place = jnp.where(valid, jnp.where(tail, tails, plain), -1)
            use(number, code, place)
            plain = plain + jnp.where(valid & jnp.logical_not(tail), 1, 0)
            tails = tails - jnp.where(tail, 1, 0)


def exchange_kernel(peers, mine, out, send_sems, recv_sems):
    me = lax.axis_index("req")
    barrier = pltpu.get_barrier_semaphore()
    for hop in range(1, peers):
        pl.semaphore_signal(
            barrier,
            inc=1,
            device_id={"req": lax.rem(me + hop, peers)},
            device_id_type=pl.DeviceIdType.MESH,
        )
    pl.semaphore_wait(barrier, peers - 1)
    copies = []
    for hop in range(1, peers):
        copy = pltpu.make_async_remote_copy(
            src_ref=mine,
            dst_ref=out.at[me],
            send_sem=send_sems.at[hop - 1],
            recv_sem=recv_sems.at[hop - 1],
            device_id={"req": lax.rem(me + hop, peers)},
            device_id_type=pl.DeviceIdType.MESH,
        )
        copy.start()
        copies.append(copy)
    out[me] = mine[...]
    for copy in copies:
        copy.wait()


def exchange(peers, mine):
    return pl.pallas_call(
        lambda *refs: exchange_kernel(peers, *refs),
        out_shape=jax.ShapeDtypeStruct((peers,) + mine.shape, mine.dtype),
        in_specs=[pl.BlockSpec(memory_space=pltpu.VMEM)],
        out_specs=pl.BlockSpec(memory_space=pltpu.VMEM),
        scratch_shapes=[
            pltpu.SemaphoreType.DMA((peers - 1,)),
            pltpu.SemaphoreType.DMA((peers - 1,)),
        ],
        compiler_params=pltpu.CompilerParams(collective_id=0, has_side_effects=True),
        name="exchange",
    )(mine)


BUFFERS = 32
AHEAD = 16


def ring(count, load, store, drain):
    def step(index, carry):
        @pl.when(index < count)
        def _():
            @pl.when(index >= BUFFERS)
            def _():
                drain(index - BUFFERS)

            load(index)

        @pl.when(index >= AHEAD)
        def _():
            store(index - AHEAD)

        return carry

    lax.fori_loop(0, count + AHEAD, step, 0)

    def last(index, carry):
        drain(index)
        return carry

    lax.fori_loop(max(count - BUFFERS, 0), count, last, 0)


def copy_rows(source, source_row, target, target_row, count, sem):
    size = target.shape[0]
    while size:
        offset = lax.div(count, 2 * size) * (2 * size)

        @pl.when(lax.rem(lax.div(count, size), 2) == 1)
        def _(size=size, offset=offset):
            pltpu.make_async_copy(
                source.at[pl.ds(source_row + offset, size)],
                target.at[pl.ds(target_row + offset, size)],
                sem,
            ).start()

        size //= 2


def pack_kernel(layout, late, table, perm, me, pool, *rest):
    if late:
        recent, zeros, out, codes, buffers, in_sems, out_sems = rest
    else:
        out, codes, buffers, in_sems, out_sems = rest
    page_len = buffers.shape[1]
    span = layout.late if late else layout.early
    start = layout.early if late else 0
    count = layout.peers * span

    def clear(index, carry):
        codes[index] = 0
        return carry

    lax.fori_loop(0, count, clear, 0)
    starts = []
    for slot in range(layout.slots):
        base, row = layout.request(perm, me[0], slot)
        starts.append(
            base + layout.slots + row * layout.row_pages - slot * layout.code_width
        )

    def block(target, carry):
        def use(number, code, place):
            inside = (place >= start) & (place < start + span)
            item = code
            if not late:
                origin = starts[0]
                for slot in range(1, layout.slots):
                    origin = jnp.where(code >= slot * layout.code_width, starts[slot], origin)
                item = table[jnp.where(inside, origin + code, 0)]

            @pl.when(inside)
            def _():
                codes[target * span + place - start] = item

        layout.visit(table, perm, me[0], target, page_len, use)
        return carry

    lax.fori_loop(0, layout.peers, block, 0)

    def load(index):
        spot = index & (BUFFERS - 1)
        target, sem = buffers.at[spot], in_sems.at[spot]
        if not late:
            pltpu.make_async_copy(pool.at[codes[index]], target, sem).start()
            return
        slot, page = layout.split(codes[index])
        cached = pool.at[layout.physical(table, perm, me[0], slot, page)]
        length = layout.length(table, perm, me[0], slot)
        full, kept = lax.div(length, page_len), lax.rem(length, page_len)

        @pl.when(page < full)
        def _():
            pltpu.make_async_copy(cached, target, sem).start()

        @pl.when(page == full)
        def _():
            copy_rows(cached, 0, target, 0, kept, sem)
            copy_rows(recent.at[slot], 0, target, kept, page_len - kept, sem)

        @pl.when(page > full)
        def _():
            copy_rows(recent.at[slot], page_len - kept, target, 0, kept, sem)
            copy_rows(zeros, 0, target, kept, page_len - kept, sem)

    def outward(index):
        spot = index & (BUFFERS - 1)
        return pltpu.make_async_copy(buffers.at[spot], out.at[index], out_sems.at[spot])

    def store(index):
        spot = index & (BUFFERS - 1)
        pltpu.make_async_copy(pool.at[0], buffers.at[spot], in_sems.at[spot]).wait()
        outward(index).start()

    ring(count, load, store, lambda index: outward(index).wait())


def scratch(layout, pool):
    return [
        pltpu.SMEM((layout.peers * layout.block,), jnp.int32),
        pltpu.VMEM((BUFFERS,) + pool.shape[-3:], pool.dtype),
        pltpu.SemaphoreType.DMA((BUFFERS,)),
        pltpu.SemaphoreType.DMA((BUFFERS,)),
    ]


def pack_pages(layout, table, perm, me, pool, *fresh):
    late = bool(fresh)
    span = layout.late if late else layout.early
    return pl.pallas_call(
        lambda *refs: pack_kernel(layout, late, *refs),
        out_shape=jax.ShapeDtypeStruct((layout.peers * span,) + pool.shape[1:], pool.dtype),
        grid_spec=pltpu.PrefetchScalarGridSpec(
            num_scalar_prefetch=3,
            grid=(1,),
            in_specs=[pl.BlockSpec(memory_space=pl.ANY)] * (1 + len(fresh)),
            out_specs=pl.BlockSpec(memory_space=pl.ANY),
            scratch_shapes=scratch(layout, pool),
        ),
        name="pack_late" if late else "pack_early",
    )(table, perm, me, pool, *fresh).reshape((layout.peers, span) + pool.shape[1:])


def place_kernel(layout, table, perm, me, arrived, zeros, *rest):
    out, numbers, places, buffers, in_sems, out_sems, blank, blank_sem = rest
    page_len = buffers.shape[1]

    def clear(index, carry):
        numbers[index] = -1
        return carry

    lax.fori_loop(0, layout.peers * layout.late, clear, 0)
    fill = pltpu.make_async_copy(zeros, blank, blank_sem)
    fill.start()

    def block(source, carry):
        def use(number, code, place):
            places[source * layout.block + number] = place

            @pl.when(place >= layout.early)
            def _():
                late_index = source * layout.late + place - layout.early
                numbers[late_index] = source * layout.block + number

        layout.visit(table, perm, source, me[0], page_len, use)
        return carry

    lax.fori_loop(0, layout.peers, block, 0)
    fill.wait()

    def inward(index):
        spot = index & (BUFFERS - 1)
        place = jnp.clip(places[index], 0, layout.early - 1)
        return pltpu.make_async_copy(
            arrived.at[lax.div(index, layout.block), place], buffers.at[spot], in_sems.at[spot]
        )

    def outward(index, held):
        return pltpu.make_async_copy(held, out.at[index], out_sems.at[index & (BUFFERS - 1)])

    def is_early(index):
        return (places[index] >= 0) & (places[index] < layout.early)

    def load(index):
        @pl.when(is_early(index))
        def _():
            inward(index).start()

    def store(index):
        @pl.when(is_early(index))
        def _():
            inward(index).wait()
            outward(index, buffers.at[index & (BUFFERS - 1)]).start()

        @pl.when(places[index] < 0)
        def _():
            outward(index, blank).start()

    def drain(index):
        @pl.when(places[index] < layout.early)
        def _():
            outward(index, blank).wait()

    ring(layout.peers * layout.block, load, store, drain)


def place_late_kernel(count, numbers, arrived, held, out, buffers, in_sems, out_sems):
    def inward(index):
        spot = index & (BUFFERS - 1)
        return pltpu.make_async_copy(arrived.at[index], buffers.at[spot], in_sems.at[spot])

    def outward(index):
        spot = index & (BUFFERS - 1)
        target = out.at[jnp.maximum(numbers[index], 0)]
        return pltpu.make_async_copy(buffers.at[spot], target, out_sems.at[spot])

    def load(index):
        @pl.when(numbers[index] >= 0)
        def _():
            inward(index).start()

    def store(index):
        @pl.when(numbers[index] >= 0)
        def _():
            inward(index).wait()
            outward(index).start()

    def drain(index):
        @pl.when(numbers[index] >= 0)
        def _():
            outward(index).wait()

    ring(count, load, store, drain)


def place_early_pages(layout, table, perm, me, arrived, zeros):
    page = arrived.shape[2:]
    return pl.pallas_call(
        lambda *refs: place_kernel(layout, *refs),
        out_shape=(
            jax.ShapeDtypeStruct((layout.peers * layout.block,) + page, arrived.dtype),
            jax.ShapeDtypeStruct((layout.peers * layout.late,), jnp.int32),
        ),
        grid_spec=pltpu.PrefetchScalarGridSpec(
            num_scalar_prefetch=3,
            grid=(1,),
            in_specs=[pl.BlockSpec(memory_space=pl.ANY)] * 2,
            out_specs=(
                pl.BlockSpec(memory_space=pl.ANY),
                pl.BlockSpec(memory_space=pltpu.SMEM),
            ),
            scratch_shapes=scratch(layout, arrived)
            + [pltpu.VMEM(page, arrived.dtype), pltpu.SemaphoreType.DMA],
        ),
        name="place_early",
    )(table, perm, me, arrived, zeros)


def place_late_pages(numbers, arrived, held):
    arrived = arrived.reshape((-1,) + held.shape[1:])
    return pl.pallas_call(
        lambda *refs: place_late_kernel(arrived.shape[0], *refs),
        out_shape=jax.ShapeDtypeStruct(held.shape, held.dtype),
        grid_spec=pltpu.PrefetchScalarGridSpec(
            num_scalar_prefetch=1,
            grid=(1,),
            in_specs=[pl.BlockSpec(memory_space=pl.ANY)] * 2,
            out_specs=pl.BlockSpec(memory_space=pl.ANY),
            scratch_shapes=[
                pltpu.VMEM((BUFFERS,) + held.shape[1:], held.dtype),
                pltpu.SemaphoreType.DMA((BUFFERS,)),
                pltpu.SemaphoreType.DMA((BUFFERS,)),
            ],
        ),
        input_output_aliases={2: 0},
        name="place_late",
    )(numbers, arrived, held)


def attend_kernel(lengths, tables, q_ref, nk_ref, nv_ref, *rest):
    k_refs, v_refs = rest[:BLOCK_PAGES], rest[BLOCK_PAGES : 2 * BLOCK_PAGES]
    out_ref, q_rows, top, total, acc = rest[2 * BLOCK_PAGES :]
    kv_heads, rows, head = q_rows.shape
    tokens = q_ref.shape[0]
    groups = rows // tokens
    slot, step = pl.program_id(0), pl.program_id(1)
    page_len = k_refs[0].shape[1]
    block_keys = BLOCK_PAGES * page_len
    length = lengths[slot]
    inv_scale = 1.0 / math.sqrt(head)

    def score(kv, keys):
        return (
            lax.dot_general(
                q_rows[kv], keys, (((1,), (1,)), ((), ())), preferred_element_type=jnp.float32
            )
            * inv_scale
        )

    @pl.when(step == 0)
    def _():
        for kv in range(kv_heads):
            columns = slice(kv * head, (kv + 1) * head)
            for group in range(groups):
                lane = (kv * groups + group) * head
                q_rows[kv, group * tokens : (group + 1) * tokens, :] = q_ref[:, lane : lane + head]
            scores = score(kv, nk_ref[:, columns])
            query_id = lax.broadcasted_iota(jnp.int32, scores.shape, 0) % tokens
            key_id = lax.broadcasted_iota(jnp.int32, scores.shape, 1)
            scores = jnp.where(key_id <= query_id, scores, -1e30)
            highest = jnp.max(scores, axis=-1, keepdims=True)
            weights = jnp.exp(scores - highest)
            top[kv] = jnp.broadcast_to(highest, (rows, head))
            total[kv] = jnp.broadcast_to(jnp.sum(weights, axis=-1, keepdims=True), (rows, head))
            acc[kv] = jnp.dot(
                weights.astype(jnp.bfloat16), nv_ref[:, columns], preferred_element_type=jnp.float32
            )

    @pl.when(step * block_keys < length)
    def _():
        for kv in range(kv_heads):
            columns = slice(kv * head, (kv + 1) * head)
            keys = jnp.concatenate([ref[0, :, columns] for ref in k_refs], axis=0)
            values = jnp.concatenate([ref[0, :, columns] for ref in v_refs], axis=0)
            scores = score(kv, keys)
            key_id = lax.broadcasted_iota(jnp.int32, scores.shape, 1)
            scores = jnp.where(key_id < length - step * block_keys, scores, -1e30)
            before = top[kv]
            highest = jnp.maximum(before, jnp.max(scores, axis=-1, keepdims=True))
            factor = jnp.exp(before - highest)
            weights = jnp.exp(scores - highest[:, :1])
            top[kv] = highest
            total[kv] = total[kv] * factor + jnp.sum(weights, axis=-1, keepdims=True)
            acc[kv] = acc[kv] * factor + jnp.dot(
                weights.astype(jnp.bfloat16), values, preferred_element_type=jnp.float32
            )

    @pl.when(step == pl.num_programs(1) - 1)
    def _():
        for kv in range(kv_heads):
            context = (acc[kv] / total[kv]).astype(jnp.bfloat16)
            for group in range(groups):
                lane = (kv * groups + group) * head
                out_ref[:, lane : lane + head] = context[group * tokens : (group + 1) * tokens]


def attend(lengths, tables, queries, new_keys, new_values, k_pool, v_pool):
    slots, row_pages = tables.shape
    tokens = queries.shape[0] // slots
    page_len, features = k_pool.shape[1:]
    kv_heads = features // HEAD_SIZE
    rows = tokens * (queries.shape[1] // features)
    steps = row_pages // BLOCK_PAGES

    def page_spec(number):
        def pick(slot, step, lengths, tables):
            last = (lengths[slot] + page_len - 1) // page_len - 1
            return (tables[slot * row_pages + jnp.minimum(step * BLOCK_PAGES + number, last)], 0, 0)

        return pl.BlockSpec((1, page_len, features), pick)

    def slot_rows(slot, step, lengths, tables):
        return (slot, 0)

    pages = [page_spec(number) for number in range(BLOCK_PAGES)]
    state = pltpu.VMEM((kv_heads, rows, HEAD_SIZE), jnp.float32)
    return pl.pallas_call(
        attend_kernel,
        out_shape=jax.ShapeDtypeStruct(queries.shape, jnp.bfloat16),
        grid_spec=pltpu.PrefetchScalarGridSpec(
            num_scalar_prefetch=2,
            grid=(slots, steps),
            in_specs=[
                pl.BlockSpec((tokens, queries.shape[1]), slot_rows),
                pl.BlockSpec((tokens, features), slot_rows),
                pl.BlockSpec((tokens, features), slot_rows),
            ]
            + pages
            + pages,
            out_specs=pl.BlockSpec((tokens, queries.shape[1]), slot_rows),
            scratch_shapes=[
                pltpu.VMEM((kv_heads, rows, HEAD_SIZE), jnp.bfloat16),
                state,
                state,
                state,
            ],
        ),
        compiler_params=pltpu.CompilerParams(
            dimension_semantics=("arbitrary", "arbitrary"), vmem_limit_bytes=40 << 20
        ),
        name="attend",
    )(
        lengths,
        tables.reshape(-1),
        queries,
        new_keys,
        new_values,
        *([k_pool] * BLOCK_PAGES),
        *([v_pool] * BLOCK_PAGES),
    )


LINKS = 3
LANE = 8
WIDE = 8
OWN_ROUNDS = 3
LATE_ROUND = 4
FIXED_ROUNDS = 12
SIDES = 3
ROUND_LIMIT = 56
SLOT_LIMIT = ROUND_LIMIT * LANE
TABLE = 2 * SLOT_LIMIT + ROUND_LIMIT * WIDE
WIDTHS = (LANE, LANE, WIDE)
OFFSETS = (0, LANE, 2 * LANE)
QUEUE = 96
ARRIVALS = 512
HELD = 1024
HELD_PAGES = 384


def neighbours():
    right = [(device, device + 2) for device in range(6)]
    left = [(device + 2, device) for device in range(6)]
    across = [(device, device ^ 1) for device in range(8)]
    return right, left, across


def loop(low, high, body):
    def step(index, carry):
        body(index)
        return carry

    lax.fori_loop(low, high, step, 0)


def plan_kernel(layout, first, table, perm, me, counts, send, *rest):
    if first:
        own_codes, early_first, runs, places, heads, tails, waiting, progress = rest
    else:
        receive, rounds = rest[:2]
        own_codes, early_first, runs, places, heads, tails, waiting, progress = rest[2:10]
        numbers, held, arrived_device, arrived_run, arrived_place, arrived_count = rest[10:]
    peers, block = layout.peers, layout.block
    own = me[0]
    page_len = layout.page_len

    def total(pair):
        return counts[pair]

    def early(pair):
        return counts[peers * peers + pair]

    def scan(source, target, use):
        whole = [
            lax.div(layout.length(table, perm, source, slot), page_len)
            for slot in range(layout.slots)
        ]
        base = source * layout.width + layout.sends + target * block
        plain, tail_rank = jnp.int32(0), early(source * peers + target)
        for number in range(block):
            code = table[base + number]
            edge = whole[0]
            for slot in range(1, layout.slots):
                low = slot * layout.code_width
                edge = jnp.where(code >= low, whole[slot] + low, edge)
            valid, tail = code >= 0, code >= edge
            use(number, code, valid, jnp.where(tail, tail_rank, plain))
            plain = plain + jnp.where(valid & jnp.logical_not(tail), 1, 0)
            tail_rank = tail_rank + jnp.where(tail, 1, 0)

    def list_own(target):
        def use(number, code, valid, rank):
            @pl.when(valid)
            def _():
                own_codes[target * block + rank] = code

        scan(own, target, use)

    loop(0, peers, list_own)
    if not first:

        def list_numbers(source):
            def use(number, code, valid, rank):
                @pl.when(valid)
                def _():
                    numbers[source * block + rank] = source * block + number

            scan(source, own, use)

        loop(0, peers, list_numbers)

    def clear(index):
        early_first[index] = 0

    loop(0, peers * peers, clear)
    half = peers // 2
    for direction in range(2):
        sources = range(direction * half, (direction + 1) * half)
        targets = range((1 - direction) * half, (2 - direction) * half)
        loads = []
        for column in range(2):
            load = jnp.int32(0)
            for source in sources:
                if source % 2 == column:
                    for target in targets:
                        load = load + total(source * peers + target)
            loads.append(load)
        heavy = jnp.where(loads[1] > loads[0], 1, 0)
        left = lax.div(jnp.abs(loads[0] - loads[1]), 2)
        zs = sorted({source // 2 for source in sources})
        zt = sorted({target // 2 for target in targets})
        for _, a, b in sorted((abs(a - b), a, b) for a in zs for b in zt):
            pair = (2 * a + heavy) * peers + 2 * b + 1 - heavy
            moved = jnp.minimum(left, early(pair))
            early_first[pair] = moved
            left = left - moved

    def clear_queue(index):
        heads[index] = 0
        tails[index] = 0

    loop(0, peers * LINKS * 4, clear_queue)

    def clear_waiting(index):
        waiting[index] = 0

    loop(0, peers * LINKS, clear_waiting)
    progress[0] = 0

    def push(device, run, place, turn):
        target = (run >> 10) & 7
        steps = (target >> 1) - (device >> 1)
        flip = (target ^ device) & 1
        across = (steps == 0) | turn
        link = jnp.where(across, 2, jnp.where(steps > 0, 0, 1))
        lane = device * LINKS + link
        waiting[lane] = waiting[lane] + 1
        queue = lane * 4 + jnp.abs(steps) + flip - 1
        spot = tails[queue]
        runs[queue * QUEUE + spot] = run
        places[queue * QUEUE + spot] = place
        tails[queue] = spot + 1

    def make_run(pair, start, count):
        return (pair << 10) | (start << 5) | count

    def open_pair(pair):
        source = pair >> 3
        moved = early_first[pair]
        count = early(pair)
        wanted = source != (pair & 7)
        if first:
            wanted = wanted & (source == own)

        @pl.when(wanted & (moved > 0))
        def _():
            push(source, make_run(pair, 0, moved), -1, True)

        @pl.when(wanted & (count > moved))
        def _():
            push(source, make_run(pair, moved, count - moved), -1, False)

    loop(0, peers * peers, open_pair)

    def open_late(pair):
        source = pair >> 3
        count = total(pair) - early(pair)

        @pl.when((source != (pair & 7)) & (count > 0))
        def _():
            push(source, make_run(pair, early(pair), count), -1, False)

    def move(step, device, link, width, toward):
        lane = device * LINKS + link

        @pl.when(waiting[lane] > 0)
        def _():
            drain(step, lane, device, link, width, toward)

    def drain(step, lane, device, link, width, toward):
        room = jnp.int32(width)
        origin = link * SLOT_LIMIT + step * width + width
        side = lax.rem(step, SIDES)
        for rank in (3, 2, 1, 0):
            queue = lane * 4 + rank

            def more(state):
                room, head, tail = state
                return (room > 0) & (head < tail)

            def take(state):
                room, head, tail = state
                spot = queue * QUEUE + head
                run, place = runs[spot], places[spot]
                pair, start, count = run >> 10, (run >> 5) & 31, run & 31
                taken = jnp.minimum(room, count)
                base = origin - room
                final = (pair & 7) == toward

                def note_sent():
                    def note(index):
                        code = own_codes[(pair & 7) * block + start + index]
                        send[base + index] = jnp.where(place < 0, code, HELD + place + index)

                    loop(0, taken, note)

                whole = taken == count
                waiting[lane] = waiting[lane] - jnp.where(whole, 1, 0)
                runs[spot] = make_run(pair, start + taken, count - taken)
                places[spot] = jnp.where(place < 0, place, place + taken)
                if first:
                    note_sent()
                else:
                    slot = held[toward]
                    passing = jnp.where(final, 0, taken)
                    progress[0] = progress[0] + taken - passing
                    held[toward] = slot + passing
                    added = arrived_count[side]
                    at = side * ARRIVALS + added
                    arrived_device[at] = toward
                    arrived_run[at] = make_run(pair, start, taken)
                    arrived_place[at] = slot
                    arrived_count[side] = added + jnp.where(final, 0, 1)

                    @pl.when((device == own) | (toward == own))
                    def _():
                        @pl.when(device == own)
                        def _():
                            note_sent()

                        @pl.when(toward == own)
                        def _():
                            def note(index):
                                number = numbers[(pair >> 3) * block + start + index]
                                receive[base + index] = jnp.where(
                                    final, number, HELD + slot + index
                                )

                            loop(0, taken, note)

                return room - taken, head + jnp.where(whole, 1, 0), tail

            room, head, _ = lax.while_loop(more, take, (room, heads[queue], tails[queue]))
            heads[queue] = head

    def blank(step):
        def one(index):
            for link in (0, 1):
                spot = link * SLOT_LIMIT + step * LANE + index
                send[spot] = -1
                if not first:
                    receive[spot] = -1

        def wide(index):
            spot = 2 * SLOT_LIMIT + step * WIDE + index
            send[spot] = -1
            if not first:
                receive[spot] = -1

        loop(0, LANE, one)
        loop(0, WIDE, wide)

    if first:
        for step in range(OWN_ROUNDS):
            blank(step)
            move(step, own, 0, LANE, own + 2)
            move(step, own, 1, LANE, own - 2)
            move(step, own, 2, WIDE, own ^ 1)
        return

    wanted = jnp.int32(0)
    for source in range(peers):
        held[source] = 0
        for target in range(peers):
            if source != target:
                wanted = wanted + total(source * peers + target)
    for side in range(SIDES):
        arrived_count[side] = 0

    def unfinished(step):
        return (step <= FIXED_ROUNDS) | (progress[0] < wanted)

    def advance(step):
        blank(step)

        @pl.when(step == LATE_ROUND)
        def _():
            loop(0, peers * peers, open_late)

        def arrive_all(side):
            def arrive(index):
                at = side * ARRIVALS + index
                push(arrived_device[at], arrived_run[at], arrived_place[at], False)

            loop(0, arrived_count[side], arrive)
            arrived_count[side] = 0

        @pl.when(step == OWN_ROUNDS)
        def _():
            for past in range(OWN_ROUNDS - 2):
                arrive_all(past)

        @pl.when(step >= OWN_ROUNDS)
        def _():
            arrive_all(lax.rem(step + 1, SIDES))

        def one(device):
            move(step, device, 0, LANE, device + 2)
            move(step, device, 1, LANE, device - 2)
            move(step, device, 2, WIDE, device ^ 1)

        loop(0, peers, one)

        @pl.when(progress[0] >= wanted)
        def _():
            rounds[0] = jnp.minimum(rounds[0], step + 1)

        return step + 1

    rounds[0] = jnp.int32(ROUND_LIMIT)
    rounds[1] = jnp.int32(0)
    end = lax.while_loop(unfinished, advance, jnp.int32(0))
    blank(end)


def plan(layout, first, table, perm, me, counts):
    tables = jax.ShapeDtypeStruct((TABLE,), jnp.int32)
    outs = (tables,) if first else (tables, tables, jax.ShapeDtypeStruct((2,), jnp.int32))
    peers = layout.peers

    def words(count):
        return pltpu.SMEM((count,), jnp.int32)

    queues = peers * LINKS * 4
    room = [
        words(peers * layout.block),
        words(peers * peers),
        words(queues * QUEUE),
        words(queues * QUEUE),
        words(queues),
        words(queues),
        words(peers * LINKS),
        words(1),
    ]
    if not first:
        room += [words(peers * layout.block), words(peers)]
        room += [words(SIDES * ARRIVALS)] * 3 + [words(SIDES)]
    out = pl.pallas_call(
        lambda *refs: plan_kernel(layout, first, *refs),
        out_shape=outs,
        grid_spec=pltpu.PrefetchScalarGridSpec(
            num_scalar_prefetch=4,
            grid=(1,),
            in_specs=[],
            out_specs=tuple(pl.BlockSpec(memory_space=pltpu.SMEM) for _ in outs),
            scratch_shapes=room,
        ),
        name="plan_first" if first else "plan_rest",
    )(table, perm, me, counts)
    return out[0] if first else out


def own_page(layout, table, perm, me, pool, recent, zeros, code, target, sem):
    slot, page = layout.split(code)
    cached = pool.at[layout.physical(table, perm, me[0], slot, page)]
    if recent is None:
        pltpu.make_async_copy(cached, target, sem).start()
        return
    page_len = layout.page_len
    length = layout.length(table, perm, me[0], slot)
    full, kept = lax.div(length, page_len), lax.rem(length, page_len)

    @pl.when(page < full)
    def _():
        pltpu.make_async_copy(cached, target, sem).start()

    @pl.when(page == full)
    def _():
        copy_rows(cached, 0, target, 0, kept, sem)
        copy_rows(recent.at[slot], 0, target, kept, page_len - kept, sem)

    @pl.when(page > full)
    def _():
        copy_rows(recent.at[slot], page_len - kept, target, 0, kept, sem)
        copy_rows(zeros, 0, target, kept, page_len - kept, sem)


def links_of(step):
    return (0, 1, 2)


def step_kernel(layout, kind, parity, table, perm, me, step, send, *rest):
    recent = zeros = None
    count = len(links_of(parity))
    if kind == "first":
        pool, *lanes, sent, load_sems, store_sems = rest
        groups = []
    elif kind == "begin":
        receive, pool = rest[:2]
        arrived = rest[2:8]
        out, held, *lanes = rest[8 : 10 + count]
        sent, load_sems, store_sems, came, land_sems, leave_sems = rest[10 + count :]
        groups = [3, 2]
    elif kind == "step":
        receive, pool, recent, zeros = rest[:4]
        arrived = rest[4 : 4 + count]
        rest = rest[6 + count :]
        out, held, *lanes = rest[: 2 + count]
        sent, load_sems, store_sems, came, land_sems, leave_sems = rest[2 + count :]
        groups = [2]
    else:
        receive = send
        arrived = rest[:6]
        out, came, land_sems, leave_sems = rest[7:]
        groups = [2, 1]
    relaying = kind in ("begin", "step")
    first_ref = [0]
    for back in groups:
        first_ref.append(first_ref[-1] + len(links_of(parity - back)))

    def spots(body):
        for link in links_of(parity):
            loop(0, WIDTHS[link], lambda index, link=link: body(link, index))

    def every(body):
        for group, back in enumerate(groups):
            for link in links_of(parity - back):
                base = link * SLOT_LIMIT + (step[0] - back) * WIDTHS[link]

                def row(index, group=group, link=link, base=base):
                    body(group, link, index, receive[base + index])

                loop(0, WIDTHS[link], row)

    def outgoing(link, index):
        return send[link * SLOT_LIMIT + step[0] * WIDTHS[link] + index]

    def load(link, index, source):
        spot = OFFSETS[link] + index
        return pltpu.make_async_copy(source, sent.at[spot], load_sems.at[spot])

    def store(link, index):
        spot = OFFSETS[link] + index
        return pltpu.make_async_copy(
            sent.at[spot], lanes[link].at[index], store_sems.at[spot]
        )

    if groups:

        def landing(group, link, index):
            return pltpu.make_async_copy(
                arrived[first_ref[group] + link].at[index],
                came.at[group, OFFSETS[link] + index],
                land_sems.at[group, OFFSETS[link] + index],
            )

        def leaving(group, link, index, target):
            spot = OFFSETS[link] + index
            return pltpu.make_async_copy(
                came.at[group, spot], target, leave_sems.at[group, spot]
            )

        def land(group, link, index, to):
            @pl.when(to >= 0)
            def _():
                landing(group, link, index).start()

        every(land)

    if kind != "last":

        def fetch(link, index):
            code = outgoing(link, index)

            @pl.when((code >= 0) & (code < HELD))
            def _():
                own_page(
                    layout, table, perm, me, pool, recent, zeros, code,
                    sent.at[OFFSETS[link] + index], load_sems.at[OFFSETS[link] + index],
                )

        spots(fetch)

    if groups:

        def leave(group, link, index, to):
            @pl.when(to >= 0)
            def _():
                landing(group, link, index).wait()

            @pl.when((to >= 0) & (to < HELD))
            def _():
                leaving(group, link, index, out.at[to]).start()

            if relaying:

                @pl.when(to >= HELD)
                def _():
                    leaving(group, link, index, held.at[to - HELD]).start()

        every(leave)

    if kind != "last":

        def pass_on(link, index):
            code = outgoing(link, index)

            @pl.when((code >= 0) & (code < HELD))
            def _():
                load(link, index, pool.at[0]).wait()
                store(link, index).start()

        spots(pass_on)

    if groups:

        def left(group, link, index, to):
            @pl.when(to >= 0)
            def _():
                leaving(group, link, index, out.at[0]).wait()

        every(left)

    if relaying:

        def reload(link, index):
            code = outgoing(link, index)

            @pl.when(code >= HELD)
            def _():
                load(link, index, held.at[code - HELD]).start()

        def relayed(link, index):
            code = outgoing(link, index)

            @pl.when(code >= HELD)
            def _():
                load(link, index, pool.at[0]).wait()
                store(link, index).start()

        spots(reload)
        spots(relayed)

    if kind != "last":

        def stored(link, index):
            @pl.when(outgoing(link, index) >= 0)
            def _():
                store(link, index).wait()

        spots(stored)


def any_specs(count):
    return [pl.BlockSpec(memory_space=pltpu.HBM)] * count


def lane_shapes(pool, parity):
    return tuple(
        jax.ShapeDtypeStruct((WIDTHS[link],) + pool.shape[1:], pool.dtype)
        for link in links_of(parity)
    )


SPOTS = 2 * LANE + WIDE


def send_room(pool):
    return [
        pltpu.VMEM((SPOTS,) + pool.shape[1:], pool.dtype),
        pltpu.SemaphoreType.DMA((SPOTS,)),
        pltpu.SemaphoreType.DMA((SPOTS,)),
    ]


def land_room(pool, groups):
    return [
        pltpu.VMEM((groups, SPOTS) + pool.shape[1:], pool.dtype),
        pltpu.SemaphoreType.DMA((groups, SPOTS)),
        pltpu.SemaphoreType.DMA((groups, SPOTS)),
    ]


ROOMY = pltpu.CompilerParams(vmem_limit_bytes=40 << 20)


def pack_first(layout, table, perm, me, step, send, pool):
    parity = step % 2
    return pl.pallas_call(
        lambda *refs: step_kernel(layout, "first", parity, *refs),
        out_shape=lane_shapes(pool, parity),
        grid_spec=pltpu.PrefetchScalarGridSpec(
            num_scalar_prefetch=5,
            grid=(1,),
            in_specs=any_specs(1),
            out_specs=tuple(any_specs(len(links_of(parity)))),
            scratch_shapes=send_room(pool),
        ),
        compiler_params=ROOMY,
        name="pack_first",
    )(table, perm, me, number(step), send, pool)


def relay_begin(layout, table, perm, me, step, send, receive, pool, arrived):
    parity = step % 2
    page = pool.shape[1:]
    results = pl.pallas_call(
        lambda *refs: step_kernel(layout, "begin", parity, *refs),
        out_shape=(
            jax.ShapeDtypeStruct((layout.peers * layout.block,) + page, pool.dtype),
            jax.ShapeDtypeStruct((HELD_PAGES,) + page, pool.dtype),
        )
        + lane_shapes(pool, parity),
        grid_spec=pltpu.PrefetchScalarGridSpec(
            num_scalar_prefetch=6,
            grid=(1,),
            in_specs=any_specs(7),
            out_specs=tuple(any_specs(2 + len(links_of(parity)))),
            scratch_shapes=send_room(pool) + land_room(pool, 2),
        ),
        compiler_params=ROOMY,
        name="relay_begin",
    )(table, perm, me, number(step), send, receive, pool, *arrived)
    return results[2:], results[0], results[1]


def relay(
    layout, parity, table, perm, me, step, send, receive, pool, recent, zeros, arrived, out, held
):
    count = len(arrived)
    results = pl.pallas_call(
        lambda *refs: step_kernel(layout, "step", parity, *refs),
        out_shape=(
            jax.ShapeDtypeStruct(out.shape, out.dtype),
            jax.ShapeDtypeStruct(held.shape, held.dtype),
        )
        + lane_shapes(pool, parity),
        grid_spec=pltpu.PrefetchScalarGridSpec(
            num_scalar_prefetch=6,
            grid=(1,),
            in_specs=any_specs(5 + count),
            out_specs=tuple(any_specs(2 + count)),
            scratch_shapes=send_room(pool) + land_room(pool, 1),
        ),
        input_output_aliases={9 + count: 0, 10 + count: 1},
        compiler_params=ROOMY,
        name="relay",
    )(table, perm, me, step, send, receive, pool, recent, zeros, *arrived, out, held)
    return results[2:], results[0], results[1]


def land_last(layout, table, perm, me, step, receive, arrived, out):
    return pl.pallas_call(
        lambda *refs: step_kernel(layout, "last", 0, *refs),
        out_shape=jax.ShapeDtypeStruct(out.shape, out.dtype),
        grid_spec=pltpu.PrefetchScalarGridSpec(
            num_scalar_prefetch=5,
            grid=(1,),
            in_specs=any_specs(7),
            out_specs=pl.BlockSpec(memory_space=pl.ANY),
            scratch_shapes=land_room(out, 2),
        ),
        input_output_aliases={11: 0},
        compiler_params=ROOMY,
        name="land_last",
    )(table, perm, me, step, receive, *arrived, out)


def fill_kernel(
    layout, table, perm, me, pool, recent, zeros, before, out, blank, mine, sems, load_sems
):
    del before
    own, block = me[0], layout.block
    fill = pltpu.make_async_copy(zeros, blank, load_sems.at[block])
    fill.start()

    def code_of(source, number):
        return table[source * layout.width + layout.sends + own * block + number]

    def outward(source, number, held_page):
        return pltpu.make_async_copy(
            held_page, out.at[source * block + number], sems.at[source & 1, number]
        )

    def inward(number):
        code = code_of(own, number)

        @pl.when(code >= 0)
        def _():
            own_page(
                layout, table, perm, me, pool, recent, zeros, code, mine.at[number],
                load_sems.at[number],
            )

    loop(0, block, inward)
    fill.wait()

    def is_ours(source, number):
        return (code_of(source, number) < 0) | (source == own)

    def finish(source):
        def one(number):
            @pl.when(is_ours(source, number))
            def _():
                outward(source, number, blank).wait()

        loop(0, block, one)

    def begin(source):
        @pl.when(source >= 2)
        def _():
            finish(source - 2)

        def one(number):
            code = code_of(source, number)

            @pl.when(code < 0)
            def _():
                outward(source, number, blank).start()

            @pl.when((code >= 0) & (source == own))
            def _():
                pltpu.make_async_copy(pool.at[0], mine.at[number], load_sems.at[number]).wait()
                outward(source, number, mine.at[number]).start()

        loop(0, block, one)

    loop(0, layout.peers, begin)
    loop(layout.peers - 2, layout.peers, finish)


def fill_local(layout, table, perm, me, pool, recent, zeros, out):
    page = pool.shape[1:]
    return pl.pallas_call(
        lambda *refs: fill_kernel(layout, *refs),
        out_shape=jax.ShapeDtypeStruct(out.shape, out.dtype),
        grid_spec=pltpu.PrefetchScalarGridSpec(
            num_scalar_prefetch=3,
            grid=(1,),
            in_specs=any_specs(4),
            out_specs=pl.BlockSpec(memory_space=pl.ANY),
            scratch_shapes=[
                pltpu.VMEM(page, pool.dtype),
                pltpu.VMEM((layout.block,) + page, pool.dtype),
                pltpu.SemaphoreType.DMA((2, layout.block)),
                pltpu.SemaphoreType.DMA((layout.block + 1,)),
            ],
        ),
        input_output_aliases={6: 0},
        compiler_params=ROOMY,
        name="fill_local",
    )(table, perm, me, pool, recent, zeros, out)


PARTS = 4


def part_kernel(slot, part, lengths, tables, q_ref, *rest):
    first, last = part == 0, part == PARTS - 1
    if first:
        (nk_ref, nv_ref), rest = rest[:2], rest[2:]
    else:
        before, rest = rest[:3], rest[3:]
    pages, rest = rest[:BLOCK_PAGES], rest[BLOCK_PAGES:]
    if last:
        out_ref, q_rows, top, total, acc = rest
    else:
        top, total, acc, q_rows = rest
    kv_heads, rows, head = q_rows.shape
    tokens = q_ref.shape[0]
    groups = rows // tokens
    step = pl.program_id(0)
    page_len = pages[0].shape[1]
    block_keys = BLOCK_PAGES * page_len
    begin = (part * pl.num_programs(0) + step) * block_keys
    length = lengths[slot]
    inv_scale = 1.0 / math.sqrt(head)

    def score(kv, keys):
        return (
            lax.dot_general(
                q_rows[kv], keys, (((1,), (1,)), ((), ())), preferred_element_type=jnp.float32
            )
            * inv_scale
        )

    @pl.when(step == 0)
    def _():
        for kv in range(kv_heads):
            for group in range(groups):
                lane = (kv * groups + group) * head
                q_rows[kv, group * tokens : (group + 1) * tokens, :] = q_ref[:, lane : lane + head]
            if not first:
                continue
            columns = slice(kv * head, (kv + 1) * head)
            scores = score(kv, nk_ref[:, columns])
            query_id = lax.broadcasted_iota(jnp.int32, scores.shape, 0) % tokens
            key_id = lax.broadcasted_iota(jnp.int32, scores.shape, 1)
            scores = jnp.where(key_id <= query_id, scores, -1e30)
            highest = jnp.max(scores, axis=-1, keepdims=True)
            weights = jnp.exp(scores - highest)
            top[kv] = jnp.broadcast_to(highest, (rows, head))
            total[kv] = jnp.broadcast_to(jnp.sum(weights, axis=-1, keepdims=True), (rows, head))
            acc[kv] = jnp.dot(
                weights.astype(jnp.bfloat16), nv_ref[:, columns], preferred_element_type=jnp.float32
            )
        if not first:
            top[...] = before[0][...]
            total[...] = before[1][...]
            acc[...] = before[2][...]

    def absorb(masked):
        flat = [ref[0].reshape(page_len, 2 * kv_heads * head) for ref in pages]
        for kv in range(kv_heads):
            keys = jnp.concatenate([x[:, kv * head : (kv + 1) * head] for x in flat], axis=0)
            low = (kv_heads + kv) * head
            values = jnp.concatenate([x[:, low : low + head] for x in flat], axis=0)
            scores = score(kv, keys)
            if masked:
                key_id = lax.broadcasted_iota(jnp.int32, scores.shape, 1)
                scores = jnp.where(key_id < length - begin, scores, -1e30)
            past = top[kv]
            highest = jnp.maximum(past, jnp.max(scores, axis=-1, keepdims=True))
            factor = jnp.exp(past - highest)
            weights = jnp.exp(scores - highest[:, :1])
            top[kv] = highest
            total[kv] = total[kv] * factor + jnp.sum(weights, axis=-1, keepdims=True)
            acc[kv] = acc[kv] * factor + jnp.dot(
                weights.astype(jnp.bfloat16), values, preferred_element_type=jnp.float32
            )

    @pl.when(begin + block_keys <= length)
    def _():
        absorb(False)

    @pl.when((begin < length) & (begin + block_keys > length))
    def _():
        absorb(True)

    if last:

        @pl.when(step == pl.num_programs(0) - 1)
        def _():
            for kv in range(kv_heads):
                context = (acc[kv] / total[kv]).astype(jnp.bfloat16)
                for group in range(groups):
                    lane = (kv * groups + group) * head
                    out_ref[:, lane : lane + head] = context[
                        group * tokens : (group + 1) * tokens
                    ]


def relay_part_kernel(layout, slot, part, *refs):
    table, perm, me, number, send, receive, lengths, tables = refs[:8]
    ins, rest = refs[8:16], refs[16:]
    count = 3 if part else 2
    inner, rest = rest[: 1 + count + BLOCK_PAGES], rest[1 + count + BLOCK_PAGES :]
    outs, rest = rest[: 2 + LINKS], rest[2 + LINKS :]
    made = 1 if part == PARTS - 1 else 3
    results, rest = rest[:made], rest[made:]
    rooms, rest = rest[:6], rest[6:]
    part_kernel(slot, part, lengths, tables, *inner, *results, *rest)

    @pl.when(pl.program_id(0) == pl.num_programs(0) - 1)
    def _():
        step_kernel(
            layout, "step", 0, table, perm, me, number, send, receive, *ins, *outs, *rooms
        )


def relay_part(
    layout, slot, part, table, perm, me, step, send, receive, lengths, tables, pool, recent, zeros,
    arrived, out, held, queries, fresh, state,
):
    slots, row_pages = tables.shape
    tokens = queries.shape[0] // slots
    page_len, features = pool.shape[1], pool.shape[3]
    kv_heads = features // HEAD_SIZE
    rows = tokens * (queries.shape[1] // features)
    steps = row_pages // BLOCK_PAGES // PARTS
    first, last = part == 0, part == PARTS - 1

    def page_spec(index):
        def pick(step, *words):
            lengths, tables = words[6:]
            final = (lengths[slot] + page_len - 1) // page_len - 1
            page = (part * steps + step) * BLOCK_PAGES + index
            return (tables[slot * row_pages + jnp.minimum(page, final)], 0, 0, 0)

        return pl.BlockSpec((1, page_len, 2, features), pick)

    def slot_rows(step, *words):
        return (slot, 0)

    shape = (kv_heads, rows, HEAD_SIZE)
    state_spec = pl.BlockSpec(shape, lambda step, *words: (0, 0, 0))
    operands = list(fresh) if first else list(state)
    specs = [pl.BlockSpec((tokens, features), slot_rows)] * 2 if first else [state_spec] * 3
    room = [pltpu.VMEM(shape, jnp.bfloat16)]
    if last:
        made = (jax.ShapeDtypeStruct((tokens, queries.shape[1]), queries.dtype),)
        made_specs = (pl.BlockSpec(made[0].shape, lambda step, *words: (0, 0)),)
        room += [pltpu.VMEM(shape, jnp.float32)] * 3
    else:
        made = (jax.ShapeDtypeStruct(shape, jnp.float32),) * 3
        made_specs = (state_spec,) * 3
    results = pl.pallas_call(
        lambda *refs: relay_part_kernel(layout, slot, part, *refs),
        out_shape=(
            jax.ShapeDtypeStruct(out.shape, out.dtype),
            jax.ShapeDtypeStruct(held.shape, held.dtype),
        )
        + lane_shapes(pool, 0)
        + made,
        grid_spec=pltpu.PrefetchScalarGridSpec(
            num_scalar_prefetch=8,
            grid=(steps,),
            in_specs=any_specs(8)
            + [pl.BlockSpec((tokens, queries.shape[1]), slot_rows)]
            + specs
            + [page_spec(page) for page in range(BLOCK_PAGES)],
            out_specs=tuple(any_specs(2 + LINKS)) + made_specs,
            scratch_shapes=send_room(pool) + land_room(pool, 1) + room,
        ),
        input_output_aliases={14: 0, 15: 1},
        compiler_params=pltpu.CompilerParams(
            dimension_semantics=("arbitrary",), vmem_limit_bytes=48 << 20
        ),
        name="relay_part",
    )(
        table, perm, me, number(step), send, receive, lengths, tables.reshape(-1), pool, recent,
        zeros, *arrived, out, held, queries, *operands, *([pool] * BLOCK_PAGES),
    )
    return results[2:5], results[0], results[1], results[5:]


PAIR_DEPTH = 640


def pair_kernel(x_ref, w_ref, out_ref):
    @pl.when(pl.program_id(0) == 0)
    def _():
        out_ref[...] = jnp.zeros_like(out_ref)

    depth = w_ref.shape[0]
    out_ref[...] += jnp.dot(
        x_ref[...], w_ref[...].reshape(depth, -1), preferred_element_type=jnp.float32
    )


def project_pair(rows, wkv):
    count, width = rows.shape
    features = wkv.shape[1] * wkv.shape[2]
    return pl.pallas_call(
        pair_kernel,
        out_shape=jax.ShapeDtypeStruct((count, features), jnp.float32),
        grid=(width // PAIR_DEPTH,),
        in_specs=[
            pl.BlockSpec((count, PAIR_DEPTH), lambda step: (0, step)),
            pl.BlockSpec((PAIR_DEPTH,) + wkv.shape[1:], lambda step: (step, 0, 0)),
        ],
        out_specs=pl.BlockSpec((count, features), lambda step: (0, 0)),
        compiler_params=ROOMY,
        name="project_pair",
    )(rows, wkv)


def after(value, *others):
    return lax.optimization_barrier((value,) + others)[0]


def page_counts(layout, by_device, perm):
    lengths = by_device[:, : layout.slots].reshape(-1)[perm].reshape(layout.peers, layout.slots)
    whole = lax.div(lengths, layout.page_len)
    codes = by_device[:, layout.sends : layout.used].reshape(
        layout.peers, layout.peers, layout.block
    )
    edge = whole[:, 0, None, None]
    for slot in range(1, layout.slots):
        low = slot * layout.code_width
        edge = jnp.where(codes >= low, whole[:, slot, None, None] + low, edge)
    valid = codes >= 0
    plain = valid & (codes < edge)
    return jnp.concatenate(
        [
            jnp.sum(valid.astype(jnp.int32), axis=-1).reshape(-1),
            jnp.sum(plain.astype(jnp.int32), axis=-1).reshape(-1),
        ]
    )


def hop(lanes):
    return tuple(
        lax.ppermute(lane, "req", pairs) for lane, pairs in zip(lanes, neighbours())
    )


def number(value):
    return jnp.asarray(value, jnp.int32).reshape(1)


def grid_shards(hidden, norm_gain, wq, wkv, wo, perm, prior_len, page_table, pool, send_table):
    slots = prior_len.shape[0]
    tokens = hidden.shape[0] // slots
    _, peers, block = send_table.shape
    layout = Layout(slots, page_table.shape[1], peers, block)
    layout.page_len = pool.shape[1]
    features = pool.shape[-1]
    device = lax.axis_index("req")
    me = device.astype(jnp.int32).reshape(1)
    mine = jnp.concatenate([prior_len, page_table.reshape(-1), send_table.reshape(-1)])
    mine = jnp.pad(mine, (0, layout.width - layout.used)).reshape(-1, 128)
    by_device = exchange(peers, mine)
    table = by_device.reshape(-1)
    by_device = by_device.reshape(peers, layout.width)
    counts = page_counts(layout, by_device, perm)
    first = plan(layout, True, table, perm, me, counts)
    lanes = [pack_first(layout, table, perm, me, step, first, pool) for step in range(2)]
    arrived = [hop(lane) for lane in lanes]
    full_rows = lax.all_gather(hidden, "tp", axis=1, tiled=True)
    requests = lax.dynamic_slice_in_dim(perm, device * slots, slots)
    lengths = by_device[:, :slots].reshape(-1)[requests]
    tables = by_device[:, slots : layout.sends].reshape(-1, layout.row_pages)[requests]
    positions = (lengths[:, None] + jnp.arange(tokens, dtype=jnp.int32)[None, :]).reshape(-1)

    full_rows = after(full_rows, lanes[1][0])
    normalized_input = normalize(full_rows, norm_gain)
    pair_proj = project_pair(normalized_input, wkv)
    pair_heads = pair_proj.reshape(pair_proj.shape[0], 2, -1, HEAD_SIZE)
    new_keys = rotate(pair_heads[:, 0], positions).astype(jnp.bfloat16).reshape(-1, features)
    new_values = pair_heads[:, 1].astype(jnp.bfloat16).reshape(-1, features)
    recent = jnp.stack([new_keys, new_values], axis=1).reshape(slots, tokens, 2, features)
    zeros = jnp.zeros(pool.shape[1:], pool.dtype)

    query_proj = jnp.dot(normalized_input, wq, preferred_element_type=jnp.float32)
    queries = rotate(
        query_proj.reshape(query_proj.shape[0], -1, HEAD_SIZE), positions
    ).astype(jnp.bfloat16)
    queries = queries.reshape(queries.shape[0], -1)
    first = after(first, queries, recent)
    lanes.append(pack_first(layout, table, perm, me, 2, first, pool))
    arrived.append(hop(lanes[2]))

    counts = after(counts, lanes[-1][0], *arrived[0])
    send, receive, rounds = plan(layout, False, table, perm, me, counts)
    lane, out, held = relay_begin(
        layout, table, perm, me, OWN_ROUNDS, send, receive, pool, arrived[0] + arrived[1]
    )
    arrived.append(hop(lane))

    def advance(step, parity, landed, out, held):
        return relay(
            layout, parity, table, perm, me, number(step), send, receive, pool, recent, zeros,
            landed, out, held,
        )

    state = None
    contexts = []
    for step in range(OWN_ROUNDS + 1, FIXED_ROUNDS):
        slot, part = divmod(step - OWN_ROUNDS - 1, PARTS)
        lane, out, held, state = relay_part(
            layout, slot, part, table, perm, me, step, send, receive, lengths, tables, pool,
            recent, zeros, arrived[step - 2], out, held, queries, (new_keys, new_values), state,
        )
        arrived.append(hop(lane))
        if part == PARTS - 1:
            contexts.append(state[0])
    out = fill_local(layout, table, perm, me, pool, recent, zeros, out)
    context = after(jnp.concatenate(contexts, axis=0), *arrived[-2])
    partial_value = jnp.dot(context, wo, preferred_element_type=jnp.float32)
    attn_out = lax.psum_scatter(
        partial_value.astype(jnp.bfloat16), "tp", scatter_dimension=1, tiled=True
    )

    newest = arrived[-1]
    newest = (after(newest[0], partial_value),) + newest[1:]

    def turn(state):
        step, older, newer, out, held = state
        lane, out, held = advance(step, 0, older, out, held)
        older = hop(lane)
        lane, out, held = advance(step + 1, 1, newer, out, held)
        return step + 2, older, hop(lane), out, held

    step, older, newer, out, _ = lax.while_loop(
        lambda state: state[0] < rounds[0],
        turn,
        (jnp.int32(FIXED_ROUNDS), arrived[-2], newest, out, held),
    )
    decode_pages = land_last(
        layout, table, perm, me, number(step), receive, older + newer, out
    )
    return (attn_out, decode_pages.reshape((1, peers, block) + pool.shape[1:]))


def shards(hidden, norm_gain, wq, wkv, wo, perm, prior_len, page_table, pool, send_table):
    slots = prior_len.shape[0]
    tokens = hidden.shape[0] // slots
    _, peers, block = send_table.shape
    layout = Layout(slots, page_table.shape[1], peers, block)
    features = pool.shape[-1]
    device = lax.axis_index("req")
    me = device.astype(jnp.int32).reshape(1)
    mine = jnp.concatenate([prior_len, page_table.reshape(-1), send_table.reshape(-1)])
    mine = jnp.pad(mine, (0, layout.width - layout.used)).reshape(-1, 128)
    by_device = exchange(peers, mine)
    table = by_device.reshape(-1)
    by_device = by_device.reshape(peers, layout.width)
    outgoing = pack_pages(layout, table, perm, me, pool)
    arrived = lax.all_to_all(outgoing, "req", split_axis=0, concat_axis=0, tiled=True)

    full_rows = lax.all_gather(hidden, "tp", axis=1, tiled=True)
    late_pool, wkv, outgoing = lax.optimization_barrier((pool, wkv, outgoing))
    requests = lax.dynamic_slice_in_dim(perm, device * slots, slots)
    lengths = by_device[:, :slots].reshape(-1)[requests]
    tables = by_device[:, slots : layout.sends].reshape(-1, layout.row_pages)[requests]

    normalized_input = normalize(full_rows, norm_gain)
    query_proj = jnp.dot(normalized_input, wq, preferred_element_type=jnp.float32)
    pair_proj = jnp.dot(
        normalized_input, wkv.reshape(wkv.shape[0], -1), preferred_element_type=jnp.float32
    )
    positions = (lengths[:, None] + jnp.arange(tokens, dtype=jnp.int32)[None, :]).reshape(-1)
    queries = rotate(query_proj.reshape(query_proj.shape[0], -1, HEAD_SIZE), positions).astype(
        jnp.bfloat16
    )
    pair_heads = pair_proj.reshape(pair_proj.shape[0], 2, -1, HEAD_SIZE)
    new_keys = rotate(pair_heads[:, 0], positions).astype(jnp.bfloat16).reshape(-1, features)
    new_values = pair_heads[:, 1].astype(jnp.bfloat16).reshape(-1, features)
    recent = jnp.stack([new_keys, new_values], axis=1).reshape(slots, tokens, 2, features)
    context = attend(
        lengths,
        tables,
        queries.reshape(queries.shape[0], -1),
        new_keys,
        new_values,
        late_pool[:, :, 0],
        late_pool[:, :, 1],
    )
    partial_value = jnp.dot(context, wo, preferred_element_type=jnp.float32)
    recent, partial_value = lax.optimization_barrier((recent, partial_value))
    attn_out = lax.psum_scatter(
        partial_value.astype(jnp.bfloat16), "tp", scatter_dimension=1, tiled=True
    )
    zeros = jnp.zeros(pool.shape[1:], pool.dtype)
    late_arrived = lax.all_to_all(
        pack_pages(layout, table, perm, me, late_pool, recent, zeros),
        "req",
        split_axis=0,
        concat_axis=0,
        tiled=True,
    )
    early_pages, numbers = place_early_pages(layout, table, perm, me, arrived, zeros)
    decode_pages = place_late_pages(numbers, late_arrived, early_pages)
    return (attn_out, decode_pages.reshape((1, peers, block) + pool.shape[1:]))


def solution(mesh):
    placed = (
        P("req", "tp"),
        P(),
        P(None, "tp"),
        P(None, None, "tp"),
        P("tp", None),
        P(),
        P("req"),
        P("req", None),
        P("req", None, None, "tp"),
        P("req", None, None),
    )
    return jax.shard_map(
        grid_shards if mesh.shape["req"] == 8 else shards,
        mesh=mesh,
        in_specs=placed,
        out_specs=(P("req", "tp"), P("req", None, None, None, None, "tp")),
        check_vma=False,
    )
```

```python
import math

import jax
import jax.numpy as jnp
from jax import lax
from jax.experimental import pallas as pl
from jax.experimental.pallas import tpu as pltpu
from jax.sharding import PartitionSpec as P

HEAD_SIZE = 128
NORM_EPSILON = 1e-05
ROPE_THETA = 100000000.0
BLOCK_PAGES = 4


def normalize(rows, gain):
    wide_rows = rows.astype(jnp.float32)
    mean_square = jnp.mean(wide_rows * wide_rows, axis=-1, keepdims=True)
    return (wide_rows * lax.rsqrt(mean_square + NORM_EPSILON) * gain.astype(jnp.float32)).astype(
        jnp.bfloat16
    )


def rotate(vectors, positions):
    half_size = vectors.shape[-1] // 2
    frequency = jnp.power(
        jnp.float32(ROPE_THETA), -2.0 * jnp.arange(half_size, dtype=jnp.float32) / vectors.shape[-1]
    )
    angles = positions.astype(jnp.float32)[:, None] * frequency[None, :]
    cosine = jnp.cos(angles)[:, None, :]
    sine_part = jnp.sin(angles)[:, None, :]
    first_half = vectors[..., :half_size]
    second_half = vectors[..., half_size:]
    return jnp.concatenate(
        [
            first_half * cosine - second_half * sine_part,
            second_half * cosine + first_half * sine_part,
        ],
        axis=-1,
    )


class Layout:
    def __init__(self, slots, row_pages, peers, block):
        self.slots, self.row_pages, self.peers, self.block = slots, row_pages, peers, block
        self.code_width = row_pages + 1
        self.sends = slots + slots * row_pages
        self.used = self.sends + peers * block
        self.width = -(-self.used // 1024) * 1024
        self.late = 2 * slots
        self.early = block - self.late

    def request(self, perm, device, slot):
        request = perm[device * self.slots + slot]
        return lax.div(request, self.slots) * self.width, lax.rem(request, self.slots)

    def length(self, table, perm, device, slot):
        base, row = self.request(perm, device, slot)
        return table[base + row]

    def physical(self, table, perm, device, slot, page):
        base, row = self.request(perm, device, slot)
        return table[base + self.slots + row * self.row_pages + jnp.minimum(page, self.row_pages - 1)]

    def split(self, code):
        return lax.div(code, self.code_width), lax.rem(code, self.code_width)

    def visit(self, table, perm, source, target, page_len, use):
        whole = [
            lax.div(self.length(table, perm, source, slot), page_len) for slot in range(self.slots)
        ]
        base = source * self.width + self.sends + target * self.block
        plain, tails = jnp.int32(0), jnp.int32(self.block - 1)
        for number in range(self.block):
            code = table[base + number]
            first = whole[0]
            for slot in range(1, self.slots):
                low = slot * self.code_width
                first = jnp.where(code >= low, whole[slot] + low, first)
            valid, tail = code >= 0, code >= first
            place = jnp.where(valid, jnp.where(tail, tails, plain), -1)
            use(number, code, place)
            plain = plain + jnp.where(valid & jnp.logical_not(tail), 1, 0)
            tails = tails - jnp.where(tail, 1, 0)


def exchange_kernel(peers, mine, out, send_sems, recv_sems):
    me = lax.axis_index("req")
    barrier = pltpu.get_barrier_semaphore()
    for hop in range(1, peers):
        pl.semaphore_signal(
            barrier,
            inc=1,
            device_id={"req": lax.rem(me + hop, peers)},
            device_id_type=pl.DeviceIdType.MESH,
        )
    pl.semaphore_wait(barrier, peers - 1)
    copies = []
    for hop in range(1, peers):
        copy = pltpu.make_async_remote_copy(
            src_ref=mine,
            dst_ref=out.at[me],
            send_sem=send_sems.at[hop - 1],
            recv_sem=recv_sems.at[hop - 1],
            device_id={"req": lax.rem(me + hop, peers)},
            device_id_type=pl.DeviceIdType.MESH,
        )
        copy.start()
        copies.append(copy)
    out[me] = mine[...]
    for copy in copies:
        copy.wait()


def exchange(peers, mine):
    return pl.pallas_call(
        lambda *refs: exchange_kernel(peers, *refs),
        out_shape=jax.ShapeDtypeStruct((peers,) + mine.shape, mine.dtype),
        in_specs=[pl.BlockSpec(memory_space=pltpu.VMEM)],
        out_specs=pl.BlockSpec(memory_space=pltpu.VMEM),
        scratch_shapes=[
            pltpu.SemaphoreType.DMA((peers - 1,)),
            pltpu.SemaphoreType.DMA((peers - 1,)),
        ],
        compiler_params=pltpu.CompilerParams(collective_id=0, has_side_effects=True),
        name="exchange",
    )(mine)


BUFFERS = 32
AHEAD = 16


def ring(count, load, store, drain):
    def step(index, carry):
        @pl.when(index < count)
        def _():
            @pl.when(index >= BUFFERS)
            def _():
                drain(index - BUFFERS)

            load(index)

        @pl.when(index >= AHEAD)
        def _():
            store(index - AHEAD)

        return carry

    lax.fori_loop(0, count + AHEAD, step, 0)

    def last(index, carry):
        drain(index)
        return carry

    lax.fori_loop(max(count - BUFFERS, 0), count, last, 0)


def copy_rows(source, source_row, target, target_row, count, sem):
    size = target.shape[0]
    while size:
        offset = lax.div(count, 2 * size) * (2 * size)

        @pl.when(lax.rem(lax.div(count, size), 2) == 1)
        def _(size=size, offset=offset):
            pltpu.make_async_copy(
                source.at[pl.ds(source_row + offset, size)],
                target.at[pl.ds(target_row + offset, size)],
                sem,
            ).start()

        size //= 2


def pack_kernel(layout, late, table, perm, me, pool, *rest):
    if late:
        recent, zeros, out, codes, buffers, in_sems, out_sems = rest
    else:
        out, codes, buffers, in_sems, out_sems = rest
    page_len = buffers.shape[1]
    span = layout.late if late else layout.early
    start = layout.early if late else 0
    count = layout.peers * span

    def clear(index, carry):
        codes[index] = 0
        return carry

    lax.fori_loop(0, count, clear, 0)
    starts = []
    for slot in range(layout.slots):
        base, row = layout.request(perm, me[0], slot)
        starts.append(
            base + layout.slots + row * layout.row_pages - slot * layout.code_width
        )

    def block(target, carry):
        def use(number, code, place):
            inside = (place >= start) & (place < start + span)
            item = code
            if not late:
                origin = starts[0]
                for slot in range(1, layout.slots):
                    origin = jnp.where(code >= slot * layout.code_width, starts[slot], origin)
                item = table[jnp.where(inside, origin + code, 0)]

            @pl.when(inside)
            def _():
                codes[target * span + place - start] = item

        layout.visit(table, perm, me[0], target, page_len, use)
        return carry

    lax.fori_loop(0, layout.peers, block, 0)

    def load(index):
        spot = index & (BUFFERS - 1)
        target, sem = buffers.at[spot], in_sems.at[spot]
        if not late:
            pltpu.make_async_copy(pool.at[codes[index]], target, sem).start()
            return
        slot, page = layout.split(codes[index])
        cached = pool.at[layout.physical(table, perm, me[0], slot, page)]
        length = layout.length(table, perm, me[0], slot)
        full, kept = lax.div(length, page_len), lax.rem(length, page_len)

        @pl.when(page < full)
        def _():
            pltpu.make_async_copy(cached, target, sem).start()

        @pl.when(page == full)
        def _():
            copy_rows(cached, 0, target, 0, kept, sem)
            copy_rows(recent.at[slot], 0, target, kept, page_len - kept, sem)

        @pl.when(page > full)
        def _():
            copy_rows(recent.at[slot], page_len - kept, target, 0, kept, sem)
            copy_rows(zeros, 0, target, kept, page_len - kept, sem)

    def outward(index):
        spot = index & (BUFFERS - 1)
        return pltpu.make_async_copy(buffers.at[spot], out.at[index], out_sems.at[spot])

    def store(index):
        spot = index & (BUFFERS - 1)
        pltpu.make_async_copy(pool.at[0], buffers.at[spot], in_sems.at[spot]).wait()
        outward(index).start()

    ring(count, load, store, lambda index: outward(index).wait())


def scratch(layout, pool):
    return [
        pltpu.SMEM((layout.peers * layout.block,), jnp.int32),
        pltpu.VMEM((BUFFERS,) + pool.shape[-3:], pool.dtype),
        pltpu.SemaphoreType.DMA((BUFFERS,)),
        pltpu.SemaphoreType.DMA((BUFFERS,)),
    ]


def pack_pages(layout, table, perm, me, pool, *fresh):
    late = bool(fresh)
    span = layout.late if late else layout.early
    return pl.pallas_call(
        lambda *refs: pack_kernel(layout, late, *refs),
        out_shape=jax.ShapeDtypeStruct((layout.peers * span,) + pool.shape[1:], pool.dtype),
        grid_spec=pltpu.PrefetchScalarGridSpec(
            num_scalar_prefetch=3,
            grid=(1,),
            in_specs=[pl.BlockSpec(memory_space=pl.ANY)] * (1 + len(fresh)),
            out_specs=pl.BlockSpec(memory_space=pl.ANY),
            scratch_shapes=scratch(layout, pool),
        ),
        name="pack_late" if late else "pack_early",
    )(table, perm, me, pool, *fresh).reshape((layout.peers, span) + pool.shape[1:])


def place_kernel(layout, table, perm, me, arrived, zeros, *rest):
    out, numbers, places, buffers, in_sems, out_sems, blank, blank_sem = rest
    page_len = buffers.shape[1]

    def clear(index, carry):
        numbers[index] = -1
        return carry

    lax.fori_loop(0, layout.peers * layout.late, clear, 0)
    fill = pltpu.make_async_copy(zeros, blank, blank_sem)
    fill.start()

    def block(source, carry):
        def use(number, code, place):
            places[source * layout.block + number] = place

            @pl.when(place >= layout.early)
            def _():
                late_index = source * layout.late + place - layout.early
                numbers[late_index] = source * layout.block + number

        layout.visit(table, perm, source, me[0], page_len, use)
        return carry

    lax.fori_loop(0, layout.peers, block, 0)
    fill.wait()

    def inward(index):
        spot = index & (BUFFERS - 1)
        place = jnp.clip(places[index], 0, layout.early - 1)
        return pltpu.make_async_copy(
            arrived.at[lax.div(index, layout.block), place], buffers.at[spot], in_sems.at[spot]
        )

    def outward(index, held):
        return pltpu.make_async_copy(held, out.at[index], out_sems.at[index & (BUFFERS - 1)])

    def is_early(index):
        return (places[index] >= 0) & (places[index] < layout.early)

    def load(index):
        @pl.when(is_early(index))
        def _():
            inward(index).start()

    def store(index):
        @pl.when(is_early(index))
        def _():
            inward(index).wait()
            outward(index, buffers.at[index & (BUFFERS - 1)]).start()

        @pl.when(places[index] < 0)
        def _():
            outward(index, blank).start()

    def drain(index):
        @pl.when(places[index] < layout.early)
        def _():
            outward(index, blank).wait()

    ring(layout.peers * layout.block, load, store, drain)


def place_late_kernel(count, numbers, arrived, held, out, buffers, in_sems, out_sems):
    def inward(index):
        spot = index & (BUFFERS - 1)
        return pltpu.make_async_copy(arrived.at[index], buffers.at[spot], in_sems.at[spot])

    def outward(index):
        spot = index & (BUFFERS - 1)
        target = out.at[jnp.maximum(numbers[index], 0)]
        return pltpu.make_async_copy(buffers.at[spot], target, out_sems.at[spot])

    def load(index):
        @pl.when(numbers[index] >= 0)
        def _():
            inward(index).start()

    def store(index):
        @pl.when(numbers[index] >= 0)
        def _():
            inward(index).wait()
            outward(index).start()

    def drain(index):
        @pl.when(numbers[index] >= 0)
        def _():
            outward(index).wait()

    ring(count, load, store, drain)


def place_early_pages(layout, table, perm, me, arrived, zeros):
    page = arrived.shape[2:]
    return pl.pallas_call(
        lambda *refs: place_kernel(layout, *refs),
        out_shape=(
            jax.ShapeDtypeStruct((layout.peers * layout.block,) + page, arrived.dtype),
            jax.ShapeDtypeStruct((layout.peers * layout.late,), jnp.int32),
        ),
        grid_spec=pltpu.PrefetchScalarGridSpec(
            num_scalar_prefetch=3,
            grid=(1,),
            in_specs=[pl.BlockSpec(memory_space=pl.ANY)] * 2,
            out_specs=(
                pl.BlockSpec(memory_space=pl.ANY),
                pl.BlockSpec(memory_space=pltpu.SMEM),
            ),
            scratch_shapes=scratch(layout, arrived)
            + [pltpu.VMEM(page, arrived.dtype), pltpu.SemaphoreType.DMA],
        ),
        name="place_early",
    )(table, perm, me, arrived, zeros)


def place_late_pages(numbers, arrived, held):
    arrived = arrived.reshape((-1,) + held.shape[1:])
    return pl.pallas_call(
        lambda *refs: place_late_kernel(arrived.shape[0], *refs),
        out_shape=jax.ShapeDtypeStruct(held.shape, held.dtype),
        grid_spec=pltpu.PrefetchScalarGridSpec(
            num_scalar_prefetch=1,
            grid=(1,),
            in_specs=[pl.BlockSpec(memory_space=pl.ANY)] * 2,
            out_specs=pl.BlockSpec(memory_space=pl.ANY),
            scratch_shapes=[
                pltpu.VMEM((BUFFERS,) + held.shape[1:], held.dtype),
                pltpu.SemaphoreType.DMA((BUFFERS,)),
                pltpu.SemaphoreType.DMA((BUFFERS,)),
            ],
        ),
        input_output_aliases={2: 0},
        name="place_late",
    )(numbers, arrived, held)


def attend_kernel(lengths, tables, q_ref, nk_ref, nv_ref, *rest):
    k_refs, v_refs = rest[:BLOCK_PAGES], rest[BLOCK_PAGES : 2 * BLOCK_PAGES]
    out_ref, q_rows, top, total, acc = rest[2 * BLOCK_PAGES :]
    kv_heads, rows, head = q_rows.shape
    tokens = q_ref.shape[0]
    groups = rows // tokens
    slot, step = pl.program_id(0), pl.program_id(1)
    page_len = k_refs[0].shape[1]
    block_keys = BLOCK_PAGES * page_len
    length = lengths[slot]
    inv_scale = 1.0 / math.sqrt(head)

    def score(kv, keys):
        return (
            lax.dot_general(
                q_rows[kv], keys, (((1,), (1,)), ((), ())), preferred_element_type=jnp.float32
            )
            * inv_scale
        )

    @pl.when(step == 0)
    def _():
        for kv in range(kv_heads):
            columns = slice(kv * head, (kv + 1) * head)
            for group in range(groups):
                lane = (kv * groups + group) * head
                q_rows[kv, group * tokens : (group + 1) * tokens, :] = q_ref[:, lane : lane + head]
            scores = score(kv, nk_ref[:, columns])
            query_id = lax.broadcasted_iota(jnp.int32, scores.shape, 0) % tokens
            key_id = lax.broadcasted_iota(jnp.int32, scores.shape, 1)
            scores = jnp.where(key_id <= query_id, scores, -1e30)
            highest = jnp.max(scores, axis=-1, keepdims=True)
            weights = jnp.exp(scores - highest)
            top[kv] = jnp.broadcast_to(highest, (rows, head))
            total[kv] = jnp.broadcast_to(jnp.sum(weights, axis=-1, keepdims=True), (rows, head))
            acc[kv] = jnp.dot(
                weights.astype(jnp.bfloat16), nv_ref[:, columns], preferred_element_type=jnp.float32
            )

    @pl.when(step * block_keys < length)
    def _():
        for kv in range(kv_heads):
            columns = slice(kv * head, (kv + 1) * head)
            keys = jnp.concatenate([ref[0, :, columns] for ref in k_refs], axis=0)
            values = jnp.concatenate([ref[0, :, columns] for ref in v_refs], axis=0)
            scores = score(kv, keys)
            key_id = lax.broadcasted_iota(jnp.int32, scores.shape, 1)
            scores = jnp.where(key_id < length - step * block_keys, scores, -1e30)
            before = top[kv]
            highest = jnp.maximum(before, jnp.max(scores, axis=-1, keepdims=True))
            factor = jnp.exp(before - highest)
            weights = jnp.exp(scores - highest[:, :1])
            top[kv] = highest
            total[kv] = total[kv] * factor + jnp.sum(weights, axis=-1, keepdims=True)
            acc[kv] = acc[kv] * factor + jnp.dot(
                weights.astype(jnp.bfloat16), values, preferred_element_type=jnp.float32
            )

    @pl.when(step == pl.num_programs(1) - 1)
    def _():
        for kv in range(kv_heads):
            context = (acc[kv] / total[kv]).astype(jnp.bfloat16)
            for group in range(groups):
                lane = (kv * groups + group) * head
                out_ref[:, lane : lane + head] = context[group * tokens : (group + 1) * tokens]


def attend(lengths, tables, queries, new_keys, new_values, k_pool, v_pool):
    slots, row_pages = tables.shape
    tokens = queries.shape[0] // slots
    page_len, features = k_pool.shape[1:]
    kv_heads = features // HEAD_SIZE
    rows = tokens * (queries.shape[1] // features)
    steps = row_pages // BLOCK_PAGES

    def page_spec(number):
        def pick(slot, step, lengths, tables):
            last = (lengths[slot] + page_len - 1) // page_len - 1
            return (tables[slot * row_pages + jnp.minimum(step * BLOCK_PAGES + number, last)], 0, 0)

        return pl.BlockSpec((1, page_len, features), pick)

    def slot_rows(slot, step, lengths, tables):
        return (slot, 0)

    pages = [page_spec(number) for number in range(BLOCK_PAGES)]
    state = pltpu.VMEM((kv_heads, rows, HEAD_SIZE), jnp.float32)
    return pl.pallas_call(
        attend_kernel,
        out_shape=jax.ShapeDtypeStruct(queries.shape, jnp.bfloat16),
        grid_spec=pltpu.PrefetchScalarGridSpec(
            num_scalar_prefetch=2,
            grid=(slots, steps),
            in_specs=[
                pl.BlockSpec((tokens, queries.shape[1]), slot_rows),
                pl.BlockSpec((tokens, features), slot_rows),
                pl.BlockSpec((tokens, features), slot_rows),
            ]
            + pages
            + pages,
            out_specs=pl.BlockSpec((tokens, queries.shape[1]), slot_rows),
            scratch_shapes=[
                pltpu.VMEM((kv_heads, rows, HEAD_SIZE), jnp.bfloat16),
                state,
                state,
                state,
            ],
        ),
        compiler_params=pltpu.CompilerParams(
            dimension_semantics=("arbitrary", "arbitrary"), vmem_limit_bytes=40 << 20
        ),
        name="attend",
    )(
        lengths,
        tables.reshape(-1),
        queries,
        new_keys,
        new_values,
        *([k_pool] * BLOCK_PAGES),
        *([v_pool] * BLOCK_PAGES),
    )


LINKS = 3
LANE = 8
WIDE = 8
OWN_ROUNDS = 3
LATE_ROUND = 4
FIXED_ROUNDS = 12
SIDES = 3
ROUND_LIMIT = 56
SLOT_LIMIT = ROUND_LIMIT * LANE
TABLE = 2 * SLOT_LIMIT + ROUND_LIMIT * WIDE
WIDTHS = (LANE, LANE, WIDE)
OFFSETS = (0, LANE, 2 * LANE)
QUEUE = 96
ARRIVALS = 512
HELD = 1024
HELD_PAGES = 384


def neighbours():
    right = [(device, device + 2) for device in range(6)]
    left = [(device + 2, device) for device in range(6)]
    across = [(device, device ^ 1) for device in range(8)]
    return right, left, across


def loop(low, high, body):
    def step(index, carry):
        body(index)
        return carry

    lax.fori_loop(low, high, step, 0)


def plan_kernel(layout, first, table, perm, me, counts, send, *rest):
    if first:
        own_codes, early_first, runs, places, heads, tails, waiting, progress = rest
    else:
        receive, rounds = rest[:2]
        own_codes, early_first, runs, places, heads, tails, waiting, progress = rest[2:10]
        numbers, held, arrived_device, arrived_run, arrived_place, arrived_count = rest[10:]
    peers, block = layout.peers, layout.block
    own = me[0]
    page_len = layout.page_len

    def total(pair):
        return counts[pair]

    def early(pair):
        return counts[peers * peers + pair]

    def scan(source, target, use):
        whole = [
            lax.div(layout.length(table, perm, source, slot), page_len)
            for slot in range(layout.slots)
        ]
        base = source * layout.width + layout.sends + target * block
        plain, tail_rank = jnp.int32(0), early(source * peers + target)
        for number in range(block):
            code = table[base + number]
            edge = whole[0]
            for slot in range(1, layout.slots):
                low = slot * layout.code_width
                edge = jnp.where(code >= low, whole[slot] + low, edge)
            valid, tail = code >= 0, code >= edge
            use(number, code, valid, jnp.where(tail, tail_rank, plain))
            plain = plain + jnp.where(valid & jnp.logical_not(tail), 1, 0)
            tail_rank = tail_rank + jnp.where(tail, 1, 0)

    def list_own(target):
        def use(number, code, valid, rank):
            @pl.when(valid)
            def _():
                own_codes[target * block + rank] = code

        scan(own, target, use)

    loop(0, peers, list_own)
    if not first:

        def list_numbers(source):
            def use(number, code, valid, rank):
                @pl.when(valid)
                def _():
                    numbers[source * block + rank] = source * block + number

            scan(source, own, use)

        loop(0, peers, list_numbers)

    def clear(index):
        early_first[index] = 0

    loop(0, peers * peers, clear)
    half = peers // 2
    for direction in range(2):
        sources = range(direction * half, (direction + 1) * half)
        targets = range((1 - direction) * half, (2 - direction) * half)
        loads = []
        for column in range(2):
            load = jnp.int32(0)
            for source in sources:
                if source % 2 == column:
                    for target in targets:
                        load = load + total(source * peers + target)
            loads.append(load)
        heavy = jnp.where(loads[1] > loads[0], 1, 0)
        left = lax.div(jnp.abs(loads[0] - loads[1]), 2)
        zs = sorted({source // 2 for source in sources})
        zt = sorted({target // 2 for target in targets})
        for _, a, b in sorted((abs(a - b), a, b) for a in zs for b in zt):
            pair = (2 * a + heavy) * peers + 2 * b + 1 - heavy
            moved = jnp.minimum(left, early(pair))
            early_first[pair] = moved
            left = left - moved

    def clear_queue(index):
        heads[index] = 0
        tails[index] = 0

    loop(0, peers * LINKS * 4, clear_queue)

    def clear_waiting(index):
        waiting[index] = 0

    loop(0, peers * LINKS, clear_waiting)
    progress[0] = 0

    def push(device, run, place, turn):
        target = (run >> 10) & 7
        steps = (target >> 1) - (device >> 1)
        flip = (target ^ device) & 1
        across = (steps == 0) | turn
        link = jnp.where(across, 2, jnp.where(steps > 0, 0, 1))
        lane = device * LINKS + link
        waiting[lane] = waiting[lane] + 1
        queue = lane * 4 + jnp.abs(steps) + flip - 1
        spot = tails[queue]
        runs[queue * QUEUE + spot] = run
        places[queue * QUEUE + spot] = place
        tails[queue] = spot + 1

    def make_run(pair, start, count):
        return (pair << 10) | (start << 5) | count

    def open_pair(pair):
        source = pair >> 3
        moved = early_first[pair]
        count = early(pair)
        wanted = source != (pair & 7)
        if first:
            wanted = wanted & (source == own)

        @pl.when(wanted & (moved > 0))
        def _():
            push(source, make_run(pair, 0, moved), -1, True)

        @pl.when(wanted & (count > moved))
        def _():
            push(source, make_run(pair, moved, count - moved), -1, False)

    loop(0, peers * peers, open_pair)

    def open_late(pair):
        source = pair >> 3
        count = total(pair) - early(pair)

        @pl.when((source != (pair & 7)) & (count > 0))
        def _():
            push(source, make_run(pair, early(pair), count), -1, False)

    def move(step, device, link, width, toward):
        lane = device * LINKS + link

        @pl.when(waiting[lane] > 0)
        def _():
            drain(step, lane, device, link, width, toward)

    def drain(step, lane, device, link, width, toward):
        room = jnp.int32(width)
        origin = link * SLOT_LIMIT + step * width + width
        side = lax.rem(step, SIDES)
        for rank in (3, 2, 1, 0):
            queue = lane * 4 + rank

            def more(state):
                room, head, tail = state
                return (room > 0) & (head < tail)

            def take(state):
                room, head, tail = state
                spot = queue * QUEUE + head
                run, place = runs[spot], places[spot]
                pair, start, count = run >> 10, (run >> 5) & 31, run & 31
                taken = jnp.minimum(room, count)
                base = origin - room
                final = (pair & 7) == toward

                def note_sent():
                    def note(index):
                        code = own_codes[(pair & 7) * block + start + index]
                        send[base + index] = jnp.where(place < 0, code, HELD + place + index)

                    loop(0, taken, note)

                whole = taken == count
                waiting[lane] = waiting[lane] - jnp.where(whole, 1, 0)
                runs[spot] = make_run(pair, start + taken, count - taken)
                places[spot] = jnp.where(place < 0, place, place + taken)
                if first:
                    note_sent()
                else:
                    slot = held[toward]
                    passing = jnp.where(final, 0, taken)
                    progress[0] = progress[0] + taken - passing
                    held[toward] = slot + passing
                    added = arrived_count[side]
                    at = side * ARRIVALS + added
                    arrived_device[at] = toward
                    arrived_run[at] = make_run(pair, start, taken)
                    arrived_place[at] = slot
                    arrived_count[side] = added + jnp.where(final, 0, 1)

                    @pl.when((device == own) | (toward == own))
                    def _():
                        @pl.when(device == own)
                        def _():
                            note_sent()

                        @pl.when(toward == own)
                        def _():
                            def note(index):
                                number = numbers[(pair >> 3) * block + start + index]
                                receive[base + index] = jnp.where(
                                    final, number, HELD + slot + index
                                )

                            loop(0, taken, note)

                return room - taken, head + jnp.where(whole, 1, 0), tail

            room, head, _ = lax.while_loop(more, take, (room, heads[queue], tails[queue]))
            heads[queue] = head

    def blank(step):
        def one(index):
            for link in (0, 1):
                spot = link * SLOT_LIMIT + step * LANE + index
                send[spot] = -1
                if not first:
                    receive[spot] = -1

        def wide(index):
            spot = 2 * SLOT_LIMIT + step * WIDE + index
            send[spot] = -1
            if not first:
                receive[spot] = -1

        loop(0, LANE, one)
        loop(0, WIDE, wide)

    if first:
        for step in range(OWN_ROUNDS):
            blank(step)
            move(step, own, 0, LANE, own + 2)
            move(step, own, 1, LANE, own - 2)
            move(step, own, 2, WIDE, own ^ 1)
        return

    wanted = jnp.int32(0)
    for source in range(peers):
        held[source] = 0
        for target in range(peers):
            if source != target:
                wanted = wanted + total(source * peers + target)
    for side in range(SIDES):
        arrived_count[side] = 0

    def unfinished(step):
        return (step <= FIXED_ROUNDS) | (progress[0] < wanted)

    def advance(step):
        blank(step)

        @pl.when(step == LATE_ROUND)
        def _():
            loop(0, peers * peers, open_late)

        def arrive_all(side):
            def arrive(index):
                at = side * ARRIVALS + index
                push(arrived_device[at], arrived_run[at], arrived_place[at], False)

            loop(0, arrived_count[side], arrive)
            arrived_count[side] = 0

        @pl.when(step == OWN_ROUNDS)
        def _():
            for past in range(OWN_ROUNDS - 2):
                arrive_all(past)

        @pl.when(step >= OWN_ROUNDS)
        def _():
            arrive_all(lax.rem(step + 1, SIDES))

        def one(device):
            move(step, device, 0, LANE, device + 2)
            move(step, device, 1, LANE, device - 2)
            move(step, device, 2, WIDE, device ^ 1)

        loop(0, peers, one)

        @pl.when(progress[0] >= wanted)
        def _():
            rounds[0] = jnp.minimum(rounds[0], step + 1)

        return step + 1

    rounds[0] = jnp.int32(ROUND_LIMIT)
    rounds[1] = jnp.int32(0)
    end = lax.while_loop(unfinished, advance, jnp.int32(0))
    blank(end)


def plan(layout, first, table, perm, me, counts):
    tables = jax.ShapeDtypeStruct((TABLE,), jnp.int32)
    outs = (tables,) if first else (tables, tables, jax.ShapeDtypeStruct((2,), jnp.int32))
    peers = layout.peers

    def words(count):
        return pltpu.SMEM((count,), jnp.int32)

    queues = peers * LINKS * 4
    room = [
        words(peers * layout.block),
        words(peers * peers),
        words(queues * QUEUE),
        words(queues * QUEUE),
        words(queues),
        words(queues),
        words(peers * LINKS),
        words(1),
    ]
    if not first:
        room += [words(peers * layout.block), words(peers)]
        room += [words(SIDES * ARRIVALS)] * 3 + [words(SIDES)]
    out = pl.pallas_call(
        lambda *refs: plan_kernel(layout, first, *refs),
        out_shape=outs,
        grid_spec=pltpu.PrefetchScalarGridSpec(
            num_scalar_prefetch=4,
            grid=(1,),
            in_specs=[],
            out_specs=tuple(pl.BlockSpec(memory_space=pltpu.SMEM) for _ in outs),
            scratch_shapes=room,
        ),
        name="plan_first" if first else "plan_rest",
    )(table, perm, me, counts)
    return out[0] if first else out


def own_page(layout, table, perm, me, pool, recent, zeros, code, target, sem):
    slot, page = layout.split(code)
    cached = pool.at[layout.physical(table, perm, me[0], slot, page)]
    if recent is None:
        pltpu.make_async_copy(cached, target, sem).start()
        return
    page_len = layout.page_len
    length = layout.length(table, perm, me[0], slot)
    full, kept = lax.div(length, page_len), lax.rem(length, page_len)

    @pl.when(page < full)
    def _():
        pltpu.make_async_copy(cached, target, sem).start()

    @pl.when(page == full)
    def _():
        copy_rows(cached, 0, target, 0, kept, sem)
        copy_rows(recent.at[slot], 0, target, kept, page_len - kept, sem)

    @pl.when(page > full)
    def _():
        copy_rows(recent.at[slot], page_len - kept, target, 0, kept, sem)
        copy_rows(zeros, 0, target, kept, page_len - kept, sem)


def links_of(step):
    return (0, 1, 2)


def step_kernel(layout, kind, parity, table, perm, me, step, send, *rest):
    recent = zeros = None
    count = len(links_of(parity))
    if kind == "first":
        pool, *lanes, sent, load_sems, store_sems = rest
        groups = []
    elif kind == "begin":
        receive, pool = rest[:2]
        arrived = rest[2:8]
        out, held, *lanes = rest[8 : 10 + count]
        sent, load_sems, store_sems, came, land_sems, leave_sems = rest[10 + count :]
        groups = [3, 2]
    elif kind == "step":
        receive, pool, recent, zeros = rest[:4]
        arrived = rest[4 : 4 + count]
        rest = rest[6 + count :]
        out, held, *lanes = rest[: 2 + count]
        sent, load_sems, store_sems, came, land_sems, leave_sems = rest[2 + count :]
        groups = [2]
    else:
        receive = send
        arrived = rest[:6]
        out, came, land_sems, leave_sems = rest[7:]
        groups = [2, 1]
    relaying = kind in ("begin", "step")
    stages = [[] for _ in range(5)]
    first_ref = [0]
    for back in groups:
        first_ref.append(first_ref[-1] + len(links_of(parity - back)))

    def spots(body):
        for link in links_of(parity):
            loop(0, WIDTHS[link], lambda index, link=link: body(link, index))

    def every(body):
        for group, back in enumerate(groups):
            for link in links_of(parity - back):
                base = link * SLOT_LIMIT + (step[0] - back) * WIDTHS[link]

                def row(index, group=group, link=link, base=base):
                    body(group, link, index, receive[base + index])

                loop(0, WIDTHS[link], row)

    def outgoing(link, index):
        return send[link * SLOT_LIMIT + step[0] * WIDTHS[link] + index]

    def load(link, index, source):
        spot = OFFSETS[link] + index
        return pltpu.make_async_copy(source, sent.at[spot], load_sems.at[spot])

    def store(link, index):
        spot = OFFSETS[link] + index
        return pltpu.make_async_copy(
            sent.at[spot], lanes[link].at[index], store_sems.at[spot]
        )

    if groups:

        def landing(group, link, index):
            return pltpu.make_async_copy(
                arrived[first_ref[group] + link].at[index],
                came.at[group, OFFSETS[link] + index],
                land_sems.at[group, OFFSETS[link] + index],
            )

        def leaving(group, link, index, target):
            spot = OFFSETS[link] + index
            return pltpu.make_async_copy(
                came.at[group, spot], target, leave_sems.at[group, spot]
            )

        def land(group, link, index, to):
            @pl.when(to >= 0)
            def _():
                landing(group, link, index).start()

        stages[0].append(lambda: every(land))

    if kind != "last":

        def fetch(link, index):
            code = outgoing(link, index)

            @pl.when((code >= 0) & (code < HELD))
            def _():
                own_page(
                    layout, table, perm, me, pool, recent, zeros, code,
                    sent.at[OFFSETS[link] + index], load_sems.at[OFFSETS[link] + index],
                )

        stages[0].append(lambda: spots(fetch))

    if groups:

        def leave(group, link, index, to):
            @pl.when(to >= 0)
            def _():
                landing(group, link, index).wait()

            @pl.when((to >= 0) & (to < HELD))
            def _():
                leaving(group, link, index, out.at[to]).start()

            if relaying:

                @pl.when(to >= HELD)
                def _():
                    leaving(group, link, index, held.at[to - HELD]).start()

        stages[1].append(lambda: every(leave))

    if kind != "last":

        def pass_on(link, index):
            code = outgoing(link, index)

            @pl.when((code >= 0) & (code < HELD))
            def _():
                load(link, index, pool.at[0]).wait()
                store(link, index).start()

        stages[1].append(lambda: spots(pass_on))

    if groups:

        def left(group, link, index, to):
            @pl.when(to >= 0)
            def _():
                leaving(group, link, index, out.at[0]).wait()

        stages[2].append(lambda: every(left))

    if relaying:

        def reload(link, index):
            code = outgoing(link, index)

            @pl.when(code >= HELD)
            def _():
                load(link, index, held.at[code - HELD]).start()

        def relayed(link, index):
            code = outgoing(link, index)

            @pl.when(code >= HELD)
            def _():
                load(link, index, pool.at[0]).wait()
                store(link, index).start()

        stages[2].append(lambda: spots(reload))
        stages[3].append(lambda: spots(relayed))

    if kind != "last":

        def stored(link, index):
            @pl.when(outgoing(link, index) >= 0)
            def _():
                store(link, index).wait()

        stages[4].append(lambda: spots(stored))

    return stages


def run_stages(stages):
    for stage in stages:
        for work in stage:
            work()


def any_specs(count):
    return [pl.BlockSpec(memory_space=pltpu.HBM)] * count


def lane_shapes(pool, parity):
    return tuple(
        jax.ShapeDtypeStruct((WIDTHS[link],) + pool.shape[1:], pool.dtype)
        for link in links_of(parity)
    )


SPOTS = 2 * LANE + WIDE


def send_room(pool):
    return [
        pltpu.VMEM((SPOTS,) + pool.shape[1:], pool.dtype),
        pltpu.SemaphoreType.DMA((SPOTS,)),
        pltpu.SemaphoreType.DMA((SPOTS,)),
    ]


def land_room(pool, groups):
    return [
        pltpu.VMEM((groups, SPOTS) + pool.shape[1:], pool.dtype),
        pltpu.SemaphoreType.DMA((groups, SPOTS)),
        pltpu.SemaphoreType.DMA((groups, SPOTS)),
    ]


ROOMY = pltpu.CompilerParams(vmem_limit_bytes=40 << 20)


def pack_first(layout, table, perm, me, step, send, pool):
    parity = step % 2
    return pl.pallas_call(
        lambda *refs: run_stages(step_kernel(layout, "first", parity, *refs)),
        out_shape=lane_shapes(pool, parity),
        grid_spec=pltpu.PrefetchScalarGridSpec(
            num_scalar_prefetch=5,
            grid=(1,),
            in_specs=any_specs(1),
            out_specs=tuple(any_specs(len(links_of(parity)))),
            scratch_shapes=send_room(pool),
        ),
        compiler_params=ROOMY,
        name="pack_first",
    )(table, perm, me, number(step), send, pool)


def relay_begin(layout, table, perm, me, step, send, receive, pool, arrived):
    parity = step % 2
    page = pool.shape[1:]
    results = pl.pallas_call(
        lambda *refs: run_stages(step_kernel(layout, "begin", parity, *refs)),
        out_shape=(
            jax.ShapeDtypeStruct((layout.peers * layout.block,) + page, pool.dtype),
            jax.ShapeDtypeStruct((HELD_PAGES,) + page, pool.dtype),
        )
        + lane_shapes(pool, parity),
        grid_spec=pltpu.PrefetchScalarGridSpec(
            num_scalar_prefetch=6,
            grid=(1,),
            in_specs=any_specs(7),
            out_specs=tuple(any_specs(2 + len(links_of(parity)))),
            scratch_shapes=send_room(pool) + land_room(pool, 2),
        ),
        compiler_params=ROOMY,
        name="relay_begin",
    )(table, perm, me, number(step), send, receive, pool, *arrived)
    return results[2:], results[0], results[1]


def relay(
    layout, parity, table, perm, me, step, send, receive, pool, recent, zeros, arrived, out, held
):
    count = len(arrived)
    results = pl.pallas_call(
        lambda *refs: run_stages(step_kernel(layout, "step", parity, *refs)),
        out_shape=(
            jax.ShapeDtypeStruct(out.shape, out.dtype),
            jax.ShapeDtypeStruct(held.shape, held.dtype),
        )
        + lane_shapes(pool, parity),
        grid_spec=pltpu.PrefetchScalarGridSpec(
            num_scalar_prefetch=6,
            grid=(1,),
            in_specs=any_specs(5 + count),
            out_specs=tuple(any_specs(2 + count)),
            scratch_shapes=send_room(pool) + land_room(pool, 1),
        ),
        input_output_aliases={9 + count: 0, 10 + count: 1},
        compiler_params=ROOMY,
        name="relay",
    )(table, perm, me, step, send, receive, pool, recent, zeros, *arrived, out, held)
    return results[2:], results[0], results[1]


def land_last(layout, table, perm, me, step, receive, arrived, out):
    return pl.pallas_call(
        lambda *refs: run_stages(step_kernel(layout, "last", 0, *refs)),
        out_shape=jax.ShapeDtypeStruct(out.shape, out.dtype),
        grid_spec=pltpu.PrefetchScalarGridSpec(
            num_scalar_prefetch=5,
            grid=(1,),
            in_specs=any_specs(7),
            out_specs=pl.BlockSpec(memory_space=pl.ANY),
            scratch_shapes=land_room(out, 2),
        ),
        input_output_aliases={11: 0},
        compiler_params=ROOMY,
        name="land_last",
    )(table, perm, me, step, receive, *arrived, out)


def fill_kernel(
    layout, table, perm, me, pool, recent, zeros, before, out, blank, mine, sems, load_sems
):
    del before
    own, block = me[0], layout.block
    fill = pltpu.make_async_copy(zeros, blank, load_sems.at[block])
    fill.start()

    def code_of(source, number):
        return table[source * layout.width + layout.sends + own * block + number]

    def outward(source, number, held_page):
        return pltpu.make_async_copy(
            held_page, out.at[source * block + number], sems.at[source & 1, number]
        )

    def inward(number):
        code = code_of(own, number)

        @pl.when(code >= 0)
        def _():
            own_page(
                layout, table, perm, me, pool, recent, zeros, code, mine.at[number],
                load_sems.at[number],
            )

    loop(0, block, inward)
    fill.wait()

    def is_ours(source, number):
        return (code_of(source, number) < 0) | (source == own)

    def finish(source):
        def one(number):
            @pl.when(is_ours(source, number))
            def _():
                outward(source, number, blank).wait()

        loop(0, block, one)

    def begin(source):
        @pl.when(source >= 2)
        def _():
            finish(source - 2)

        def one(number):
            code = code_of(source, number)

            @pl.when(code < 0)
            def _():
                outward(source, number, blank).start()

            @pl.when((code >= 0) & (source == own))
            def _():
                pltpu.make_async_copy(pool.at[0], mine.at[number], load_sems.at[number]).wait()
                outward(source, number, mine.at[number]).start()

        loop(0, block, one)

    loop(0, layout.peers, begin)
    loop(layout.peers - 2, layout.peers, finish)


def fill_local(layout, table, perm, me, pool, recent, zeros, out):
    page = pool.shape[1:]
    return pl.pallas_call(
        lambda *refs: fill_kernel(layout, *refs),
        out_shape=jax.ShapeDtypeStruct(out.shape, out.dtype),
        grid_spec=pltpu.PrefetchScalarGridSpec(
            num_scalar_prefetch=3,
            grid=(1,),
            in_specs=any_specs(4),
            out_specs=pl.BlockSpec(memory_space=pl.ANY),
            scratch_shapes=[
                pltpu.VMEM(page, pool.dtype),
                pltpu.VMEM((layout.block,) + page, pool.dtype),
                pltpu.SemaphoreType.DMA((2, layout.block)),
                pltpu.SemaphoreType.DMA((layout.block + 1,)),
            ],
        ),
        input_output_aliases={6: 0},
        compiler_params=ROOMY,
        name="fill_local",
    )(table, perm, me, pool, recent, zeros, out)


PARTS = 4


def part_kernel(slot, part, lengths, tables, q_ref, *rest):
    first, last = part == 0, part == PARTS - 1
    if first:
        (nk_ref, nv_ref), rest = rest[:2], rest[2:]
    else:
        before, rest = rest[:3], rest[3:]
    pages, rest = rest[:BLOCK_PAGES], rest[BLOCK_PAGES:]
    if last:
        out_ref, q_rows, top, total, acc = rest
    else:
        top, total, acc, q_rows = rest
    kv_heads, rows, head = q_rows.shape
    tokens = q_ref.shape[0]
    groups = rows // tokens
    step = pl.program_id(0)
    page_len = pages[0].shape[1]
    block_keys = BLOCK_PAGES * page_len
    begin = (part * pl.num_programs(0) + step) * block_keys
    length = lengths[slot]
    inv_scale = 1.0 / math.sqrt(head)

    def score(kv, keys):
        return (
            lax.dot_general(
                q_rows[kv], keys, (((1,), (1,)), ((), ())), preferred_element_type=jnp.float32
            )
            * inv_scale
        )

    @pl.when(step == 0)
    def _():
        for kv in range(kv_heads):
            for group in range(groups):
                lane = (kv * groups + group) * head
                q_rows[kv, group * tokens : (group + 1) * tokens, :] = q_ref[:, lane : lane + head]
            if not first:
                continue
            columns = slice(kv * head, (kv + 1) * head)
            scores = score(kv, nk_ref[:, columns])
            query_id = lax.broadcasted_iota(jnp.int32, scores.shape, 0) % tokens
            key_id = lax.broadcasted_iota(jnp.int32, scores.shape, 1)
            scores = jnp.where(key_id <= query_id, scores, -1e30)
            highest = jnp.max(scores, axis=-1, keepdims=True)
            weights = jnp.exp(scores - highest)
            top[kv] = jnp.broadcast_to(highest, (rows, head))
            total[kv] = jnp.broadcast_to(jnp.sum(weights, axis=-1, keepdims=True), (rows, head))
            acc[kv] = jnp.dot(
                weights.astype(jnp.bfloat16), nv_ref[:, columns], preferred_element_type=jnp.float32
            )
        if not first:
            top[...] = before[0][...]
            total[...] = before[1][...]
            acc[...] = before[2][...]

    def absorb(masked):
        flat = [ref[0].reshape(page_len, 2 * kv_heads * head) for ref in pages]
        for kv in range(kv_heads):
            keys = jnp.concatenate([x[:, kv * head : (kv + 1) * head] for x in flat], axis=0)
            low = (kv_heads + kv) * head
            values = jnp.concatenate([x[:, low : low + head] for x in flat], axis=0)
            scores = score(kv, keys)
            if masked:
                key_id = lax.broadcasted_iota(jnp.int32, scores.shape, 1)
                scores = jnp.where(key_id < length - begin, scores, -1e30)
            past = top[kv]
            highest = jnp.maximum(past, jnp.max(scores, axis=-1, keepdims=True))
            factor = jnp.exp(past - highest)
            weights = jnp.exp(scores - highest[:, :1])
            top[kv] = highest
            total[kv] = total[kv] * factor + jnp.sum(weights, axis=-1, keepdims=True)
            acc[kv] = acc[kv] * factor + jnp.dot(
                weights.astype(jnp.bfloat16), values, preferred_element_type=jnp.float32
            )

    @pl.when(begin + block_keys <= length)
    def _():
        absorb(False)

    @pl.when((begin < length) & (begin + block_keys > length))
    def _():
        absorb(True)

    if last:

        @pl.when(step == pl.num_programs(0) - 1)
        def _():
            for kv in range(kv_heads):
                context = (acc[kv] / total[kv]).astype(jnp.bfloat16)
                for group in range(groups):
                    lane = (kv * groups + group) * head
                    out_ref[:, lane : lane + head] = context[
                        group * tokens : (group + 1) * tokens
                    ]


def relay_part_kernel(layout, slot, part, *refs):
    table, perm, me, number, send, receive, lengths, tables = refs[:8]
    ins, rest = refs[8:16], refs[16:]
    count = 3 if part else 2
    inner, rest = rest[: 1 + count + BLOCK_PAGES], rest[1 + count + BLOCK_PAGES :]
    outs, rest = rest[: 2 + LINKS], rest[2 + LINKS :]
    made = 1 if part == PARTS - 1 else 3
    results, rest = rest[:made], rest[made:]
    rooms, rest = rest[:6], rest[6:]
    stages = step_kernel(
        layout, "step", 0, table, perm, me, number, send, receive, *ins, *outs, *rooms
    )
    steps = tables.shape[0] // layout.slots // BLOCK_PAGES // PARTS
    for index in range(4):

        @pl.when(pl.program_id(0) == index * steps // 4)
        def _(index=index):
            run_stages(stages[index : index + 1])

    part_kernel(slot, part, lengths, tables, *inner, *results, *rest)

    @pl.when(pl.program_id(0) == pl.num_programs(0) - 1)
    def _():
        run_stages(stages[4:])


def relay_part(
    layout, slot, part, table, perm, me, step, send, receive, lengths, tables, pool, recent, zeros,
    arrived, out, held, queries, fresh, state,
):
    slots, row_pages = tables.shape
    tokens = queries.shape[0] // slots
    page_len, features = pool.shape[1], pool.shape[3]
    kv_heads = features // HEAD_SIZE
    rows = tokens * (queries.shape[1] // features)
    steps = row_pages // BLOCK_PAGES // PARTS
    first, last = part == 0, part == PARTS - 1

    def page_spec(index):
        def pick(step, *words):
            lengths, tables = words[6:]
            final = (lengths[slot] + page_len - 1) // page_len - 1
            page = (part * steps + step) * BLOCK_PAGES + index
            return (tables[slot * row_pages + jnp.minimum(page, final)], 0, 0, 0)

        return pl.BlockSpec((1, page_len, 2, features), pick)

    def slot_rows(step, *words):
        return (slot, 0)

    shape = (kv_heads, rows, HEAD_SIZE)
    state_spec = pl.BlockSpec(shape, lambda step, *words: (0, 0, 0))
    operands = list(fresh) if first else list(state)
    specs = [pl.BlockSpec((tokens, features), slot_rows)] * 2 if first else [state_spec] * 3
    room = [pltpu.VMEM(shape, jnp.bfloat16)]
    if last:
        made = (jax.ShapeDtypeStruct((tokens, queries.shape[1]), queries.dtype),)
        made_specs = (pl.BlockSpec(made[0].shape, lambda step, *words: (0, 0)),)
        room += [pltpu.VMEM(shape, jnp.float32)] * 3
    else:
        made = (jax.ShapeDtypeStruct(shape, jnp.float32),) * 3
        made_specs = (state_spec,) * 3
    results = pl.pallas_call(
        lambda *refs: relay_part_kernel(layout, slot, part, *refs),
        out_shape=(
            jax.ShapeDtypeStruct(out.shape, out.dtype),
            jax.ShapeDtypeStruct(held.shape, held.dtype),
        )
        + lane_shapes(pool, 0)
        + made,
        grid_spec=pltpu.PrefetchScalarGridSpec(
            num_scalar_prefetch=8,
            grid=(steps,),
            in_specs=any_specs(8)
            + [pl.BlockSpec((tokens, queries.shape[1]), slot_rows)]
            + specs
            + [page_spec(page) for page in range(BLOCK_PAGES)],
            out_specs=tuple(any_specs(2 + LINKS)) + made_specs,
            scratch_shapes=send_room(pool) + land_room(pool, 1) + room,
        ),
        input_output_aliases={14: 0, 15: 1},
        compiler_params=pltpu.CompilerParams(
            dimension_semantics=("arbitrary",), vmem_limit_bytes=48 << 20
        ),
        name="relay_part",
    )(
        table, perm, me, number(step), send, receive, lengths, tables.reshape(-1), pool, recent,
        zeros, *arrived, out, held, queries, *operands, *([pool] * BLOCK_PAGES),
    )
    return results[2:5], results[0], results[1], results[5:]


PAIR_DEPTH = 640


def pair_kernel(x_ref, w_ref, out_ref):
    @pl.when(pl.program_id(0) == 0)
    def _():
        out_ref[...] = jnp.zeros_like(out_ref)

    depth = w_ref.shape[0]
    out_ref[...] += jnp.dot(
        x_ref[...], w_ref[...].reshape(depth, -1), preferred_element_type=jnp.float32
    )


def project_pair(rows, wkv):
    count, width = rows.shape
    features = wkv.shape[1] * wkv.shape[2]
    return pl.pallas_call(
        pair_kernel,
        out_shape=jax.ShapeDtypeStruct((count, features), jnp.float32),
        grid=(width // PAIR_DEPTH,),
        in_specs=[
            pl.BlockSpec((count, PAIR_DEPTH), lambda step: (0, step)),
            pl.BlockSpec((PAIR_DEPTH,) + wkv.shape[1:], lambda step: (step, 0, 0)),
        ],
        out_specs=pl.BlockSpec((count, features), lambda step: (0, 0)),
        compiler_params=ROOMY,
        name="project_pair",
    )(rows, wkv)


def after(value, *others):
    return lax.optimization_barrier((value,) + others)[0]


def page_counts(layout, by_device, perm):
    lengths = by_device[:, : layout.slots].reshape(-1)[perm].reshape(layout.peers, layout.slots)
    whole = lax.div(lengths, layout.page_len)
    codes = by_device[:, layout.sends : layout.used].reshape(
        layout.peers, layout.peers, layout.block
    )
    edge = whole[:, 0, None, None]
    for slot in range(1, layout.slots):
        low = slot * layout.code_width
        edge = jnp.where(codes >= low, whole[:, slot, None, None] + low, edge)
    valid = codes >= 0
    plain = valid & (codes < edge)
    return jnp.concatenate(
        [
            jnp.sum(valid.astype(jnp.int32), axis=-1).reshape(-1),
            jnp.sum(plain.astype(jnp.int32), axis=-1).reshape(-1),
        ]
    )


def hop(lanes):
    return tuple(
        lax.ppermute(lane, "req", pairs) for lane, pairs in zip(lanes, neighbours())
    )


def number(value):
    return jnp.asarray(value, jnp.int32).reshape(1)


def grid_shards(hidden, norm_gain, wq, wkv, wo, perm, prior_len, page_table, pool, send_table):
    slots = prior_len.shape[0]
    tokens = hidden.shape[0] // slots
    _, peers, block = send_table.shape
    layout = Layout(slots, page_table.shape[1], peers, block)
    layout.page_len = pool.shape[1]
    features = pool.shape[-1]
    device = lax.axis_index("req")
    me = device.astype(jnp.int32).reshape(1)
    mine = jnp.concatenate([prior_len, page_table.reshape(-1), send_table.reshape(-1)])
    mine = jnp.pad(mine, (0, layout.width - layout.used)).reshape(-1, 128)
    by_device = exchange(peers, mine)
    table = by_device.reshape(-1)
    by_device = by_device.reshape(peers, layout.width)
    counts = page_counts(layout, by_device, perm)
    first = plan(layout, True, table, perm, me, counts)
    lanes = [pack_first(layout, table, perm, me, step, first, pool) for step in range(2)]
    arrived = [hop(lane) for lane in lanes]
    full_rows = lax.all_gather(hidden, "tp", axis=1, tiled=True)
    requests = lax.dynamic_slice_in_dim(perm, device * slots, slots)
    lengths = by_device[:, :slots].reshape(-1)[requests]
    tables = by_device[:, slots : layout.sends].reshape(-1, layout.row_pages)[requests]
    positions = (lengths[:, None] + jnp.arange(tokens, dtype=jnp.int32)[None, :]).reshape(-1)

    full_rows = after(full_rows, lanes[1][0])
    normalized_input = normalize(full_rows, norm_gain)
    pair_proj = project_pair(normalized_input, wkv)
    pair_heads = pair_proj.reshape(pair_proj.shape[0], 2, -1, HEAD_SIZE)
    new_keys = rotate(pair_heads[:, 0], positions).astype(jnp.bfloat16).reshape(-1, features)
    new_values = pair_heads[:, 1].astype(jnp.bfloat16).reshape(-1, features)
    recent = jnp.stack([new_keys, new_values], axis=1).reshape(slots, tokens, 2, features)
    zeros = jnp.zeros(pool.shape[1:], pool.dtype)

    query_proj = jnp.dot(normalized_input, wq, preferred_element_type=jnp.float32)
    queries = rotate(
        query_proj.reshape(query_proj.shape[0], -1, HEAD_SIZE), positions
    ).astype(jnp.bfloat16)
    queries = queries.reshape(queries.shape[0], -1)
    first = after(first, queries, recent)
    lanes.append(pack_first(layout, table, perm, me, 2, first, pool))
    arrived.append(hop(lanes[2]))

    counts = after(counts, lanes[-1][0], *arrived[0])
    send, receive, rounds = plan(layout, False, table, perm, me, counts)
    lane, out, held = relay_begin(
        layout, table, perm, me, OWN_ROUNDS, send, receive, pool, arrived[0] + arrived[1]
    )
    arrived.append(hop(lane))

    def advance(step, parity, landed, out, held):
        return relay(
            layout, parity, table, perm, me, number(step), send, receive, pool, recent, zeros,
            landed, out, held,
        )

    state = None
    contexts = []
    for step in range(OWN_ROUNDS + 1, FIXED_ROUNDS):
        slot, part = divmod(step - OWN_ROUNDS - 1, PARTS)
        lane, out, held, state = relay_part(
            layout, slot, part, table, perm, me, step, send, receive, lengths, tables, pool,
            recent, zeros, arrived[step - 2], out, held, queries, (new_keys, new_values), state,
        )
        arrived.append(hop(lane))
        if part == PARTS - 1:
            contexts.append(state[0])
    out = fill_local(layout, table, perm, me, pool, recent, zeros, out)
    context = after(jnp.concatenate(contexts, axis=0), out, *arrived[-2])
    partial_value = jnp.dot(context, wo, preferred_element_type=jnp.float32)
    attn_out = lax.psum_scatter(
        partial_value.astype(jnp.bfloat16), "tp", scatter_dimension=1, tiled=True
    )

    newest = arrived[-1]
    newest = (after(newest[0], partial_value),) + newest[1:]

    def turn(state):
        step, older, newer, out, held = state
        lane, out, held = advance(step, 0, older, out, held)
        older = hop(lane)
        lane, out, held = advance(step + 1, 1, newer, out, held)
        return step + 2, older, hop(lane), out, held

    step, older, newer, out, _ = lax.while_loop(
        lambda state: state[0] < rounds[0],
        turn,
        (jnp.int32(FIXED_ROUNDS), arrived[-2], newest, out, held),
    )
    decode_pages = land_last(
        layout, table, perm, me, number(step), receive, older + newer, out
    )
    return (attn_out, decode_pages.reshape((1, peers, block) + pool.shape[1:]))


def shards(hidden, norm_gain, wq, wkv, wo, perm, prior_len, page_table, pool, send_table):
    slots = prior_len.shape[0]
    tokens = hidden.shape[0] // slots
    _, peers, block = send_table.shape
    layout = Layout(slots, page_table.shape[1], peers, block)
    features = pool.shape[-1]
    device = lax.axis_index("req")
    me = device.astype(jnp.int32).reshape(1)
    mine = jnp.concatenate([prior_len, page_table.reshape(-1), send_table.reshape(-1)])
    mine = jnp.pad(mine, (0, layout.width - layout.used)).reshape(-1, 128)
    by_device = exchange(peers, mine)
    table = by_device.reshape(-1)
    by_device = by_device.reshape(peers, layout.width)
    outgoing = pack_pages(layout, table, perm, me, pool)
    arrived = lax.all_to_all(outgoing, "req", split_axis=0, concat_axis=0, tiled=True)

    full_rows = lax.all_gather(hidden, "tp", axis=1, tiled=True)
    late_pool, wkv, outgoing = lax.optimization_barrier((pool, wkv, outgoing))
    requests = lax.dynamic_slice_in_dim(perm, device * slots, slots)
    lengths = by_device[:, :slots].reshape(-1)[requests]
    tables = by_device[:, slots : layout.sends].reshape(-1, layout.row_pages)[requests]

    normalized_input = normalize(full_rows, norm_gain)
    query_proj = jnp.dot(normalized_input, wq, preferred_element_type=jnp.float32)
    pair_proj = jnp.dot(
        normalized_input, wkv.reshape(wkv.shape[0], -1), preferred_element_type=jnp.float32
    )
    positions = (lengths[:, None] + jnp.arange(tokens, dtype=jnp.int32)[None, :]).reshape(-1)
    queries = rotate(query_proj.reshape(query_proj.shape[0], -1, HEAD_SIZE), positions).astype(
        jnp.bfloat16
    )
    pair_heads = pair_proj.reshape(pair_proj.shape[0], 2, -1, HEAD_SIZE)
    new_keys = rotate(pair_heads[:, 0], positions).astype(jnp.bfloat16).reshape(-1, features)
    new_values = pair_heads[:, 1].astype(jnp.bfloat16).reshape(-1, features)
    recent = jnp.stack([new_keys, new_values], axis=1).reshape(slots, tokens, 2, features)
    context = attend(
        lengths,
        tables,
        queries.reshape(queries.shape[0], -1),
        new_keys,
        new_values,
        late_pool[:, :, 0],
        late_pool[:, :, 1],
    )
    partial_value = jnp.dot(context, wo, preferred_element_type=jnp.float32)
    recent, partial_value = lax.optimization_barrier((recent, partial_value))
    attn_out = lax.psum_scatter(
        partial_value.astype(jnp.bfloat16), "tp", scatter_dimension=1, tiled=True
    )
    zeros = jnp.zeros(pool.shape[1:], pool.dtype)
    late_arrived = lax.all_to_all(
        pack_pages(layout, table, perm, me, late_pool, recent, zeros),
        "req",
        split_axis=0,
        concat_axis=0,
        tiled=True,
    )
    early_pages, numbers = place_early_pages(layout, table, perm, me, arrived, zeros)
    decode_pages = place_late_pages(numbers, late_arrived, early_pages)
    return (attn_out, decode_pages.reshape((1, peers, block) + pool.shape[1:]))


def solution(mesh):
    placed = (
        P("req", "tp"),
        P(),
        P(None, "tp"),
        P(None, None, "tp"),
        P("tp", None),
        P(),
        P("req"),
        P("req", None),
        P("req", None, None, "tp"),
        P("req", None, None),
    )
    return jax.shard_map(
        grid_shards if mesh.shape["req"] == 8 else shards,
        mesh=mesh,
        in_specs=placed,
        out_specs=(P("req", "tp"), P("req", None, None, None, None, "tp")),
        check_vma=False,
    )
```

```python
import math

import jax
import jax.numpy as jnp
from jax import lax
from jax.experimental import pallas as pl
from jax.experimental.pallas import tpu as pltpu
from jax.sharding import PartitionSpec as P

HEAD_SIZE = 128
NORM_EPSILON = 1e-05
ROPE_THETA = 100000000.0
BLOCK_PAGES = 4


def normalize(rows, gain):
    wide_rows = rows.astype(jnp.float32)
    mean_square = jnp.mean(wide_rows * wide_rows, axis=-1, keepdims=True)
    return (wide_rows * lax.rsqrt(mean_square + NORM_EPSILON) * gain.astype(jnp.float32)).astype(
        jnp.bfloat16
    )


def rotate(vectors, positions):
    half_size = vectors.shape[-1] // 2
    frequency = jnp.power(
        jnp.float32(ROPE_THETA), -2.0 * jnp.arange(half_size, dtype=jnp.float32) / vectors.shape[-1]
    )
    angles = positions.astype(jnp.float32)[:, None] * frequency[None, :]
    cosine = jnp.cos(angles)[:, None, :]
    sine_part = jnp.sin(angles)[:, None, :]
    first_half = vectors[..., :half_size]
    second_half = vectors[..., half_size:]
    return jnp.concatenate(
        [
            first_half * cosine - second_half * sine_part,
            second_half * cosine + first_half * sine_part,
        ],
        axis=-1,
    )


class Layout:
    def __init__(self, slots, row_pages, peers, block):
        self.slots, self.row_pages, self.peers, self.block = slots, row_pages, peers, block
        self.code_width = row_pages + 1
        self.sends = slots + slots * row_pages
        self.used = self.sends + peers * block
        self.width = -(-self.used // 1024) * 1024
        self.late = 2 * slots
        self.early = block - self.late

    def request(self, perm, device, slot):
        request = perm[device * self.slots + slot]
        return lax.div(request, self.slots) * self.width, lax.rem(request, self.slots)

    def length(self, table, perm, device, slot):
        base, row = self.request(perm, device, slot)
        return table[base + row]

    def physical(self, table, perm, device, slot, page):
        base, row = self.request(perm, device, slot)
        return table[base + self.slots + row * self.row_pages + jnp.minimum(page, self.row_pages - 1)]

    def split(self, code):
        return lax.div(code, self.code_width), lax.rem(code, self.code_width)

    def visit(self, table, perm, source, target, page_len, use):
        whole = [
            lax.div(self.length(table, perm, source, slot), page_len) for slot in range(self.slots)
        ]
        base = source * self.width + self.sends + target * self.block
        plain, tails = jnp.int32(0), jnp.int32(self.block - 1)
        for number in range(self.block):
            code = table[base + number]
            first = whole[0]
            for slot in range(1, self.slots):
                low = slot * self.code_width
                first = jnp.where(code >= low, whole[slot] + low, first)
            valid, tail = code >= 0, code >= first
            place = jnp.where(valid, jnp.where(tail, tails, plain), -1)
            use(number, code, place)
            plain = plain + jnp.where(valid & jnp.logical_not(tail), 1, 0)
            tails = tails - jnp.where(tail, 1, 0)


def exchange_kernel(peers, mine, out, send_sems, recv_sems):
    me = lax.axis_index("req")
    barrier = pltpu.get_barrier_semaphore()
    for hop in range(1, peers):
        pl.semaphore_signal(
            barrier,
            inc=1,
            device_id={"req": lax.rem(me + hop, peers)},
            device_id_type=pl.DeviceIdType.MESH,
        )
    pl.semaphore_wait(barrier, peers - 1)
    copies = []
    for hop in range(1, peers):
        copy = pltpu.make_async_remote_copy(
            src_ref=mine,
            dst_ref=out.at[me],
            send_sem=send_sems.at[hop - 1],
            recv_sem=recv_sems.at[hop - 1],
            device_id={"req": lax.rem(me + hop, peers)},
            device_id_type=pl.DeviceIdType.MESH,
        )
        copy.start()
        copies.append(copy)
    out[me] = mine[...]
    for copy in copies:
        copy.wait()


def exchange(peers, mine):
    return pl.pallas_call(
        lambda *refs: exchange_kernel(peers, *refs),
        out_shape=jax.ShapeDtypeStruct((peers,) + mine.shape, mine.dtype),
        in_specs=[pl.BlockSpec(memory_space=pltpu.VMEM)],
        out_specs=pl.BlockSpec(memory_space=pltpu.VMEM),
        scratch_shapes=[
            pltpu.SemaphoreType.DMA((peers - 1,)),
            pltpu.SemaphoreType.DMA((peers - 1,)),
        ],
        compiler_params=pltpu.CompilerParams(collective_id=0, has_side_effects=True),
        name="exchange",
    )(mine)


BUFFERS = 32
AHEAD = 16


def ring(count, load, store, drain):
    def step(index, carry):
        @pl.when(index < count)
        def _():
            @pl.when(index >= BUFFERS)
            def _():
                drain(index - BUFFERS)

            load(index)

        @pl.when(index >= AHEAD)
        def _():
            store(index - AHEAD)

        return carry

    lax.fori_loop(0, count + AHEAD, step, 0)

    def last(index, carry):
        drain(index)
        return carry

    lax.fori_loop(max(count - BUFFERS, 0), count, last, 0)


def copy_rows(source, source_row, target, target_row, count, sem):
    size = target.shape[0]
    while size:
        offset = lax.div(count, 2 * size) * (2 * size)

        @pl.when(lax.rem(lax.div(count, size), 2) == 1)
        def _(size=size, offset=offset):
            pltpu.make_async_copy(
                source.at[pl.ds(source_row + offset, size)],
                target.at[pl.ds(target_row + offset, size)],
                sem,
            ).start()

        size //= 2


def pack_kernel(layout, late, table, perm, me, pool, *rest):
    if late:
        recent, zeros, out, codes, buffers, in_sems, out_sems = rest
    else:
        out, codes, buffers, in_sems, out_sems = rest
    page_len = buffers.shape[1]
    span = layout.late if late else layout.early
    start = layout.early if late else 0
    count = layout.peers * span

    def clear(index, carry):
        codes[index] = 0
        return carry

    lax.fori_loop(0, count, clear, 0)
    starts = []
    for slot in range(layout.slots):
        base, row = layout.request(perm, me[0], slot)
        starts.append(
            base + layout.slots + row * layout.row_pages - slot * layout.code_width
        )

    def block(target, carry):
        def use(number, code, place):
            inside = (place >= start) & (place < start + span)
            item = code
            if not late:
                origin = starts[0]
                for slot in range(1, layout.slots):
                    origin = jnp.where(code >= slot * layout.code_width, starts[slot], origin)
                item = table[jnp.where(inside, origin + code, 0)]

            @pl.when(inside)
            def _():
                codes[target * span + place - start] = item

        layout.visit(table, perm, me[0], target, page_len, use)
        return carry

    lax.fori_loop(0, layout.peers, block, 0)

    def load(index):
        spot = index & (BUFFERS - 1)
        target, sem = buffers.at[spot], in_sems.at[spot]
        if not late:
            pltpu.make_async_copy(pool.at[codes[index]], target, sem).start()
            return
        slot, page = layout.split(codes[index])
        cached = pool.at[layout.physical(table, perm, me[0], slot, page)]
        length = layout.length(table, perm, me[0], slot)
        full, kept = lax.div(length, page_len), lax.rem(length, page_len)

        @pl.when(page < full)
        def _():
            pltpu.make_async_copy(cached, target, sem).start()

        @pl.when(page == full)
        def _():
            copy_rows(cached, 0, target, 0, kept, sem)
            copy_rows(recent.at[slot], 0, target, kept, page_len - kept, sem)

        @pl.when(page > full)
        def _():
            copy_rows(recent.at[slot], page_len - kept, target, 0, kept, sem)
            copy_rows(zeros, 0, target, kept, page_len - kept, sem)

    def outward(index):
        spot = index & (BUFFERS - 1)
        return pltpu.make_async_copy(buffers.at[spot], out.at[index], out_sems.at[spot])

    def store(index):
        spot = index & (BUFFERS - 1)
        pltpu.make_async_copy(pool.at[0], buffers.at[spot], in_sems.at[spot]).wait()
        outward(index).start()

    ring(count, load, store, lambda index: outward(index).wait())


def scratch(layout, pool):
    return [
        pltpu.SMEM((layout.peers * layout.block,), jnp.int32),
        pltpu.VMEM((BUFFERS,) + pool.shape[-3:], pool.dtype),
        pltpu.SemaphoreType.DMA((BUFFERS,)),
        pltpu.SemaphoreType.DMA((BUFFERS,)),
    ]


def pack_pages(layout, table, perm, me, pool, *fresh):
    late = bool(fresh)
    span = layout.late if late else layout.early
    return pl.pallas_call(
        lambda *refs: pack_kernel(layout, late, *refs),
        out_shape=jax.ShapeDtypeStruct((layout.peers * span,) + pool.shape[1:], pool.dtype),
        grid_spec=pltpu.PrefetchScalarGridSpec(
            num_scalar_prefetch=3,
            grid=(1,),
            in_specs=[pl.BlockSpec(memory_space=pl.ANY)] * (1 + len(fresh)),
            out_specs=pl.BlockSpec(memory_space=pl.ANY),
            scratch_shapes=scratch(layout, pool),
        ),
        name="pack_late" if late else "pack_early",
    )(table, perm, me, pool, *fresh).reshape((layout.peers, span) + pool.shape[1:])


def place_kernel(layout, table, perm, me, arrived, zeros, *rest):
    out, numbers, places, buffers, in_sems, out_sems, blank, blank_sem = rest
    page_len = buffers.shape[1]

    def clear(index, carry):
        numbers[index] = -1
        return carry

    lax.fori_loop(0, layout.peers * layout.late, clear, 0)
    fill = pltpu.make_async_copy(zeros, blank, blank_sem)
    fill.start()

    def block(source, carry):
        def use(number, code, place):
            places[source * layout.block + number] = place

            @pl.when(place >= layout.early)
            def _():
                late_index = source * layout.late + place - layout.early
                numbers[late_index] = source * layout.block + number

        layout.visit(table, perm, source, me[0], page_len, use)
        return carry

    lax.fori_loop(0, layout.peers, block, 0)
    fill.wait()

    def inward(index):
        spot = index & (BUFFERS - 1)
        place = jnp.clip(places[index], 0, layout.early - 1)
        return pltpu.make_async_copy(
            arrived.at[lax.div(index, layout.block), place], buffers.at[spot], in_sems.at[spot]
        )

    def outward(index, held):
        return pltpu.make_async_copy(held, out.at[index], out_sems.at[index & (BUFFERS - 1)])

    def is_early(index):
        return (places[index] >= 0) & (places[index] < layout.early)

    def load(index):
        @pl.when(is_early(index))
        def _():
            inward(index).start()

    def store(index):
        @pl.when(is_early(index))
        def _():
            inward(index).wait()
            outward(index, buffers.at[index & (BUFFERS - 1)]).start()

        @pl.when(places[index] < 0)
        def _():
            outward(index, blank).start()

    def drain(index):
        @pl.when(places[index] < layout.early)
        def _():
            outward(index, blank).wait()

    ring(layout.peers * layout.block, load, store, drain)


def place_late_kernel(count, numbers, arrived, held, out, buffers, in_sems, out_sems):
    def inward(index):
        spot = index & (BUFFERS - 1)
        return pltpu.make_async_copy(arrived.at[index], buffers.at[spot], in_sems.at[spot])

    def outward(index):
        spot = index & (BUFFERS - 1)
        target = out.at[jnp.maximum(numbers[index], 0)]
        return pltpu.make_async_copy(buffers.at[spot], target, out_sems.at[spot])

    def load(index):
        @pl.when(numbers[index] >= 0)
        def _():
            inward(index).start()

    def store(index):
        @pl.when(numbers[index] >= 0)
        def _():
            inward(index).wait()
            outward(index).start()

    def drain(index):
        @pl.when(numbers[index] >= 0)
        def _():
            outward(index).wait()

    ring(count, load, store, drain)


def place_early_pages(layout, table, perm, me, arrived, zeros):
    page = arrived.shape[2:]
    return pl.pallas_call(
        lambda *refs: place_kernel(layout, *refs),
        out_shape=(
            jax.ShapeDtypeStruct((layout.peers * layout.block,) + page, arrived.dtype),
            jax.ShapeDtypeStruct((layout.peers * layout.late,), jnp.int32),
        ),
        grid_spec=pltpu.PrefetchScalarGridSpec(
            num_scalar_prefetch=3,
            grid=(1,),
            in_specs=[pl.BlockSpec(memory_space=pl.ANY)] * 2,
            out_specs=(
                pl.BlockSpec(memory_space=pl.ANY),
                pl.BlockSpec(memory_space=pltpu.SMEM),
            ),
            scratch_shapes=scratch(layout, arrived)
            + [pltpu.VMEM(page, arrived.dtype), pltpu.SemaphoreType.DMA],
        ),
        name="place_early",
    )(table, perm, me, arrived, zeros)


def place_late_pages(numbers, arrived, held):
    arrived = arrived.reshape((-1,) + held.shape[1:])
    return pl.pallas_call(
        lambda *refs: place_late_kernel(arrived.shape[0], *refs),
        out_shape=jax.ShapeDtypeStruct(held.shape, held.dtype),
        grid_spec=pltpu.PrefetchScalarGridSpec(
            num_scalar_prefetch=1,
            grid=(1,),
            in_specs=[pl.BlockSpec(memory_space=pl.ANY)] * 2,
            out_specs=pl.BlockSpec(memory_space=pl.ANY),
            scratch_shapes=[
                pltpu.VMEM((BUFFERS,) + held.shape[1:], held.dtype),
                pltpu.SemaphoreType.DMA((BUFFERS,)),
                pltpu.SemaphoreType.DMA((BUFFERS,)),
            ],
        ),
        input_output_aliases={2: 0},
        name="place_late",
    )(numbers, arrived, held)


def attend_kernel(lengths, tables, q_ref, nk_ref, nv_ref, *rest):
    k_refs, v_refs = rest[:BLOCK_PAGES], rest[BLOCK_PAGES : 2 * BLOCK_PAGES]
    out_ref, q_rows, top, total, acc = rest[2 * BLOCK_PAGES :]
    kv_heads, rows, head = q_rows.shape
    tokens = q_ref.shape[0]
    groups = rows // tokens
    slot, step = pl.program_id(0), pl.program_id(1)
    page_len = k_refs[0].shape[1]
    block_keys = BLOCK_PAGES * page_len
    length = lengths[slot]
    inv_scale = 1.0 / math.sqrt(head)

    def score(kv, keys):
        return (
            lax.dot_general(
                q_rows[kv], keys, (((1,), (1,)), ((), ())), preferred_element_type=jnp.float32
            )
            * inv_scale
        )

    @pl.when(step == 0)
    def _():
        for kv in range(kv_heads):
            columns = slice(kv * head, (kv + 1) * head)
            for group in range(groups):
                lane = (kv * groups + group) * head
                q_rows[kv, group * tokens : (group + 1) * tokens, :] = q_ref[:, lane : lane + head]
            scores = score(kv, nk_ref[:, columns])
            query_id = lax.broadcasted_iota(jnp.int32, scores.shape, 0) % tokens
            key_id = lax.broadcasted_iota(jnp.int32, scores.shape, 1)
            scores = jnp.where(key_id <= query_id, scores, -1e30)
            highest = jnp.max(scores, axis=-1, keepdims=True)
            weights = jnp.exp(scores - highest)
            top[kv] = jnp.broadcast_to(highest, (rows, head))
            total[kv] = jnp.broadcast_to(jnp.sum(weights, axis=-1, keepdims=True), (rows, head))
            acc[kv] = jnp.dot(
                weights.astype(jnp.bfloat16), nv_ref[:, columns], preferred_element_type=jnp.float32
            )

    @pl.when(step * block_keys < length)
    def _():
        for kv in range(kv_heads):
            columns = slice(kv * head, (kv + 1) * head)
            keys = jnp.concatenate([ref[0, :, columns] for ref in k_refs], axis=0)
            values = jnp.concatenate([ref[0, :, columns] for ref in v_refs], axis=0)
            scores = score(kv, keys)
            key_id = lax.broadcasted_iota(jnp.int32, scores.shape, 1)
            scores = jnp.where(key_id < length - step * block_keys, scores, -1e30)
            before = top[kv]
            highest = jnp.maximum(before, jnp.max(scores, axis=-1, keepdims=True))
            factor = jnp.exp(before - highest)
            weights = jnp.exp(scores - highest[:, :1])
            top[kv] = highest
            total[kv] = total[kv] * factor + jnp.sum(weights, axis=-1, keepdims=True)
            acc[kv] = acc[kv] * factor + jnp.dot(
                weights.astype(jnp.bfloat16), values, preferred_element_type=jnp.float32
            )

    @pl.when(step == pl.num_programs(1) - 1)
    def _():
        for kv in range(kv_heads):
            context = (acc[kv] / total[kv]).astype(jnp.bfloat16)
            for group in range(groups):
                lane = (kv * groups + group) * head
                out_ref[:, lane : lane + head] = context[group * tokens : (group + 1) * tokens]


def attend(lengths, tables, queries, new_keys, new_values, k_pool, v_pool):
    slots, row_pages = tables.shape
    tokens = queries.shape[0] // slots
    page_len, features = k_pool.shape[1:]
    kv_heads = features // HEAD_SIZE
    rows = tokens * (queries.shape[1] // features)
    steps = row_pages // BLOCK_PAGES

    def page_spec(number):
        def pick(slot, step, lengths, tables):
            last = (lengths[slot] + page_len - 1) // page_len - 1
            return (tables[slot * row_pages + jnp.minimum(step * BLOCK_PAGES + number, last)], 0, 0)

        return pl.BlockSpec((1, page_len, features), pick)

    def slot_rows(slot, step, lengths, tables):
        return (slot, 0)

    pages = [page_spec(number) for number in range(BLOCK_PAGES)]
    state = pltpu.VMEM((kv_heads, rows, HEAD_SIZE), jnp.float32)
    return pl.pallas_call(
        attend_kernel,
        out_shape=jax.ShapeDtypeStruct(queries.shape, jnp.bfloat16),
        grid_spec=pltpu.PrefetchScalarGridSpec(
            num_scalar_prefetch=2,
            grid=(slots, steps),
            in_specs=[
                pl.BlockSpec((tokens, queries.shape[1]), slot_rows),
                pl.BlockSpec((tokens, features), slot_rows),
                pl.BlockSpec((tokens, features), slot_rows),
            ]
            + pages
            + pages,
            out_specs=pl.BlockSpec((tokens, queries.shape[1]), slot_rows),
            scratch_shapes=[
                pltpu.VMEM((kv_heads, rows, HEAD_SIZE), jnp.bfloat16),
                state,
                state,
                state,
            ],
        ),
        compiler_params=pltpu.CompilerParams(
            dimension_semantics=("arbitrary", "arbitrary"), vmem_limit_bytes=40 << 20
        ),
        name="attend",
    )(
        lengths,
        tables.reshape(-1),
        queries,
        new_keys,
        new_values,
        *([k_pool] * BLOCK_PAGES),
        *([v_pool] * BLOCK_PAGES),
    )


LINKS = 3
LANE = 8
WIDE = 8
OWN_ROUNDS = 3
LATE_ROUND = 4
FIXED_ROUNDS = 12
SIDES = 3
ROUND_LIMIT = 56
SLOT_LIMIT = ROUND_LIMIT * LANE
TABLE = 2 * SLOT_LIMIT + ROUND_LIMIT * WIDE
WIDTHS = (LANE, LANE, WIDE)
OFFSETS = (0, LANE, 2 * LANE)
QUEUE = 96
ARRIVALS = 512
HELD = 1024
HELD_PAGES = 384


def neighbours():
    right = [(device, device + 2) for device in range(6)]
    left = [(device + 2, device) for device in range(6)]
    across = [(device, device ^ 1) for device in range(8)]
    return right, left, across


def loop(low, high, body):
    def step(index, carry):
        body(index)
        return carry

    lax.fori_loop(low, high, step, 0)


def plan_kernel(layout, first, table, perm, me, counts, send, *rest):
    if first:
        own_codes, early_first, runs, places, heads, tails, waiting, progress = rest
    else:
        receive, rounds = rest[:2]
        own_codes, early_first, runs, places, heads, tails, waiting, progress = rest[2:10]
        numbers, held, arrived_device, arrived_run, arrived_place, arrived_count = rest[10:]
    peers, block = layout.peers, layout.block
    own = me[0]
    page_len = layout.page_len

    def total(pair):
        return counts[pair]

    def early(pair):
        return counts[peers * peers + pair]

    def scan(source, target, use):
        whole = [
            lax.div(layout.length(table, perm, source, slot), page_len)
            for slot in range(layout.slots)
        ]
        base = source * layout.width + layout.sends + target * block
        plain, tail_rank = jnp.int32(0), early(source * peers + target)
        for number in range(block):
            code = table[base + number]
            edge = whole[0]
            for slot in range(1, layout.slots):
                low = slot * layout.code_width
                edge = jnp.where(code >= low, whole[slot] + low, edge)
            valid, tail = code >= 0, code >= edge
            use(number, code, valid, jnp.where(tail, tail_rank, plain))
            plain = plain + jnp.where(valid & jnp.logical_not(tail), 1, 0)
            tail_rank = tail_rank + jnp.where(tail, 1, 0)

    def list_own(target):
        def use(number, code, valid, rank):
            @pl.when(valid)
            def _():
                own_codes[target * block + rank] = code

        scan(own, target, use)

    loop(0, peers, list_own)
    if not first:

        def list_numbers(source):
            def use(number, code, valid, rank):
                @pl.when(valid)
                def _():
                    numbers[source * block + rank] = source * block + number

            scan(source, own, use)

        loop(0, peers, list_numbers)

    def clear(index):
        early_first[index] = 0

    loop(0, peers * peers, clear)
    half = peers // 2
    for direction in range(2):
        sources = range(direction * half, (direction + 1) * half)
        targets = range((1 - direction) * half, (2 - direction) * half)
        loads = []
        for column in range(2):
            load = jnp.int32(0)
            for source in sources:
                if source % 2 == column:
                    for target in targets:
                        load = load + total(source * peers + target)
            loads.append(load)
        heavy = jnp.where(loads[1] > loads[0], 1, 0)
        left = lax.div(jnp.abs(loads[0] - loads[1]), 2)
        zs = sorted({source // 2 for source in sources})
        zt = sorted({target // 2 for target in targets})
        for _, a, b in sorted((abs(a - b), a, b) for a in zs for b in zt):
            pair = (2 * a + heavy) * peers + 2 * b + 1 - heavy
            moved = jnp.minimum(left, early(pair))
            early_first[pair] = moved
            left = left - moved

    def clear_queue(index):
        heads[index] = 0
        tails[index] = 0

    loop(0, peers * LINKS * 4, clear_queue)

    def clear_waiting(index):
        waiting[index] = 0

    loop(0, peers * LINKS, clear_waiting)
    progress[0] = 0

    def push(device, run, place, turn):
        target = (run >> 10) & 7
        steps = (target >> 1) - (device >> 1)
        flip = (target ^ device) & 1
        across = (steps == 0) | turn
        link = jnp.where(across, 2, jnp.where(steps > 0, 0, 1))
        lane = device * LINKS + link
        waiting[lane] = waiting[lane] + 1
        queue = lane * 4 + jnp.abs(steps) + flip - 1
        spot = tails[queue]
        runs[queue * QUEUE + spot] = run
        places[queue * QUEUE + spot] = place
        tails[queue] = spot + 1

    def make_run(pair, start, count):
        return (pair << 10) | (start << 5) | count

    def open_pair(pair):
        source = pair >> 3
        moved = early_first[pair]
        count = early(pair)
        wanted = source != (pair & 7)
        if first:
            wanted = wanted & (source == own)

        @pl.when(wanted & (moved > 0))
        def _():
            push(source, make_run(pair, 0, moved), -1, True)

        @pl.when(wanted & (count > moved))
        def _():
            push(source, make_run(pair, moved, count - moved), -1, False)

    loop(0, peers * peers, open_pair)

    def open_late(pair):
        source = pair >> 3
        count = total(pair) - early(pair)

        @pl.when((source != (pair & 7)) & (count > 0))
        def _():
            push(source, make_run(pair, early(pair), count), -1, False)

    def move(step, device, link, width, toward):
        lane = device * LINKS + link

        @pl.when(waiting[lane] > 0)
        def _():
            drain(step, lane, device, link, width, toward)

    def drain(step, lane, device, link, width, toward):
        room = jnp.int32(width)
        origin = link * SLOT_LIMIT + step * width + width
        side = lax.rem(step, SIDES)
        for rank in (3, 2, 1, 0):
            queue = lane * 4 + rank

            def more(state):
                room, head, tail = state
                return (room > 0) & (head < tail)

            def take(state):
                room, head, tail = state
                spot = queue * QUEUE + head
                run, place = runs[spot], places[spot]
                pair, start, count = run >> 10, (run >> 5) & 31, run & 31
                taken = jnp.minimum(room, count)
                base = origin - room
                final = (pair & 7) == toward

                def note_sent():
                    def note(index):
                        code = own_codes[(pair & 7) * block + start + index]
                        send[base + index] = jnp.where(place < 0, code, HELD + place + index)

                    loop(0, taken, note)

                whole = taken == count
                waiting[lane] = waiting[lane] - jnp.where(whole, 1, 0)
                runs[spot] = make_run(pair, start + taken, count - taken)
                places[spot] = jnp.where(place < 0, place, place + taken)
                if first:
                    note_sent()
                else:
                    slot = held[toward]
                    passing = jnp.where(final, 0, taken)
                    progress[0] = progress[0] + taken - passing
                    held[toward] = slot + passing
                    added = arrived_count[side]
                    at = side * ARRIVALS + added
                    arrived_device[at] = toward
                    arrived_run[at] = make_run(pair, start, taken)
                    arrived_place[at] = slot
                    arrived_count[side] = added + jnp.where(final, 0, 1)

                    @pl.when((device == own) | (toward == own))
                    def _():
                        @pl.when(device == own)
                        def _():
                            note_sent()

                        @pl.when(toward == own)
                        def _():
                            def note(index):
                                number = numbers[(pair >> 3) * block + start + index]
                                receive[base + index] = jnp.where(
                                    final, number, HELD + slot + index
                                )

                            loop(0, taken, note)

                return room - taken, head + jnp.where(whole, 1, 0), tail

            room, head, _ = lax.while_loop(more, take, (room, heads[queue], tails[queue]))
            heads[queue] = head

    def blank(step):
        def one(index):
            for link in (0, 1):
                spot = link * SLOT_LIMIT + step * LANE + index
                send[spot] = -1
                if not first:
                    receive[spot] = -1

        def wide(index):
            spot = 2 * SLOT_LIMIT + step * WIDE + index
            send[spot] = -1
            if not first:
                receive[spot] = -1

        loop(0, LANE, one)
        loop(0, WIDE, wide)

    if first:
        for step in range(OWN_ROUNDS):
            blank(step)
            move(step, own, 0, LANE, own + 2)
            move(step, own, 1, LANE, own - 2)
            move(step, own, 2, WIDE, own ^ 1)
        return

    wanted = jnp.int32(0)
    for source in range(peers):
        held[source] = 0
        for target in range(peers):
            if source != target:
                wanted = wanted + total(source * peers + target)
    for side in range(SIDES):
        arrived_count[side] = 0

    def unfinished(step):
        return (step <= FIXED_ROUNDS) | (progress[0] < wanted)

    def advance(step):
        blank(step)

        @pl.when(step == LATE_ROUND)
        def _():
            loop(0, peers * peers, open_late)

        def arrive_all(side):
            def arrive(index):
                at = side * ARRIVALS + index
                push(arrived_device[at], arrived_run[at], arrived_place[at], False)

            loop(0, arrived_count[side], arrive)
            arrived_count[side] = 0

        @pl.when(step == OWN_ROUNDS)
        def _():
            for past in range(OWN_ROUNDS - 2):
                arrive_all(past)

        @pl.when(step >= OWN_ROUNDS)
        def _():
            arrive_all(lax.rem(step + 1, SIDES))

        def one(device):
            move(step, device, 0, LANE, device + 2)
            move(step, device, 1, LANE, device - 2)
            move(step, device, 2, WIDE, device ^ 1)

        loop(0, peers, one)

        @pl.when(progress[0] >= wanted)
        def _():
            rounds[0] = jnp.minimum(rounds[0], step + 1)

        return step + 1

    rounds[0] = jnp.int32(ROUND_LIMIT)
    rounds[1] = jnp.int32(0)
    end = lax.while_loop(unfinished, advance, jnp.int32(0))
    blank(end)


def plan(layout, first, table, perm, me, counts):
    tables = jax.ShapeDtypeStruct((TABLE,), jnp.int32)
    outs = (tables,) if first else (tables, tables, jax.ShapeDtypeStruct((2,), jnp.int32))
    peers = layout.peers

    def words(count):
        return pltpu.SMEM((count,), jnp.int32)

    queues = peers * LINKS * 4
    room = [
        words(peers * layout.block),
        words(peers * peers),
        words(queues * QUEUE),
        words(queues * QUEUE),
        words(queues),
        words(queues),
        words(peers * LINKS),
        words(1),
    ]
    if not first:
        room += [words(peers * layout.block), words(peers)]
        room += [words(SIDES * ARRIVALS)] * 3 + [words(SIDES)]
    out = pl.pallas_call(
        lambda *refs: plan_kernel(layout, first, *refs),
        out_shape=outs,
        grid_spec=pltpu.PrefetchScalarGridSpec(
            num_scalar_prefetch=4,
            grid=(1,),
            in_specs=[],
            out_specs=tuple(pl.BlockSpec(memory_space=pltpu.SMEM) for _ in outs),
            scratch_shapes=room,
        ),
        name="plan_first" if first else "plan_rest",
    )(table, perm, me, counts)
    return out[0] if first else out


def own_page(layout, table, perm, me, pool, recent, zeros, code, target, sem):
    slot, page = layout.split(code)
    cached = pool.at[layout.physical(table, perm, me[0], slot, page)]
    if recent is None:
        pltpu.make_async_copy(cached, target, sem).start()
        return
    page_len = layout.page_len
    length = layout.length(table, perm, me[0], slot)
    full, kept = lax.div(length, page_len), lax.rem(length, page_len)

    @pl.when(page < full)
    def _():
        pltpu.make_async_copy(cached, target, sem).start()

    @pl.when(page == full)
    def _():
        copy_rows(cached, 0, target, 0, kept, sem)
        copy_rows(recent.at[slot], 0, target, kept, page_len - kept, sem)

    @pl.when(page > full)
    def _():
        copy_rows(recent.at[slot], page_len - kept, target, 0, kept, sem)
        copy_rows(zeros, 0, target, kept, page_len - kept, sem)


def links_of(step):
    return (0, 1, 2)


def step_kernel(layout, kind, parity, table, perm, me, step, send, *rest):
    recent = zeros = None
    count = len(links_of(parity))
    if kind == "first":
        pool, *lanes, sent, load_sems, store_sems = rest
        groups = []
    elif kind == "begin":
        receive, pool = rest[:2]
        arrived = rest[2:8]
        out, held, *lanes = rest[8 : 10 + count]
        sent, load_sems, store_sems, came, land_sems, leave_sems = rest[10 + count :]
        groups = [3, 2]
    elif kind == "step":
        receive, pool, recent, zeros = rest[:4]
        arrived = rest[4 : 4 + count]
        rest = rest[6 + count :]
        out, held, *lanes = rest[: 2 + count]
        sent, load_sems, store_sems, came, land_sems, leave_sems = rest[2 + count :]
        groups = [2]
    else:
        receive = send
        arrived = rest[:6]
        out, came, land_sems, leave_sems = rest[7:]
        groups = [2, 1]
    relaying = kind in ("begin", "step")
    stages = [[] for _ in range(5)]
    first_ref = [0]
    for back in groups:
        first_ref.append(first_ref[-1] + len(links_of(parity - back)))

    def spots(body):
        for link in links_of(parity):
            loop(0, WIDTHS[link], lambda index, link=link: body(link, index))

    def every(body):
        for group, back in enumerate(groups):
            for link in links_of(parity - back):
                base = link * SLOT_LIMIT + (step[0] - back) * WIDTHS[link]

                def row(index, group=group, link=link, base=base):
                    body(group, link, index, receive[base + index])

                loop(0, WIDTHS[link], row)

    def outgoing(link, index):
        return send[link * SLOT_LIMIT + step[0] * WIDTHS[link] + index]

    def load(link, index, source):
        spot = OFFSETS[link] + index
        return pltpu.make_async_copy(source, sent.at[spot], load_sems.at[spot])

    def store(link, index):
        spot = OFFSETS[link] + index
        return pltpu.make_async_copy(
            sent.at[spot], lanes[link].at[index], store_sems.at[spot]
        )

    if groups:

        def landing(group, link, index):
            return pltpu.make_async_copy(
                arrived[first_ref[group] + link].at[index],
                came.at[group, OFFSETS[link] + index],
                land_sems.at[group, OFFSETS[link] + index],
            )

        def leaving(group, link, index, target):
            spot = OFFSETS[link] + index
            return pltpu.make_async_copy(
                came.at[group, spot], target, leave_sems.at[group, spot]
            )

        def land(group, link, index, to):
            @pl.when(to >= 0)
            def _():
                landing(group, link, index).start()

        stages[0].append(lambda: every(land))

    if kind != "last":

        def fetch(link, index):
            code = outgoing(link, index)

            @pl.when((code >= 0) & (code < HELD))
            def _():
                own_page(
                    layout, table, perm, me, pool, recent, zeros, code,
                    sent.at[OFFSETS[link] + index], load_sems.at[OFFSETS[link] + index],
                )

        stages[0].append(lambda: spots(fetch))

    if groups:

        def leave(group, link, index, to):
            @pl.when(to >= 0)
            def _():
                landing(group, link, index).wait()

            @pl.when((to >= 0) & (to < HELD))
            def _():
                leaving(group, link, index, out.at[to]).start()

            if relaying:

                @pl.when(to >= HELD)
                def _():
                    leaving(group, link, index, held.at[to - HELD]).start()

        stages[1].append(lambda: every(leave))

    if kind != "last":

        def pass_on(link, index):
            code = outgoing(link, index)

            @pl.when((code >= 0) & (code < HELD))
            def _():
                load(link, index, pool.at[0]).wait()
                store(link, index).start()

        stages[1].append(lambda: spots(pass_on))

    if groups:

        def left(group, link, index, to):
            @pl.when(to >= 0)
            def _():
                leaving(group, link, index, out.at[0]).wait()

        stages[2].append(lambda: every(left))

    if relaying:

        def reload(link, index):
            code = outgoing(link, index)

            @pl.when(code >= HELD)
            def _():
                load(link, index, held.at[code - HELD]).start()

        def relayed(link, index):
            code = outgoing(link, index)

            @pl.when(code >= HELD)
            def _():
                load(link, index, pool.at[0]).wait()
                store(link, index).start()

        stages[2].append(lambda: spots(reload))
        stages[3].append(lambda: spots(relayed))

    if kind != "last":

        def stored(link, index):
            @pl.when(outgoing(link, index) >= 0)
            def _():
                store(link, index).wait()

        stages[4].append(lambda: spots(stored))

    return stages


def run_stages(stages):
    for stage in stages:
        for work in stage:
            work()


def any_specs(count):
    return [pl.BlockSpec(memory_space=pltpu.HBM)] * count


def lane_shapes(pool, parity):
    return tuple(
        jax.ShapeDtypeStruct((WIDTHS[link],) + pool.shape[1:], pool.dtype)
        for link in links_of(parity)
    )


SPOTS = 2 * LANE + WIDE


def send_room(pool):
    return [
        pltpu.VMEM((SPOTS,) + pool.shape[1:], pool.dtype),
        pltpu.SemaphoreType.DMA((SPOTS,)),
        pltpu.SemaphoreType.DMA((SPOTS,)),
    ]


def land_room(pool, groups):
    return [
        pltpu.VMEM((groups, SPOTS) + pool.shape[1:], pool.dtype),
        pltpu.SemaphoreType.DMA((groups, SPOTS)),
        pltpu.SemaphoreType.DMA((groups, SPOTS)),
    ]


ROOMY = pltpu.CompilerParams(vmem_limit_bytes=40 << 20)


def pack_first(layout, table, perm, me, step, send, pool):
    parity = step % 2
    return pl.pallas_call(
        lambda *refs: run_stages(step_kernel(layout, "first", parity, *refs)),
        out_shape=lane_shapes(pool, parity),
        grid_spec=pltpu.PrefetchScalarGridSpec(
            num_scalar_prefetch=5,
            grid=(1,),
            in_specs=any_specs(1),
            out_specs=tuple(any_specs(len(links_of(parity)))),
            scratch_shapes=send_room(pool),
        ),
        compiler_params=ROOMY,
        name="pack_first",
    )(table, perm, me, number(step), send, pool)


def relay_begin(layout, table, perm, me, step, send, receive, pool, arrived):
    parity = step % 2
    page = pool.shape[1:]
    results = pl.pallas_call(
        lambda *refs: run_stages(step_kernel(layout, "begin", parity, *refs)),
        out_shape=(
            jax.ShapeDtypeStruct((layout.peers * layout.block,) + page, pool.dtype),
            jax.ShapeDtypeStruct((HELD_PAGES,) + page, pool.dtype),
        )
        + lane_shapes(pool, parity),
        grid_spec=pltpu.PrefetchScalarGridSpec(
            num_scalar_prefetch=6,
            grid=(1,),
            in_specs=any_specs(7),
            out_specs=tuple(any_specs(2 + len(links_of(parity)))),
            scratch_shapes=send_room(pool) + land_room(pool, 2),
        ),
        compiler_params=ROOMY,
        name="relay_begin",
    )(table, perm, me, number(step), send, receive, pool, *arrived)
    return results[2:], results[0], results[1]


def relay(
    layout, parity, table, perm, me, step, send, receive, pool, recent, zeros, arrived, out, held
):
    count = len(arrived)
    results = pl.pallas_call(
        lambda *refs: run_stages(step_kernel(layout, "step", parity, *refs)),
        out_shape=(
            jax.ShapeDtypeStruct(out.shape, out.dtype),
            jax.ShapeDtypeStruct(held.shape, held.dtype),
        )
        + lane_shapes(pool, parity),
        grid_spec=pltpu.PrefetchScalarGridSpec(
            num_scalar_prefetch=6,
            grid=(1,),
            in_specs=any_specs(5 + count),
            out_specs=tuple(any_specs(2 + count)),
            scratch_shapes=send_room(pool) + land_room(pool, 1),
        ),
        input_output_aliases={9 + count: 0, 10 + count: 1},
        compiler_params=ROOMY,
        name="relay",
    )(table, perm, me, step, send, receive, pool, recent, zeros, *arrived, out, held)
    return results[2:], results[0], results[1]


def land_last(layout, table, perm, me, step, receive, arrived, out):
    return pl.pallas_call(
        lambda *refs: run_stages(step_kernel(layout, "last", 0, *refs)),
        out_shape=jax.ShapeDtypeStruct(out.shape, out.dtype),
        grid_spec=pltpu.PrefetchScalarGridSpec(
            num_scalar_prefetch=5,
            grid=(1,),
            in_specs=any_specs(7),
            out_specs=pl.BlockSpec(memory_space=pl.ANY),
            scratch_shapes=land_room(out, 2),
        ),
        input_output_aliases={11: 0},
        compiler_params=ROOMY,
        name="land_last",
    )(table, perm, me, step, receive, *arrived, out)


def fill_kernel(
    layout, table, perm, me, pool, recent, zeros, before, out, blank, mine, sems, load_sems
):
    del before
    own, block = me[0], layout.block
    fill = pltpu.make_async_copy(zeros, blank, load_sems.at[block])
    fill.start()

    def code_of(source, number):
        return table[source * layout.width + layout.sends + own * block + number]

    def outward(source, number, held_page):
        return pltpu.make_async_copy(
            held_page, out.at[source * block + number], sems.at[source & 1, number]
        )

    def inward(number):
        code = code_of(own, number)

        @pl.when(code >= 0)
        def _():
            own_page(
                layout, table, perm, me, pool, recent, zeros, code, mine.at[number],
                load_sems.at[number],
            )

    loop(0, block, inward)
    fill.wait()

    def is_ours(source, number):
        return (code_of(source, number) < 0) | (source == own)

    def finish(source):
        def one(number):
            @pl.when(is_ours(source, number))
            def _():
                outward(source, number, blank).wait()

        loop(0, block, one)

    def begin(source):
        @pl.when(source >= 2)
        def _():
            finish(source - 2)

        def one(number):
            code = code_of(source, number)

            @pl.when(code < 0)
            def _():
                outward(source, number, blank).start()

            @pl.when((code >= 0) & (source == own))
            def _():
                pltpu.make_async_copy(pool.at[0], mine.at[number], load_sems.at[number]).wait()
                outward(source, number, mine.at[number]).start()

        loop(0, block, one)

    loop(0, layout.peers, begin)
    loop(layout.peers - 2, layout.peers, finish)


def fill_local(layout, table, perm, me, pool, recent, zeros, out):
    page = pool.shape[1:]
    return pl.pallas_call(
        lambda *refs: fill_kernel(layout, *refs),
        out_shape=jax.ShapeDtypeStruct(out.shape, out.dtype),
        grid_spec=pltpu.PrefetchScalarGridSpec(
            num_scalar_prefetch=3,
            grid=(1,),
            in_specs=any_specs(4),
            out_specs=pl.BlockSpec(memory_space=pl.ANY),
            scratch_shapes=[
                pltpu.VMEM(page, pool.dtype),
                pltpu.VMEM((layout.block,) + page, pool.dtype),
                pltpu.SemaphoreType.DMA((2, layout.block)),
                pltpu.SemaphoreType.DMA((layout.block + 1,)),
            ],
        ),
        input_output_aliases={6: 0},
        compiler_params=ROOMY,
        name="fill_local",
    )(table, perm, me, pool, recent, zeros, out)


PARTS = 4


def part_kernel(slot, part, lengths, tables, q_ref, *rest):
    first, last = part == 0, part == PARTS - 1
    if first:
        (nk_ref, nv_ref), rest = rest[:2], rest[2:]
    else:
        before, rest = rest[:3], rest[3:]
    pages, rest = rest[:BLOCK_PAGES], rest[BLOCK_PAGES:]
    if last:
        out_ref, q_rows, top, total, acc = rest
    else:
        top, total, acc, q_rows = rest
    kv_heads, rows, head = q_rows.shape
    tokens = q_ref.shape[0]
    groups = rows // tokens
    step = pl.program_id(0)
    page_len = pages[0].shape[1]
    block_keys = BLOCK_PAGES * page_len
    begin = (part * pl.num_programs(0) + step) * block_keys
    length = lengths[slot]
    inv_scale = 1.0 / math.sqrt(head)

    def score(kv, keys):
        return (
            lax.dot_general(
                q_rows[kv], keys, (((1,), (1,)), ((), ())), preferred_element_type=jnp.float32
            )
            * inv_scale
        )

    @pl.when(step == 0)
    def _():
        for kv in range(kv_heads):
            for group in range(groups):
                lane = (kv * groups + group) * head
                q_rows[kv, group * tokens : (group + 1) * tokens, :] = q_ref[:, lane : lane + head]
            if not first:
                continue
            columns = slice(kv * head, (kv + 1) * head)
            scores = score(kv, nk_ref[:, columns])
            query_id = lax.broadcasted_iota(jnp.int32, scores.shape, 0) % tokens
            key_id = lax.broadcasted_iota(jnp.int32, scores.shape, 1)
            scores = jnp.where(key_id <= query_id, scores, -1e30)
            highest = jnp.max(scores, axis=-1, keepdims=True)
            weights = jnp.exp(scores - highest)
            top[kv] = jnp.broadcast_to(highest, (rows, head))
            total[kv] = jnp.broadcast_to(jnp.sum(weights, axis=-1, keepdims=True), (rows, head))
            acc[kv] = jnp.dot(
                weights.astype(jnp.bfloat16), nv_ref[:, columns], preferred_element_type=jnp.float32
            )
        if not first:
            top[...] = before[0][...]
            total[...] = before[1][...]
            acc[...] = before[2][...]

    def absorb(masked):
        flat = [ref[0].reshape(page_len, 2 * kv_heads * head) for ref in pages]
        for kv in range(kv_heads):
            keys = jnp.concatenate([x[:, kv * head : (kv + 1) * head] for x in flat], axis=0)
            low = (kv_heads + kv) * head
            values = jnp.concatenate([x[:, low : low + head] for x in flat], axis=0)
            scores = score(kv, keys)
            if masked:
                key_id = lax.broadcasted_iota(jnp.int32, scores.shape, 1)
                scores = jnp.where(key_id < length - begin, scores, -1e30)
            past = top[kv]
            highest = jnp.maximum(past, jnp.max(scores, axis=-1, keepdims=True))
            factor = jnp.exp(past - highest)
            weights = jnp.exp(scores - highest[:, :1])
            top[kv] = highest
            total[kv] = total[kv] * factor + jnp.sum(weights, axis=-1, keepdims=True)
            acc[kv] = acc[kv] * factor + jnp.dot(
                weights.astype(jnp.bfloat16), values, preferred_element_type=jnp.float32
            )

    @pl.when(begin + block_keys <= length)
    def _():
        absorb(False)

    @pl.when((begin < length) & (begin + block_keys > length))
    def _():
        absorb(True)

    if last:

        @pl.when(step == pl.num_programs(0) - 1)
        def _():
            for kv in range(kv_heads):
                context = (acc[kv] / total[kv]).astype(jnp.bfloat16)
                for group in range(groups):
                    lane = (kv * groups + group) * head
                    out_ref[:, lane : lane + head] = context[
                        group * tokens : (group + 1) * tokens
                    ]


def relay_part_kernel(layout, slot, part, *refs):
    table, perm, me, number, send, receive, lengths, tables = refs[:8]
    ins, rest = refs[8:16], refs[16:]
    count = 3 if part else 2
    inner, rest = rest[: 1 + count + BLOCK_PAGES], rest[1 + count + BLOCK_PAGES :]
    outs, rest = rest[: 2 + LINKS], rest[2 + LINKS :]
    made = 1 if part == PARTS - 1 else 3
    results, rest = rest[:made], rest[made:]
    rooms, rest = rest[:6], rest[6:]
    stages = step_kernel(
        layout, "step", 0, table, perm, me, number, send, receive, *ins, *outs, *rooms
    )
    steps = tables.shape[0] // layout.slots // BLOCK_PAGES // PARTS
    for index in range(4):

        @pl.when(pl.program_id(0) == index * steps // 4)
        def _(index=index):
            run_stages(stages[index : index + 1])

    part_kernel(slot, part, lengths, tables, *inner, *results, *rest)

    @pl.when(pl.program_id(0) == pl.num_programs(0) - 1)
    def _():
        run_stages(stages[4:])


def relay_part(
    layout, slot, part, table, perm, me, step, send, receive, lengths, tables, pool, recent, zeros,
    arrived, out, held, queries, fresh, state,
):
    slots, row_pages = tables.shape
    tokens = queries.shape[0] // slots
    page_len, features = pool.shape[1], pool.shape[3]
    kv_heads = features // HEAD_SIZE
    rows = tokens * (queries.shape[1] // features)
    steps = row_pages // BLOCK_PAGES // PARTS
    first, last = part == 0, part == PARTS - 1

    def page_spec(index):
        def pick(step, *words):
            lengths, tables = words[6:]
            final = (lengths[slot] + page_len - 1) // page_len - 1
            page = (part * steps + step) * BLOCK_PAGES + index
            return (tables[slot * row_pages + jnp.minimum(page, final)], 0, 0, 0)

        return pl.BlockSpec((1, page_len, 2, features), pick)

    def slot_rows(step, *words):
        return (slot, 0)

    shape = (kv_heads, rows, HEAD_SIZE)
    state_spec = pl.BlockSpec(shape, lambda step, *words: (0, 0, 0))
    operands = list(fresh) if first else list(state)
    specs = [pl.BlockSpec((tokens, features), slot_rows)] * 2 if first else [state_spec] * 3
    room = [pltpu.VMEM(shape, jnp.bfloat16)]
    if last:
        made = (jax.ShapeDtypeStruct((tokens, queries.shape[1]), queries.dtype),)
        made_specs = (pl.BlockSpec(made[0].shape, lambda step, *words: (0, 0)),)
        room += [pltpu.VMEM(shape, jnp.float32)] * 3
    else:
        made = (jax.ShapeDtypeStruct(shape, jnp.float32),) * 3
        made_specs = (state_spec,) * 3
    results = pl.pallas_call(
        lambda *refs: relay_part_kernel(layout, slot, part, *refs),
        out_shape=(
            jax.ShapeDtypeStruct(out.shape, out.dtype),
            jax.ShapeDtypeStruct(held.shape, held.dtype),
        )
        + lane_shapes(pool, 0)
        + made,
        grid_spec=pltpu.PrefetchScalarGridSpec(
            num_scalar_prefetch=8,
            grid=(steps,),
            in_specs=any_specs(8)
            + [pl.BlockSpec((tokens, queries.shape[1]), slot_rows)]
            + specs
            + [page_spec(page) for page in range(BLOCK_PAGES)],
            out_specs=tuple(any_specs(2 + LINKS)) + made_specs,
            scratch_shapes=send_room(pool) + land_room(pool, 1) + room,
        ),
        input_output_aliases={14: 0, 15: 1},
        compiler_params=pltpu.CompilerParams(
            dimension_semantics=("arbitrary",), vmem_limit_bytes=48 << 20
        ),
        name="relay_part",
    )(
        table, perm, me, number(step), send, receive, lengths, tables.reshape(-1), pool, recent,
        zeros, *arrived, out, held, queries, *operands, *([pool] * BLOCK_PAGES),
    )
    return results[2:5], results[0], results[1], results[5:]


PAIR_DEPTH = 640


def pair_kernel(x_ref, w_ref, out_ref):
    @pl.when(pl.program_id(0) == 0)
    def _():
        out_ref[...] = jnp.zeros_like(out_ref)

    depth = w_ref.shape[0]
    out_ref[...] += jnp.dot(
        x_ref[...], w_ref[...].reshape(depth, -1), preferred_element_type=jnp.float32
    )


def project_pair(rows, wkv):
    count, width = rows.shape
    features = wkv.shape[1] * wkv.shape[2]
    return pl.pallas_call(
        pair_kernel,
        out_shape=jax.ShapeDtypeStruct((count, features), jnp.float32),
        grid=(width // PAIR_DEPTH,),
        in_specs=[
            pl.BlockSpec((count, PAIR_DEPTH), lambda step: (0, step)),
            pl.BlockSpec((PAIR_DEPTH,) + wkv.shape[1:], lambda step: (step, 0, 0)),
        ],
        out_specs=pl.BlockSpec((count, features), lambda step: (0, 0)),
        compiler_params=ROOMY,
        name="project_pair",
    )(rows, wkv)


def after(value, *others):
    return lax.optimization_barrier((value,) + others)[0]


def page_counts(layout, by_device, perm):
    lengths = by_device[:, : layout.slots].reshape(-1)[perm].reshape(layout.peers, layout.slots)
    whole = lax.div(lengths, layout.page_len)
    codes = by_device[:, layout.sends : layout.used].reshape(
        layout.peers, layout.peers, layout.block
    )
    edge = whole[:, 0, None, None]
    for slot in range(1, layout.slots):
        low = slot * layout.code_width
        edge = jnp.where(codes >= low, whole[:, slot, None, None] + low, edge)
    valid = codes >= 0
    plain = valid & (codes < edge)
    return jnp.concatenate(
        [
            jnp.sum(valid.astype(jnp.int32), axis=-1).reshape(-1),
            jnp.sum(plain.astype(jnp.int32), axis=-1).reshape(-1),
        ]
    )


def hop(lanes):
    return tuple(
        lax.ppermute(lane, "req", pairs) for lane, pairs in zip(lanes, neighbours())
    )


def number(value):
    return jnp.asarray(value, jnp.int32).reshape(1)


def grid_shards(hidden, norm_gain, wq, wkv, wo, perm, prior_len, page_table, pool, send_table):
    slots = prior_len.shape[0]
    tokens = hidden.shape[0] // slots
    _, peers, block = send_table.shape
    layout = Layout(slots, page_table.shape[1], peers, block)
    layout.page_len = pool.shape[1]
    features = pool.shape[-1]
    device = lax.axis_index("req")
    me = device.astype(jnp.int32).reshape(1)
    mine = jnp.concatenate([prior_len, page_table.reshape(-1), send_table.reshape(-1)])
    mine = jnp.pad(mine, (0, layout.width - layout.used)).reshape(-1, 128)
    by_device = exchange(peers, mine)
    table = by_device.reshape(-1)
    by_device = by_device.reshape(peers, layout.width)
    counts = page_counts(layout, by_device, perm)
    first = plan(layout, True, table, perm, me, counts)
    lanes = [pack_first(layout, table, perm, me, step, first, pool) for step in range(2)]
    arrived = [hop(lane) for lane in lanes]
    full_rows = lax.all_gather(hidden, "tp", axis=1, tiled=True)
    requests = lax.dynamic_slice_in_dim(perm, device * slots, slots)
    lengths = by_device[:, :slots].reshape(-1)[requests]
    tables = by_device[:, slots : layout.sends].reshape(-1, layout.row_pages)[requests]
    positions = (lengths[:, None] + jnp.arange(tokens, dtype=jnp.int32)[None, :]).reshape(-1)

    full_rows = after(full_rows, lanes[1][0])
    normalized_input = normalize(full_rows, norm_gain)
    pair_proj = project_pair(normalized_input, wkv)
    pair_heads = pair_proj.reshape(pair_proj.shape[0], 2, -1, HEAD_SIZE)
    new_keys = rotate(pair_heads[:, 0], positions).astype(jnp.bfloat16).reshape(-1, features)
    new_values = pair_heads[:, 1].astype(jnp.bfloat16).reshape(-1, features)
    recent = jnp.stack([new_keys, new_values], axis=1).reshape(slots, tokens, 2, features)
    zeros = jnp.zeros(pool.shape[1:], pool.dtype)

    query_proj = jnp.dot(normalized_input, wq, preferred_element_type=jnp.float32)
    queries = rotate(
        query_proj.reshape(query_proj.shape[0], -1, HEAD_SIZE), positions
    ).astype(jnp.bfloat16)
    queries = queries.reshape(queries.shape[0], -1)
    first = after(first, queries, recent)
    lanes.append(pack_first(layout, table, perm, me, 2, first, pool))
    arrived.append(hop(lanes[2]))

    counts = after(counts, lanes[-1][0], *arrived[0])
    send, receive, rounds = plan(layout, False, table, perm, me, counts)
    lane, out, held = relay_begin(
        layout, table, perm, me, OWN_ROUNDS, send, receive, pool, arrived[0] + arrived[1]
    )
    arrived.append(hop(lane))

    def advance(step, parity, landed, out, held):
        return relay(
            layout, parity, table, perm, me, number(step), send, receive, pool, recent, zeros,
            landed, out, held,
        )

    def scatter(value):
        return lax.psum_scatter(
            value.astype(jnp.bfloat16), "tp", scatter_dimension=1, tiled=True
        )

    state = None
    contexts = []
    for step in range(OWN_ROUNDS + 1, FIXED_ROUNDS):
        slot, part = divmod(step - OWN_ROUNDS - 1, PARTS)
        landed = arrived[step - 2]
        if step == 11:
            landed = (after(landed[0], value),) + landed[1:]
        lane, out, held, state = relay_part(
            layout, slot, part, table, perm, me, step, send, receive, lengths, tables, pool,
            recent, zeros, landed, out, held, queries, (new_keys, new_values), state,
        )
        arrived.append(hop(lane))
        if part == PARTS - 1:
            contexts.append(state[0])
        if step == 10:
            value = jnp.dot(after(contexts[0], *arrived[8]), wo, preferred_element_type=jnp.float32)
            output = scatter(value)
    out = fill_local(layout, table, perm, me, pool, recent, zeros, out)
    outputs = [output]
    last_value = jnp.dot(after(contexts[-1], *arrived[-2]), wo, preferred_element_type=jnp.float32)
    outputs.append(scatter(last_value))
    attn_out = jnp.concatenate(outputs, axis=0)

    newest = arrived[-1]
    newest = (after(newest[0], last_value),) + newest[1:]

    def turn(state):
        step, older, newer, out, held = state
        lane, out, held = advance(step, 0, older, out, held)
        older = hop(lane)
        lane, out, held = advance(step + 1, 1, newer, out, held)
        return step + 2, older, hop(lane), out, held

    step, older, newer, out, _ = lax.while_loop(
        lambda state: state[0] < rounds[0],
        turn,
        (jnp.int32(FIXED_ROUNDS), arrived[-2], newest, out, held),
    )
    decode_pages = land_last(
        layout, table, perm, me, number(step), receive, older + newer, out
    )
    return (attn_out, decode_pages.reshape((1, peers, block) + pool.shape[1:]))


def shards(hidden, norm_gain, wq, wkv, wo, perm, prior_len, page_table, pool, send_table):
    slots = prior_len.shape[0]
    tokens = hidden.shape[0] // slots
    _, peers, block = send_table.shape
    layout = Layout(slots, page_table.shape[1], peers, block)
    features = pool.shape[-1]
    device = lax.axis_index("req")
    me = device.astype(jnp.int32).reshape(1)
    mine = jnp.concatenate([prior_len, page_table.reshape(-1), send_table.reshape(-1)])
    mine = jnp.pad(mine, (0, layout.width - layout.used)).reshape(-1, 128)
    by_device = exchange(peers, mine)
    table = by_device.reshape(-1)
    by_device = by_device.reshape(peers, layout.width)
    outgoing = pack_pages(layout, table, perm, me, pool)
    arrived = lax.all_to_all(outgoing, "req", split_axis=0, concat_axis=0, tiled=True)

    full_rows = lax.all_gather(hidden, "tp", axis=1, tiled=True)
    late_pool, wkv, outgoing = lax.optimization_barrier((pool, wkv, outgoing))
    requests = lax.dynamic_slice_in_dim(perm, device * slots, slots)
    lengths = by_device[:, :slots].reshape(-1)[requests]
    tables = by_device[:, slots : layout.sends].reshape(-1, layout.row_pages)[requests]

    normalized_input = normalize(full_rows, norm_gain)
    query_proj = jnp.dot(normalized_input, wq, preferred_element_type=jnp.float32)
    pair_proj = jnp.dot(
        normalized_input, wkv.reshape(wkv.shape[0], -1), preferred_element_type=jnp.float32
    )
    positions = (lengths[:, None] + jnp.arange(tokens, dtype=jnp.int32)[None, :]).reshape(-1)
    queries = rotate(query_proj.reshape(query_proj.shape[0], -1, HEAD_SIZE), positions).astype(
        jnp.bfloat16
    )
    pair_heads = pair_proj.reshape(pair_proj.shape[0], 2, -1, HEAD_SIZE)
    new_keys = rotate(pair_heads[:, 0], positions).astype(jnp.bfloat16).reshape(-1, features)
    new_values = pair_heads[:, 1].astype(jnp.bfloat16).reshape(-1, features)
    recent = jnp.stack([new_keys, new_values], axis=1).reshape(slots, tokens, 2, features)
    context = attend(
        lengths,
        tables,
        queries.reshape(queries.shape[0], -1),
        new_keys,
        new_values,
        late_pool[:, :, 0],
        late_pool[:, :, 1],
    )
    partial_value = jnp.dot(context, wo, preferred_element_type=jnp.float32)
    recent, partial_value = lax.optimization_barrier((recent, partial_value))
    attn_out = lax.psum_scatter(
        partial_value.astype(jnp.bfloat16), "tp", scatter_dimension=1, tiled=True
    )
    zeros = jnp.zeros(pool.shape[1:], pool.dtype)
    late_arrived = lax.all_to_all(
        pack_pages(layout, table, perm, me, late_pool, recent, zeros),
        "req",
        split_axis=0,
        concat_axis=0,
        tiled=True,
    )
    early_pages, numbers = place_early_pages(layout, table, perm, me, arrived, zeros)
    decode_pages = place_late_pages(numbers, late_arrived, early_pages)
    return (attn_out, decode_pages.reshape((1, peers, block) + pool.shape[1:]))


def solution(mesh):
    placed = (
        P("req", "tp"),
        P(),
        P(None, "tp"),
        P(None, None, "tp"),
        P("tp", None),
        P(),
        P("req"),
        P("req", None),
        P("req", None, None, "tp"),
        P("req", None, None),
    )
    return jax.shard_map(
        grid_shards if mesh.shape["req"] == 8 else shards,
        mesh=mesh,
        in_specs=placed,
        out_specs=(P("req", "tp"), P("req", None, None, None, None, "tp")),
        check_vma=False,
    )
```
